128 devices in a mesh: row: 8 (over y, z_lo), col: 16 (over z_hi, x, core).
Axes of the slice: x: 4, y: 4, z: 4 (z_hi: 2, z_lo: 2; z = z_hi * 2 + z_lo), core: 2. Of those that a mesh axis runs over, the one named last changes fastest.
Arguments:
- latents: bfloat16 [256, 256, 512], P('row', 'col'), may hold values from -6 to 6
- cotangent: bfloat16 [256, 256, 512], P('row', 'col'), may hold values from -6 to 6
- w_row: bfloat16 [4, 512, 512], replicated, may hold values from -6.6733202 to 6.6733202, as said below
- w_col: bfloat16 [4, 512, 512], replicated, may hold values from -6.6733202 to 6.6733202, as said below
- keep_heads: int32 [2, 8], replicated, may hold values 0 or 1
Outputs:
- output: bfloat16 [256, 256, 512], P('row', 'col')
- grad_latents: bfloat16 [256, 256, 512], P('row', 'col')
- grad_row: float32 [4, 512, 512], replicated
- grad_col: float32 [4, 512, 512], replicated
The draws below stay inside these ranges and needn't reach their ends.
Inputs may be any that keep to these rules, and one draw needn't show every extreme that they name: `w_row`: projection weights. `w_col`: projection weights.
All inputs are finite; a program needn't handle non-finite values.
Results may differ from the reference program's by a relative error of at most 0.033.
Values may be sent and summed in bfloat16 or wider, within the bound.
No kernel may reach another device: no remote copies, remote signals or barrier semaphores. Data moves between devices by JAX's collectives and lax.ppermute only.
A program may use at most 128 MiB of HBM per device.

```python
import jax
import jax.numpy as jnp
from jax import lax

HEADS = 8
HEAD = 64
D = 512
RT = 32
CT = 16
GH = 256
GW = 256
N_ROW = 8
N_COL = 16


def stacked_weights(key, salt):
    base_key = jax.random.fold_in(key, salt)
    normal_part = jnp.clip(jax.random.normal(base_key, (4, D, D), jnp.float32), -5.0, 5.0) * D ** (-0.5)
    return normal_part.astype(jnp.bfloat16)


def draw_w_row(key, part):
    return stacked_weights(key, 11)


def draw_w_col(key, part):
    return stacked_weights(key, 23)


def touch_ends(values, stream_key, low, largest):
    longest = values.shape.index(max(values.shape))
    spots = []
    for shift in (0, 1):
        where = [jax.random.randint(jax.random.fold_in(stream_key, axis), (), 0, length) for axis, length in enumerate(values.shape)]
        where[longest] = (where[longest] + shift) % values.shape[longest]
        spots.append(tuple(where))
    return values.at[spots[0]].set(low).at[spots[1]].set(largest)


def shard_levels(key, extent, shards, smallest, high):
    def one(position, parts):
        steps = jax.random.uniform(jax.random.fold_in(jax.random.fold_in(key, 6), position), (parts,), jnp.float32, smallest / len(shards), high / len(shards))
        return jnp.repeat(jnp.exp(steps), extent[position] // parts).reshape((-1,) + (1,) * (len(extent) - position - 1))

    factor_of = one(*shards[0])
    for cut in shards[1:]:
        factor_of = factor_of * one(*cut)
    return factor_of


def normal_values(stream_key, extent, deviation, most, pieces=(), kind=jnp.bfloat16):
    factor_of = shard_levels(stream_key, extent, pieces, -0.22, 0.18) if pieces else 1.0
    values = jax.random.normal(stream_key, extent, jnp.float32) * deviation * factor_of
    return jnp.minimum(jnp.maximum(values, -most), most).astype(kind)


def setup_inputs(seed: int = 0) -> dict:
    arg_keys = jax.random.split(jax.random.key(seed), 6)
    latents = normal_values(arg_keys[0], (GH, GW, D), 1.0, 6.0, ((0, 8), (1, 16)))
    cotangent = normal_values(arg_keys[1], (GH, GW, D), 1.0, 6.0, ((0, 8), (1, 16)))
    w_row = draw_w_row(jax.random.fold_in(arg_keys[5], 71), 0)
    w_col = draw_w_col(jax.random.fold_in(arg_keys[5], 71), 0)
    keep_heads = touch_ends((jax.random.randint(arg_keys[4], (2, HEADS), 0, 4) < 3).astype(jnp.int32), jax.random.fold_in(arg_keys[4], 1), 0, 1)
    return {"latents": latents, "cotangent": cotangent, "w_row": w_row, "w_col": w_col, "keep_heads": keep_heads}


EPSILON = 1e-06

def mat_tn(left, right):
    return lax.dot_general(left, right, (((0,), (0,)), ((), ())), preferred_element_type=jnp.float32)

def mat_nt(left, right):
    return lax.dot_general(left, right, (((1,), (1,)), ((), ())), preferred_element_type=jnp.float32)

def head_specs(letters):
    if letters == 'nl':
        return ('nlhe', 'nmhe')
    return ('lnhe', 'mnhe')

def line_forward(inputs, weights, head_gain, letters):
    in_shape = inputs.shape
    model_width = in_shape[2]
    q_spec, k_spec = head_specs(letters)
    values_f = inputs.astype(jnp.float32)
    inv_rms = lax.rsqrt(lax.optimization_barrier(jnp.mean(values_f * values_f, axis=-1, keepdims=True)) + EPSILON)
    normed = (values_f * inv_rms).astype(jnp.bfloat16).reshape(-1, model_width)

    def project(which_proj):
        result = jnp.dot(normed, weights[which_proj], preferred_element_type=jnp.float32)
        return result.astype(jnp.bfloat16).reshape(in_shape[0], in_shape[1], HEADS, HEAD)
    q_proj, k_proj, v_proj = (project(0), project(1), project(2))
    scores = jnp.einsum(q_spec + ',' + k_spec + '->nhlm', q_proj, k_proj, preferred_element_type=jnp.float32) * HEAD ** (-0.5)
    row_max = lax.optimization_barrier(jnp.max(scores, axis=-1, keepdims=True))
    exp_scores = jnp.exp(scores - row_max)
    attn_probs = exp_scores / lax.optimization_barrier(jnp.sum(exp_scores, axis=-1, keepdims=True))
    probs_low = attn_probs.astype(jnp.bfloat16)
    mixed_heads = jnp.einsum('nhlm,' + k_spec + '->' + q_spec, probs_low, v_proj, preferred_element_type=jnp.float32)
    attended = (mixed_heads * head_gain[:, None]).astype(jnp.bfloat16).reshape(-1, model_width)
    result = values_f + jnp.dot(attended, weights[3], preferred_element_type=jnp.float32).reshape(in_shape)
    saved_state = (normed, q_proj, k_proj, v_proj, attn_probs, probs_low, attended, inv_rms)
    return (result.astype(jnp.bfloat16), saved_state)

def line_backward(grad_out, inputs, saved_state, weights, head_gain, letters):
    normed, q_proj, k_proj, v_proj, attn_probs, probs_low, attended, inv_rms = saved_state
    in_shape = inputs.shape
    model_width = in_shape[2]
    q_spec, k_spec = head_specs(letters)
    grad_flat = grad_out.reshape(-1, model_width)
    grad_wo = mat_tn(attended, grad_flat)
    grad_att = mat_nt(grad_flat, weights[3]).reshape(in_shape[0], in_shape[1], HEADS, HEAD)
    grad_att = (grad_att * head_gain[:, None]).astype(jnp.bfloat16)
    grad_probs = jnp.einsum(q_spec + ',' + k_spec + '->nhlm', grad_att, v_proj, preferred_element_type=jnp.float32)
    grad_scores = attn_probs * (grad_probs - lax.optimization_barrier(jnp.sum(attn_probs * grad_probs, axis=-1, keepdims=True))) * HEAD ** (-0.5)
    grad_scores = grad_scores.astype(jnp.bfloat16)
    grad_q = jnp.einsum('nhlm,' + k_spec + '->' + q_spec, grad_scores, k_proj, preferred_element_type=jnp.float32)
    grad_k = jnp.einsum('nhlm,' + q_spec + '->' + k_spec, grad_scores, q_proj, preferred_element_type=jnp.float32)
    grad_v = jnp.einsum('nhlm,' + q_spec + '->' + k_spec, probs_low, grad_att, preferred_element_type=jnp.float32)
    grad_q = grad_q.astype(jnp.bfloat16).reshape(-1, model_width)
    grad_k = grad_k.astype(jnp.bfloat16).reshape(-1, model_width)
    grad_v = grad_v.astype(jnp.bfloat16).reshape(-1, model_width)
    grad_weights = jnp.stack([mat_tn(normed, grad_q), mat_tn(normed, grad_k), mat_tn(normed, grad_v), grad_wo])
    grad_normed = mat_nt(grad_q, weights[0]) + mat_nt(grad_k, weights[1]) + mat_nt(grad_v, weights[2])
    values_f = inputs.astype(jnp.float32).reshape(-1, model_width)
    inv_flat = inv_rms.reshape(-1, 1)
    grad_in = grad_flat.astype(jnp.float32) + inv_flat * grad_normed
    grad_in = grad_in - values_f * inv_flat * inv_flat * inv_flat * lax.optimization_barrier(jnp.mean(grad_normed * values_f, axis=-1, keepdims=True))
    return (grad_in.astype(jnp.bfloat16).reshape(in_shape), grad_weights)

def reference(latents, cotangent, w_row, w_col, keep_heads):
    head_gain = keep_heads.astype(jnp.float32)
    rows_group = RT // N_COL
    cols_group = CT // N_ROW
    grid_rows, grid_cols, model_width = latents.shape
    row_blocks = latents.reshape(grid_rows // rows_group, rows_group, grid_cols, model_width)

    def row_forward(line_block):
        return line_forward(line_block, w_row, head_gain[0], 'nl')[0]
    mid_rows = lax.map(row_forward, row_blocks).reshape(grid_rows, grid_cols, model_width)
    col_blocks = mid_rows.reshape(grid_rows, grid_cols // cols_group, cols_group, model_width).transpose(1, 0, 2, 3)
    grad_blocks = cotangent.reshape(grid_rows, grid_cols // cols_group, cols_group, model_width).transpose(1, 0, 2, 3)
    zero_grads = jnp.zeros((4, model_width, model_width), jnp.float32)

    def col_step(totals, inputs_pair):
        line_block, grad_block = inputs_pair
        result, saved_state = line_forward(line_block, w_col, head_gain[1], 'ln')
        grad_in, grad_weights = line_backward(grad_block, line_block, saved_state, w_col, head_gain[1], 'ln')
        return (totals + grad_weights, (result, grad_in))
    grad_col, (col_outs, col_grads) = lax.scan(col_step, zero_grads, (col_blocks, grad_blocks))
    output = col_outs.transpose(1, 0, 2, 3).reshape(grid_rows, grid_cols, model_width)
    grad_mid = col_grads.transpose(1, 0, 2, 3).reshape(grid_rows // rows_group, rows_group, grid_cols, model_width)

    def row_step(totals, inputs_pair):
        line_block, grad_block = inputs_pair
        result, saved_state = line_forward(line_block, w_row, head_gain[0], 'nl')
        grad_in, grad_weights = line_backward(grad_block, line_block, saved_state, w_row, head_gain[0], 'nl')
        return (totals + grad_weights, grad_in)
    grad_row, row_grads = lax.scan(row_step, zero_grads, (row_blocks, grad_mid))
    grad_latents = row_grads.reshape(grid_rows, grid_cols, model_width)
    return (output, grad_latents, grad_row, grad_col)
```

```python
import functools

import jax
import jax.numpy as jnp
from jax import lax
from jax.experimental import pallas as pl
from jax.experimental.pallas import tpu as pltpu
from jax.sharding import Mesh, PartitionSpec as P

HEADS = 8
HEAD = 64
D = 512
PAIR = 128
N_PAIR = D // PAIR
LINE = 256
TOK = 512
N_ROW = 8
N_COL = 16
N_DEV = N_ROW * N_COL
EPSILON = 1e-06
SCALE = HEAD ** (-0.5)

F32 = jnp.float32
BF16 = jnp.bfloat16

ROW = ("y", "zl")
COL = ("zh", "x", "c")
BOTH = COL + ROW
CHIPS = ("y", "zl", "zh", "x")


def dot(left, right):
    return lax.dot_general(left, right, (((1,), (0,)), ((), ())), preferred_element_type=F32)


def dot_nt(left, right):
    return lax.dot_general(left, right, (((1,), (1,)), ((), ())), preferred_element_type=F32)


def dot_tn(left, right):
    return lax.dot_general(left, right, (((0,), (0,)), ((), ())), preferred_element_type=F32)


def halves(value):
    lane = lax.broadcasted_iota(jnp.int32, value.shape, 1)
    zero = jnp.zeros_like(value)
    return (jnp.where(lane < HEAD, value, zero), jnp.where(lane >= HEAD, value, zero))


def inverse_rms(values_f):
    return lax.rsqrt(jnp.mean(values_f * values_f, axis=-1, keepdims=True) + EPSILON)


def softmax(q_half, k_pair):
    scores = dot_nt(q_half, k_pair)
    peak = jnp.max(scores, axis=-1, keepdims=True)
    grown = jnp.exp(scores - peak)
    return grown * (1.0 / jnp.sum(grown, axis=-1, keepdims=True))


def slot(col_local, group, row_local):
    return col_local * 8 + group * 2 + row_local


def row_forward_kernel(x_ref, w_ref, gain_ref, mid_ref, qkv_ref, att_ref, n_s, mix_s):
    for rr in range(2):
        u = x_ref[:, rr].astype(F32).reshape(LINE, D)
        n_s[rr * LINE : (rr + 1) * LINE, :] = (u * inverse_rms(u)).astype(BF16)
    normed = n_s[...]
    qkv_ref[0] = (dot(normed, w_ref[0]).astype(BF16).astype(F32) * SCALE).astype(BF16)
    qkv_ref[1] = dot(normed, w_ref[1]).astype(BF16)
    qkv_ref[2] = dot(normed, w_ref[2]).astype(BF16)
    for rr in range(2):
        rows = slice(rr * LINE, (rr + 1) * LINE)
        for pair in range(N_PAIR):
            lanes = slice(pair * PAIR, (pair + 1) * PAIR)
            q_half = halves(qkv_ref[0, rows, lanes])
            v_half = halves(qkv_ref[2, rows, lanes])
            k_pair = qkv_ref[1, rows, lanes]
            probs = [softmax(q_half[h], k_pair).astype(BF16) for h in range(2)]
            mixed = dot(probs[0], v_half[0]) + dot(probs[1], v_half[1])
            att_ref[rows, lanes] = (mixed * gain_ref[:, lanes]).astype(BF16)
    added = dot(att_ref[...], w_ref[3])
    for rr in range(2):
        u = x_ref[:, rr].astype(F32).reshape(LINE, D)
        mid = (u + added[rr * LINE : (rr + 1) * LINE]).reshape(16, 2, 8, D)
        for cc in range(2):
            for group in range(4):
                piece = mid[:, cc, :, group * 128 : (group + 1) * 128].reshape(128, 128)
                mix_s[pl.ds(slot(cc, group, rr), 128, stride=16), :] = piece
    mid_ref[...] = mix_s[...].reshape(N_DEV, 16, 128).astype(BF16)


def attention_backward(rows, lanes, qkv, da_ref, probs_of, dqkv_ref):
    q_half = halves(qkv[0, rows, lanes])
    k_pair = qkv[1, rows, lanes]
    k_half = halves(k_pair)
    v_pair = qkv[2, rows, lanes]
    da_half = halves(da_ref[rows, lanes])
    grads = []
    lows = []
    for h in range(2):
        probs = probs_of(h, q_half, k_pair)
        lows.append(probs.astype(BF16))
        grad_probs = dot_nt(da_half[h], v_pair)
        total = jnp.sum(probs * grad_probs, axis=-1, keepdims=True)
        grads.append((probs * (grad_probs - total)).astype(BF16))
    dqkv_ref[0, rows, lanes] = (
        (dot(grads[0], k_half[0]) + dot(grads[1], k_half[1])) * SCALE
    ).astype(BF16)
    dqkv_ref[1, rows, lanes] = (
        dot_tn(grads[0], q_half[0]) + dot_tn(grads[1], q_half[1])
    ).astype(BF16)
    dqkv_ref[2, rows, lanes] = (
        dot_tn(lows[0], da_half[0]) + dot_tn(lows[1], da_half[1])
    ).astype(BF16)
    return lows


def input_gradient(grad_f, u, dqkv_ref, w_ref, rows):
    inv = inverse_rms(u)
    dn = (
        dot_nt(dqkv_ref[0, rows, :], w_ref[0])
        + dot_nt(dqkv_ref[1, rows, :], w_ref[1])
        + dot_nt(dqkv_ref[2, rows, :], w_ref[2])
    )
    mean = jnp.mean(dn * u, axis=-1, keepdims=True)
    return grad_f + inv * dn - u * (inv * inv * inv * mean)


def recomputed(h, q_half, k_pair):
    return softmax(q_half[h], k_pair)


def row_backward_kernel(
    g_ref, x_ref, qkv_ref, att_ref, w_ref, gain_ref, gin_ref, dw_ref, mix_s, g_s, da_s, dqkv_s, n_s
):
    mix_s[...] = g_ref[...].astype(F32).reshape(N_DEV * 16, 128)
    for rr in range(2):
        for cc in range(2):
            for group in range(4):
                piece = mix_s[pl.ds(slot(cc, group, rr), 128, stride=16), :]
                g_s[rr, :, cc, :, group * 128 : (group + 1) * 128] = piece.reshape(16, 8, 128)
    grad_f = g_s[...].reshape(TOK, D)
    grad_low = grad_f.astype(BF16)
    da_s[...] = (dot_nt(grad_low, w_ref[3]) * gain_ref[...]).astype(BF16)
    for rr in range(2):
        u = x_ref[:, rr].astype(F32).reshape(LINE, D)
        n_s[rr * LINE : (rr + 1) * LINE, :] = (u * inverse_rms(u)).astype(BF16)
        rows = slice(rr * LINE, (rr + 1) * LINE)
        for pair in range(N_PAIR):
            lanes = slice(pair * PAIR, (pair + 1) * PAIR)
            attention_backward(rows, lanes, qkv_ref, da_s, recomputed, dqkv_s)
    for which in range(3):
        dw_ref[which] = dot_tn(n_s[...], dqkv_s[which]).astype(BF16)
    dw_ref[3] = dot_tn(att_ref[...], grad_low).astype(BF16)
    for rr in range(2):
        rows = slice(rr * LINE, (rr + 1) * LINE)
        u = x_ref[:, rr].astype(F32).reshape(LINE, D)
        grad_in = input_gradient(g_s[rr].reshape(LINE, D), u, dqkv_s, w_ref, rows)
        gin_ref[:, rr] = grad_in.astype(BF16).reshape(16, 16, D)


def col_kernel(
    m_ref, c_ref, w_ref, gain_ref, out_ref, gmid_ref, dw_ref,
    mix_s, u_s, g_s, n_s, qkv_s, att_s, da_s, dqkv_s, p_s,
):
    mix_s[...] = m_ref[...].astype(F32).reshape(N_DEV * 16, 128)
    for cc in range(2):
        for rr in range(2):
            base = cc * LINE + rr * 128
            g_s[base : base + 128, :] = c_ref[:, cc, rr * 16 : (rr + 1) * 16, :].reshape(128, D)
            for group in range(4):
                for grid_row in range(N_ROW):
                    start = base + grid_row * 16
                    u_s[start : start + 16, group * 128 : (group + 1) * 128] = mix_s[
                        pl.ds(grid_row * 16 + slot(cc, group, rr), 16, stride=128), :
                    ]
    da_s[...] = (dot_nt(g_s[...], w_ref[3]) * gain_ref[...]).astype(BF16)
    u = u_s[...]
    n_s[...] = (u * inverse_rms(u)).astype(BF16)
    normed = n_s[...]
    qkv_s[0] = (dot(normed, w_ref[0]).astype(BF16).astype(F32) * SCALE).astype(BF16)
    qkv_s[1] = dot(normed, w_ref[1]).astype(BF16)
    qkv_s[2] = dot(normed, w_ref[2]).astype(BF16)
    for cc in range(2):
        rows = slice(cc * LINE, (cc + 1) * LINE)
        for pair in range(N_PAIR):
            lanes = slice(pair * PAIR, (pair + 1) * PAIR)
            lows = attention_backward(rows, lanes, qkv_s, da_s, recomputed, dqkv_s)
            v_half = halves(qkv_s[2, rows, lanes])
            mixed = dot(lows[0], v_half[0]) + dot(lows[1], v_half[1])
            att_s[rows, lanes] = (mixed * gain_ref[:, lanes]).astype(BF16)
    for cc in range(2):
        rows = slice(cc * LINE, (cc + 1) * LINE)
        u = u_s[rows, :]
        grad_in = input_gradient(g_s[rows, :].astype(F32), u, dqkv_s, w_ref, rows)
        for rr in range(2):
            for group in range(4):
                for grid_row in range(N_ROW):
                    start = rr * 128 + grid_row * 16
                    mix_s[pl.ds(grid_row * 16 + slot(cc, group, rr), 16, stride=128), :] = grad_in[
                        start : start + 16, group * 128 : (group + 1) * 128
                    ]
    gmid_ref[...] = mix_s[...].reshape(N_DEV, 16, 128).astype(BF16)
    for cc in range(2):
        rows = slice(cc * LINE, (cc + 1) * LINE)
        result = (u_s[rows, :] + dot(att_s[rows, :], w_ref[3])).astype(BF16)
        for rr in range(2):
            out_ref[:, cc, rr * 16 : (rr + 1) * 16, :] = result[rr * 128 : (rr + 1) * 128].reshape(
                8, 16, D
            )
    for which in range(3):
        dw_ref[which] = dot_tn(n_s[...], dqkv_s[which]).astype(BF16)
    dw_ref[3] = dot_tn(att_s[...], g_s[...]).astype(BF16)


def tile_to_lines_kernel(tile_ref, lines_ref, mix_s):
    tile = tile_ref[...].astype(F32).reshape(TOK, D)
    for group in range(4):
        lanes = slice(group * 128, (group + 1) * 128)
        mix_s[group] = tile[:, lanes]
        for grid_row in range(N_ROW):
            for cc in range(2):
                for rr in range(2):
                    piece = mix_s[group, pl.ds(rr * 16 + cc * 8 + grid_row, 16, stride=32), :]
                    lines_ref[grid_row, cc, rr * 16 : (rr + 1) * 16, lanes] = piece.astype(BF16)


def lines_to_tile_kernel(lines_ref, tile_ref, mix_s):
    for group in range(4):
        lanes = slice(group * 128, (group + 1) * 128)
        for grid_row in range(N_ROW):
            for cc in range(2):
                for rr in range(2):
                    piece = lines_ref[grid_row, cc, rr * 16 : (rr + 1) * 16, lanes].astype(F32)
                    mix_s[group, pl.ds(rr * 16 + cc * 8 + grid_row, 16, stride=32), :] = piece
        tile_ref[:, :, lanes] = mix_s[group].astype(BF16).reshape(32, 16, 128)


def call(kernel, outs, scratch, flops, moved, name):
    return pl.pallas_call(
        kernel,
        out_shape=outs,
        scratch_shapes=scratch,
        name=name,
        compiler_params=pltpu.CompilerParams(vmem_limit_bytes=40 * 1024 * 1024),
        cost_estimate=pl.CostEstimate(flops=flops, bytes_accessed=moved, transcendentals=0),
    )


def shape(*dims, dtype=BF16):
    return jax.ShapeDtypeStruct(dims, dtype)


MATMUL = 2 * TOK * D * D
ATTEND = 2 * 16 * LINE * LINE * HEAD
MIB = 1 << 20

row_forward = call(
    row_forward_kernel,
    (shape(N_DEV, 16, 128), shape(3, TOK, D), shape(TOK, D)),
    [pltpu.VMEM((TOK, D), BF16), pltpu.VMEM((N_DEV * 16, 128), F32)],
    4 * MATMUL + 2 * ATTEND,
    6 * MIB,
    "row_forward",
)
row_backward = call(
    row_backward_kernel,
    (shape(16, 2, 16, D), shape(4, D, D)),
    [
        pltpu.VMEM((N_DEV * 16, 128), F32),
        pltpu.VMEM((2, 16, 2, 8, D), F32),
        pltpu.VMEM((TOK, D), BF16),
        pltpu.VMEM((3, TOK, D), BF16),
        pltpu.VMEM((TOK, D), BF16),
    ],
    8 * MATMUL + 5 * ATTEND,
    8 * MIB,
    "row_backward",
)
col_both = call(
    col_kernel,
    (shape(8, 2, 32, D), shape(N_DEV, 16, 128), shape(4, D, D)),
    [
        pltpu.VMEM((N_DEV * 16, 128), F32),
        pltpu.VMEM((TOK, D), F32),
        pltpu.VMEM((TOK, D), BF16),
        pltpu.VMEM((TOK, D), BF16),
        pltpu.VMEM((3, TOK, D), BF16),
        pltpu.VMEM((TOK, D), BF16),
        pltpu.VMEM((TOK, D), BF16),
        pltpu.VMEM((3, TOK, D), BF16),
        pltpu.VMEM((8, 128), F32),
    ],
    12 * MATMUL + 6 * ATTEND,
    6 * MIB,
    "col_both",
)
tile_to_lines = call(
    tile_to_lines_kernel, shape(8, 2, 32, D), [pltpu.VMEM((4, TOK, 128), F32)], 0, MIB, "tile_to_lines"
)
lines_to_tile = call(
    lines_to_tile_kernel, shape(32, 16, D), [pltpu.VMEM((4, TOK, 128), F32)], 0, MIB, "lines_to_tile"
)


def exchange(values, axes):
    return lax.all_to_all(values, axes, split_axis=0, concat_axis=0, tiled=True)


def reduce_all(partial):
    pieces = partial.reshape(2, 1024, 512)
    both = exchange(pieces, ("c",))
    mine = (both[0].astype(F32) + both[1].astype(F32)).astype(BF16)
    parts = exchange(mine.reshape(64, 64, 128), CHIPS)
    total = jnp.sum(parts.astype(F32), axis=0).astype(BF16)
    spread = exchange(jnp.broadcast_to(total[None], (64, 64, 128)), CHIPS)
    whole = exchange(jnp.broadcast_to(spread.reshape(1, 1024, 512), (2, 1024, 512)), ("c",))
    return whole.reshape(4, D, D).astype(F32)


def body(latents, cotangent, w_row, w_col, keep_heads):
    gain = jnp.repeat(keep_heads.astype(F32), HEAD, axis=1)
    gain_row, gain_col = gain[0:1], gain[1:2]
    rows_in = exchange(latents.reshape(16, 2, 16, D), COL)
    grad_lines = exchange(tile_to_lines(cotangent), ROW)
    mid_send, qkv_row, att_row = row_forward(rows_in, w_row, gain_row)
    mid_lines = exchange(mid_send, BOTH)
    out_lines, grad_send, part_col = col_both(mid_lines, grad_lines, w_col, gain_col)
    grad_rows = exchange(grad_send, BOTH)
    output = lines_to_tile(exchange(out_lines, ROW))
    grad_in, part_row = row_backward(grad_rows, rows_in, qkv_row, att_row, w_row, gain_row)
    grad_latents = exchange(grad_in, COL).reshape(32, 16, D)
    return (output, grad_latents, reduce_all(part_row), reduce_all(part_col))


def solution(mesh):
    fine = Mesh(mesh.devices.reshape(4, 2, 2, 4, 2), ("y", "zl", "zh", "x", "c"))
    tile = P(ROW, COL, None)
    return jax.shard_map(
        body,
        mesh=fine,
        in_specs=(tile, tile, P(), P(), P()),
        out_specs=(tile, tile, P(), P()),
        check_vma=False,
    )
```

```python
import functools

import jax
import jax.numpy as jnp
from jax import lax
from jax.experimental import pallas as pl
from jax.experimental.pallas import tpu as pltpu
from jax.sharding import Mesh, PartitionSpec as P

HEADS = 8
HEAD = 64
D = 512
PAIR = 128
N_PAIR = D // PAIR
LINE = 256
TOK = 512
N_ROW = 8
N_COL = 16
N_DEV = N_ROW * N_COL
EPSILON = 1e-06
SCALE = HEAD ** (-0.5)

F32 = jnp.float32
BF16 = jnp.bfloat16

ROW = ("y", "zl")
COL = ("zh", "x", "c")
BOTH = COL + ROW
CHIPS = ("y", "zl", "zh", "x")


def dot(left, right):
    return lax.dot_general(left, right, (((1,), (0,)), ((), ())), preferred_element_type=F32)


def dot_nt(left, right):
    return lax.dot_general(left, right, (((1,), (1,)), ((), ())), preferred_element_type=F32)


def dot_tn(left, right):
    return lax.dot_general(left, right, (((0,), (0,)), ((), ())), preferred_element_type=F32)


def halves(value):
    lane = lax.broadcasted_iota(jnp.int32, value.shape, 1)
    zero = jnp.zeros_like(value)
    return (jnp.where(lane < HEAD, value, zero), jnp.where(lane >= HEAD, value, zero))


def inverse_rms(values_f):
    return lax.rsqrt(jnp.mean(values_f * values_f, axis=-1, keepdims=True) + EPSILON)


def softmax(q_half, k_pair):
    scores = dot_nt(q_half, k_pair)
    peak = jnp.max(scores, axis=-1, keepdims=True)
    grown = jnp.exp(scores - peak)
    return grown * (1.0 / jnp.sum(grown, axis=-1, keepdims=True))


def slot(col_local, group, row_local):
    return col_local * 8 + group * 2 + row_local


def weight_copies(w_ref, w_s, sems):
    return [pltpu.make_async_copy(w_ref.at[i], w_s.at[i], sems.at[i]) for i in range(4)]


def project(normed, qkv_ref, w_s, copies):
    copies[0].wait()
    qkv_ref[0] = (dot(normed, w_s[0]).astype(BF16).astype(F32) * SCALE).astype(BF16)
    copies[1].wait()
    qkv_ref[1] = dot(normed, w_s[1]).astype(BF16)
    copies[2].wait()
    qkv_ref[2] = dot(normed, w_s[2]).astype(BF16)


def row_forward_kernel(x_ref, gain_ref, w_ref, mid_ref, qkv_ref, left_ref, mix_s, w_s, sems):
    copies = weight_copies(w_ref, w_s, sems)
    for copy in copies:
        copy.start()
    for rr in range(2):
        u = x_ref[:, rr].astype(F32).reshape(LINE, D)
        left_ref[0, rr * LINE : (rr + 1) * LINE, :] = (u * inverse_rms(u)).astype(BF16)
    project(left_ref[0], qkv_ref, w_s, copies)
    for rr in range(2):
        rows = slice(rr * LINE, (rr + 1) * LINE)
        for pair in range(N_PAIR):
            lanes = slice(pair * PAIR, (pair + 1) * PAIR)
            q_half = halves(qkv_ref[0, rows, lanes])
            v_half = halves(qkv_ref[2, rows, lanes])
            k_pair = qkv_ref[1, rows, lanes]
            probs = [softmax(q_half[h], k_pair).astype(BF16) for h in range(2)]
            mixed = dot(probs[0], v_half[0]) + dot(probs[1], v_half[1])
            left_ref[1, rows, lanes] = (mixed * gain_ref[:, lanes]).astype(BF16)
    copies[3].wait()
    added = dot(left_ref[1], w_s[3])
    for rr in range(2):
        u = x_ref[:, rr].astype(F32).reshape(LINE, D)
        mid = (u + added[rr * LINE : (rr + 1) * LINE]).reshape(16, 2, 8, D)
        for cc in range(2):
            for group in range(4):
                piece = mid[:, cc, :, group * 128 : (group + 1) * 128].reshape(128, 128)
                mix_s[pl.ds(slot(cc, group, rr), 128, stride=16), :] = piece
    mid_ref[...] = mix_s[...].reshape(N_DEV, 16, 128).astype(BF16)


def row_prepare_kernel(qkv_ref, left_ref, probs_ref, turned_ref):
    for rr in range(2):
        rows = slice(rr * LINE, (rr + 1) * LINE)
        for pair in range(N_PAIR):
            lanes = slice(pair * PAIR, (pair + 1) * PAIR)
            q_half = halves(qkv_ref[0, rows, lanes])
            k_pair = qkv_ref[1, rows, lanes]
            for h in range(2):
                probs_ref[(rr * N_PAIR + pair) * 2 + h] = softmax(q_half[h], k_pair)
    for which in range(2):
        turned_ref[which] = left_ref[which].T


def attention_backward(rows, lanes, qkv, da_ref, probs_of, right_ref):
    q_half = halves(qkv[0, rows, lanes])
    k_pair = qkv[1, rows, lanes]
    k_half = halves(k_pair)
    v_pair = qkv[2, rows, lanes]
    da_half = halves(da_ref[rows, lanes])
    grads = []
    lows = []
    for h in range(2):
        probs = probs_of(h, q_half, k_pair)
        lows.append(probs.astype(BF16))
        grad_probs = dot_nt(da_half[h], v_pair)
        total = jnp.sum(probs * grad_probs, axis=-1, keepdims=True)
        grads.append((probs * (grad_probs - total)).astype(BF16))
    right_ref[0, rows, lanes] = (
        (dot(grads[0], k_half[0]) + dot(grads[1], k_half[1])) * SCALE
    ).astype(BF16)
    right_ref[1, rows, lanes] = (
        dot_tn(grads[0], q_half[0]) + dot_tn(grads[1], q_half[1])
    ).astype(BF16)
    right_ref[2, rows, lanes] = (
        dot_tn(lows[0], da_half[0]) + dot_tn(lows[1], da_half[1])
    ).astype(BF16)
    return lows


def input_gradient(u, right_ref, w_s, rows):
    inv = inverse_rms(u)
    dn = (
        dot_nt(right_ref[0, rows, :], w_s[0])
        + dot_nt(right_ref[1, rows, :], w_s[1])
        + dot_nt(right_ref[2, rows, :], w_s[2])
    )
    mean = jnp.mean(dn * u, axis=-1, keepdims=True)
    return right_ref[3, rows, :].astype(F32) + inv * dn - u * (inv * inv * inv * mean)


def recomputed(h, q_half, k_pair):
    return softmax(q_half[h], k_pair)


def weight_gradients(core, turned, right_ref, keep_ref, send_ref):
    for side, target in ((1 - core, send_ref), (core, keep_ref)):
        for j in range(2):
            which = side * 2 + j
            target[j] = dot(turned[which // 3], right_ref[which]).astype(BF16)


def row_backward_kernel(
    where_ref, g_ref, qkv_ref, turned_ref, gain_ref, probs_ref, w_ref,
    keep_ref, send_ref, right_ref, mix_s, da_s, wo_s, sem,
):
    copy = pltpu.make_async_copy(w_ref.at[3], wo_s, sem)
    copy.start()
    mix_s[...] = g_ref[...].astype(F32).reshape(N_DEV * 16, 128)
    for rr in range(2):
        pieces = []
        for group in range(4):
            sides = [
                mix_s[pl.ds(slot(cc, group, rr), 128, stride=16), :].reshape(16, 8, 128)
                for cc in range(2)
            ]
            right_ref[3, rr * LINE : (rr + 1) * LINE, group * 128 : (group + 1) * 128] = (
                jnp.stack(sides, axis=1).reshape(LINE, 128).astype(BF16)
            )
    copy.wait()
    da_s[...] = (dot_nt(right_ref[3], wo_s[...]) * gain_ref[...]).astype(BF16)
    for rr in range(2):
        rows = slice(rr * LINE, (rr + 1) * LINE)
        for pair in range(N_PAIR):
            lanes = slice(pair * PAIR, (pair + 1) * PAIR)
            attention_backward(
                rows, lanes, qkv_ref, da_s,
                lambda h, q, k: probs_ref[(rr * N_PAIR + pair) * 2 + h], right_ref,
            )
    weight_gradients(where_ref[2], turned_ref, right_ref, keep_ref, send_ref)


def row_input_gradient_kernel(where_ref, x_ref, right_ref, w_ref, *refs):
    outs, w_s, sems = refs[:8], refs[8], refs[9]
    gin_s = refs[10]
    chip = where_ref[1]
    copies = weight_copies(w_ref, w_s, sems)
    for copy in copies[:3]:
        copy.start()
    for copy in copies[:3]:
        copy.wait()
    for rr in range(2):
        rows = slice(rr * LINE, (rr + 1) * LINE)
        u = x_ref[:, rr].astype(F32).reshape(LINE, D)
        grad_in = input_gradient(u, right_ref, w_s, rows)
        gin_s[:, :, rr] = grad_in.astype(BF16).reshape(8, 2, 16, D)
    for shift in range(8):
        outs[shift][...] = gin_s[lax.rem(chip + shift, 8)]


def col_kernel(where_ref, m_ref, gain_ref, w_ref, *refs):
    parts, refs = refs[:8], refs[8:]
    gmid_ref, left_ref, right_ref, u_ref = refs[:4]
    mix_s, u_s, qkv_s, da_s, w_s, sems = refs[4:]
    me = where_ref[0]
    copies = weight_copies(w_ref, w_s, sems)
    for i in (3, 0, 1, 2):
        copies[i].start()
    for shift in range(8):
        start = lax.rem(me + (8 - shift), 8) * 16
        for cc in range(2):
            for rr in range(2):
                at = pl.multiple_of(start + (cc * LINE + rr * 128), 16)
                right_ref[3, pl.ds(at, 16), :] = parts[shift][cc, rr * 16 : (rr + 1) * 16, :]
    copies[3].wait()
    da_s[...] = (dot_nt(right_ref[3], w_s[3]) * gain_ref[...]).astype(BF16)
    mix_s[...] = m_ref[...].astype(F32).reshape(N_DEV * 16, 128)
    for cc in range(2):
        for rr in range(2):
            base = cc * LINE + rr * 128
            for group in range(4):
                for grid_row in range(N_ROW):
                    start = base + grid_row * 16
                    u_s[start : start + 16, group * 128 : (group + 1) * 128] = mix_s[
                        pl.ds(grid_row * 16 + slot(cc, group, rr), 16, stride=128), :
                    ]
    u = u_s[...]
    u_ref[...] = u.astype(BF16)
    left_ref[0] = (u * inverse_rms(u)).astype(BF16)
    project(left_ref[0], qkv_s, w_s, copies)
    for cc in range(2):
        rows = slice(cc * LINE, (cc + 1) * LINE)
        for pair in range(N_PAIR):
            lanes = slice(pair * PAIR, (pair + 1) * PAIR)
            lows = attention_backward(rows, lanes, qkv_s, da_s, recomputed, right_ref)
            v_half = halves(qkv_s[2, rows, lanes])
            mixed = dot(lows[0], v_half[0]) + dot(lows[1], v_half[1])
            left_ref[1, rows, lanes] = (mixed * gain_ref[:, lanes]).astype(BF16)
    for cc in range(2):
        rows = slice(cc * LINE, (cc + 1) * LINE)
        grad_in = input_gradient(u_s[rows, :], right_ref, w_s, rows)
        for rr in range(2):
            for group in range(4):
                for grid_row in range(N_ROW):
                    start = rr * 128 + grid_row * 16
                    mix_s[pl.ds(grid_row * 16 + slot(cc, group, rr), 16, stride=128), :] = grad_in[
                        start : start + 16, group * 128 : (group + 1) * 128
                    ]
    gmid_ref[...] = mix_s[...].reshape(N_DEV, 16, 128).astype(BF16)


def col_output_kernel(where_ref, left_ref, right_ref, u_ref, w_ref, *refs):
    keep_ref, send_ref, outs = refs[0], refs[1], refs[2:10]
    turned_s, out_s, wo_s, sem = refs[10:]
    me, core = where_ref[0], where_ref[2]
    copy = pltpu.make_async_copy(w_ref.at[3], wo_s, sem)
    copy.start()
    for which in range(2):
        turned_s[which] = left_ref[which].T
    weight_gradients(core, turned_s, right_ref, keep_ref, send_ref)
    copy.wait()
    out_s[...] = (u_ref[...].astype(F32) + dot(left_ref[1], wo_s[...])).astype(BF16)
    for shift in range(8):
        start = lax.rem(me + shift, 8) * 16
        for cc in range(2):
            for rr in range(2):
                at = pl.multiple_of(start + (cc * LINE + rr * 128), 16)
                outs[shift][cc, rr * 16 : (rr + 1) * 16, :] = out_s[pl.ds(at, 16), :]


def tile_to_lines_kernel(where_ref, tile_ref, *refs):
    outs, mix_s = refs[:8], refs[8]
    me = where_ref[0]
    tile = tile_ref[...].astype(F32).reshape(TOK, D)
    for group in range(4):
        lanes = slice(group * 128, (group + 1) * 128)
        mix_s[group] = tile[:, lanes]
        for shift in range(8):
            peer = lax.rem(me + shift, 8)
            for cc in range(2):
                for rr in range(2):
                    piece = mix_s[group, pl.ds(peer + (rr * 16 + cc * 8), 16, stride=32), :]
                    outs[shift][cc, rr * 16 : (rr + 1) * 16, lanes] = piece.astype(BF16)


def lines_to_tile_kernel(where_ref, *refs):
    parts, tile_ref, mix_s = refs[:8], refs[8], refs[9]
    me = where_ref[0]
    for group in range(4):
        lanes = slice(group * 128, (group + 1) * 128)
        for shift in range(8):
            peer = lax.rem(me + (8 - shift), 8)
            for cc in range(2):
                for rr in range(2):
                    piece = parts[shift][cc, rr * 16 : (rr + 1) * 16, lanes].astype(F32)
                    mix_s[group, pl.ds(peer + (rr * 16 + cc * 8), 16, stride=32), :] = piece
        tile_ref[:, :, lanes] = mix_s[group].astype(BF16).reshape(32, 16, 128)


def forward_kernel(where_ref, *refs):
    parts, pass_ref, mine_ref = refs[:8], refs[8], refs[9]
    chip, core = where_ref[1], where_ref[2]
    for shift in range(8):
        source = lax.rem(chip + (8 - shift), 8)
        pass_ref[source] = parts[shift][1 - core]
        mine_ref[source] = parts[shift][core]


def join_kernel(where_ref, mine_ref, passed_ref, tile_ref):
    core = where_ref[2]
    for source in range(8):
        tile_ref[source, core] = mine_ref[source]
        tile_ref[source, 1 - core] = passed_ref[source]


def pair_sum_kernel(keep_ref, got_ref, sum_ref):
    total = keep_ref[...].astype(F32) + got_ref[...].astype(F32)
    sum_ref[...] = total.astype(BF16).reshape(64, 16, D)


def chip_sum(parts_ref, first):
    total = parts_ref[0, first : first + 16, :].astype(F32)
    for chip in range(1, 64):
        total = total + parts_ref[chip, first : first + 16, :].astype(F32)
    return total.astype(BF16)


def merge_kernel(keep_ref, got_ref, parts_ref, both_ref):
    total = keep_ref[...].astype(F32) + got_ref[...].astype(F32)
    both_ref[:, 0:16, :] = total.astype(BF16).reshape(64, 16, D)
    both_ref[:, 16:32, :] = jnp.broadcast_to(chip_sum(parts_ref, 0)[None], (64, 16, D))


def spread_kernel(both_ref, spread_ref):
    spread_ref[...] = jnp.broadcast_to(chip_sum(both_ref, 0)[None], (64, 16, D))


def pick_kernel(both_ref, half_ref):
    half_ref[...] = both_ref[:, 16:32, :]


def widen_kernel(where_ref, own_ref, got_ref, out_ref):
    core = where_ref[2]
    out_ref[core] = own_ref[...].reshape(256, D).astype(F32)
    out_ref[1 - core] = got_ref[...].reshape(256, D).astype(F32)


MIB = 1 << 20
SMEM = pl.BlockSpec(memory_space=pltpu.SMEM)
VMEM = pl.BlockSpec(memory_space=pltpu.VMEM)
HBM = pl.BlockSpec(memory_space=pltpu.HBM)


def call(kernel, ins, outs, scratch, flops, moved, name, limit=24):
    return pl.pallas_call(
        kernel,
        in_specs=[{"s": SMEM, "v": VMEM, "h": HBM}[kind] for kind in ins],
        out_specs=jax.tree.map(lambda _: VMEM, outs),
        out_shape=outs,
        scratch_shapes=scratch,
        name=name,
        compiler_params=pltpu.CompilerParams(vmem_limit_bytes=limit * MIB),
        cost_estimate=pl.CostEstimate(flops=flops, bytes_accessed=moved, transcendentals=0),
    )


def shape(*dims, dtype=BF16):
    return jax.ShapeDtypeStruct(dims, dtype)


MATMUL = 2 * TOK * D * D
ATTEND = 2 * 16 * LINE * LINE * HEAD
MIX = pltpu.VMEM((N_DEV * 16, 128), F32)
MIX_TILE = pltpu.VMEM((4, TOK, 128), F32)
WEIGHTS = [pltpu.VMEM((4, D, D), BF16), pltpu.SemaphoreType.DMA((4,))]
WEIGHT = [pltpu.VMEM((D, D), BF16), pltpu.SemaphoreType.DMA]
PIECE = shape(2, 32, D)
HALF = shape(2, D, D)

row_forward = call(
    row_forward_kernel,
    "vvh",
    (shape(N_DEV, 16, 128), shape(3, TOK, D), shape(2, TOK, D)),
    [MIX, *WEIGHTS],
    4 * MATMUL + 2 * ATTEND,
    6 * MIB,
    "row_forward",
)
row_prepare = call(
    row_prepare_kernel,
    "vv",
    (shape(16, LINE, LINE, dtype=F32), shape(2, D, TOK)),
    [],
    ATTEND,
    8 * MIB,
    "row_prepare",
)
row_backward = call(
    row_backward_kernel,
    "svvvvvh",
    (HALF, HALF, shape(4, TOK, D)),
    [MIX, pltpu.VMEM((TOK, D), BF16), *WEIGHT],
    5 * MATMUL + 5 * ATTEND,
    12 * MIB,
    "row_backward",
)
row_input_gradient = call(
    row_input_gradient_kernel,
    "svvh",
    (shape(2, 2, 16, D),) * 8,
    [*WEIGHTS, pltpu.VMEM((8, 2, 2, 16, D), BF16)],
    3 * MATMUL,
    5 * MIB,
    "row_input_gradient",
)
col_grad = call(
    col_kernel,
    "svvh" + "v" * 8,
    (shape(N_DEV, 16, 128), shape(2, TOK, D), shape(4, TOK, D), shape(TOK, D)),
    [
        MIX,
        pltpu.VMEM((TOK, D), F32),
        pltpu.VMEM((3, TOK, D), BF16),
        pltpu.VMEM((TOK, D), BF16),
        *WEIGHTS,
    ],
    8 * MATMUL + 6 * ATTEND,
    8 * MIB,
    "col_grad",
)
col_output = call(
    col_output_kernel,
    "svvvh",
    (HALF, HALF) + (PIECE,) * 8,
    [pltpu.VMEM((2, D, TOK), BF16), pltpu.VMEM((TOK, D), BF16), *WEIGHT],
    5 * MATMUL,
    7 * MIB,
    "col_output",
)
tile_to_lines = call(
    tile_to_lines_kernel, "sv", (PIECE,) * 8, [MIX_TILE], 0, MIB, "tile_to_lines"
)
lines_to_tile = call(
    lines_to_tile_kernel, "s" + "v" * 8, shape(32, 16, D), [MIX_TILE], 0, MIB, "lines_to_tile"
)
forward = call(
    forward_kernel,
    "s" + "v" * 8,
    (shape(8, 2, 16, D), shape(8, 2, 16, D)),
    [],
    0,
    MIB,
    "forward",
)
join = call(join_kernel, "svv", shape(8, 2, 2, 16, D), [], 0, MIB, "join")
pair_sum = call(pair_sum_kernel, "vv", shape(64, 16, D), [], 0, 3 * MIB, "pair_sum")
merge = call(merge_kernel, "vvv", shape(64, 32, D), [], 0, 5 * MIB, "merge")
spread = call(spread_kernel, "v", shape(64, 16, D), [], 0, 3 * MIB, "spread")
pick = call(pick_kernel, "v", shape(64, 16, D), [], 0, 3 * MIB, "pick")


def widen(where, own, got):
    block = pl.BlockSpec((16, 16, D), lambda i: (i, 0, 0))
    return pl.pallas_call(
        widen_kernel,
        grid=(4,),
        in_specs=[SMEM, block, block],
        out_specs=pl.BlockSpec((2, 256, D), lambda i: (0, i, 0)),
        out_shape=shape(2, 1024, D, dtype=F32),
        name="widen",
        compiler_params=pltpu.CompilerParams(vmem_limit_bytes=8 * MIB),
        cost_estimate=pl.CostEstimate(flops=0, bytes_accessed=6 * MIB, transcendentals=0),
    )(where, own, got).reshape(4, D, D)


def exchange(values, axes):
    return lax.all_to_all(values, axes, split_axis=0, concat_axis=0, tiled=True)


def shifted(pieces, axes):
    n = len(pieces)
    return [pieces[0]] + [
        lax.ppermute(pieces[k], axes, [(i, (i + k) % n) for i in range(n)]) for k in range(1, n)
    ]


def swap(value):
    return lax.ppermute(value, "c", [(0, 1), (1, 0)])


def body(latents, cotangent, w_row, w_col, keep_heads):
    where = jnp.stack(
        [lax.axis_index(ROW), lax.axis_index(("zh", "x")), lax.axis_index("c")]
    ).astype(jnp.int32)
    gain = jnp.repeat(keep_heads.astype(F32), HEAD, axis=1)
    gain_row, gain_col = gain[0:1], gain[1:2]
    rows_in = exchange(latents.reshape(16, 2, 16, D), COL)
    grad_parts = shifted(tile_to_lines(where, cotangent), ROW)
    mid_send, qkv_row, left_row = row_forward(rows_in, gain_row, w_row)
    mid_lines = exchange(mid_send, BOTH)
    probs_row, turned_row = row_prepare(qkv_row, left_row)
    grad_send, left_col, right_col, u_col = col_grad(where, mid_lines, gain_col, w_col, *grad_parts)
    grad_rows = exchange(grad_send, BOTH)
    keep_col, send_col, *out_parts = col_output(where, left_col, right_col, u_col, w_col)
    sums_col = exchange(pair_sum(keep_col, swap(send_col)), CHIPS)
    keep_row, send_row, right_row = row_backward(
        where, grad_rows, qkv_row, turned_row, gain_row, probs_row, w_row
    )
    both = exchange(merge(keep_row, swap(send_row), sums_col), CHIPS)
    own_row = exchange(spread(both), CHIPS)
    gin_parts = shifted(row_input_gradient(where, rows_in, right_row, w_row), ("zh", "x"))
    passed, mine = forward(where, *gin_parts)
    grad_latents = join(where, mine, swap(passed)).reshape(32, 16, D)
    output = lines_to_tile(where, *shifted(out_parts, ROW))
    own_col = pick(both)
    grad_col = widen(where, own_col, swap(own_col))
    grad_row = widen(where, own_row, swap(own_row))
    return (output, grad_latents, grad_row, grad_col)


def solution(mesh):
    fine = Mesh(mesh.devices.reshape(4, 2, 2, 4, 2), ("y", "zl", "zh", "x", "c"))
    tile = P(ROW, COL, None)
    return jax.shard_map(
        body,
        mesh=fine,
        in_specs=(tile, tile, P(), P(), P()),
        out_specs=(tile, tile, P(), P()),
        check_vma=False,
    )
```

```python
import jax
import jax.numpy as jnp
from jax import lax
from jax.experimental import pallas as pl
from jax.experimental.pallas import tpu as pltpu
from jax.sharding import Mesh, PartitionSpec as P


HEAD = 64
D = 512
PAIR = 128
N_PAIR = D // PAIR
LINE = 256
TOK = 512
N_ROW = 8
N_COL = 16
N_DEV = N_ROW * N_COL
EPSILON = 1e-06
SCALE = HEAD ** (-0.5)

F32 = jnp.float32
BF16 = jnp.bfloat16

ROW = ("y", "zl")
COL = ("zh", "x", "c")
BOTH = COL + ROW
CHIPS = ("y", "zl", "zh", "x")


def dot(left, right):
    return lax.dot_general(left, right, (((1,), (0,)), ((), ())), preferred_element_type=F32)


def dot_nt(left, right):
    return lax.dot_general(left, right, (((1,), (1,)), ((), ())), preferred_element_type=F32)


def dot_tn(left, right):
    return lax.dot_general(left, right, (((0,), (0,)), ((), ())), preferred_element_type=F32)


def halves(value):
    lane = lax.broadcasted_iota(jnp.int32, value.shape, 1)
    zero = jnp.zeros_like(value)
    return (jnp.where(lane < HEAD, value, zero), jnp.where(lane >= HEAD, value, zero))


def inverse_rms(values_f):
    return lax.rsqrt(jnp.mean(values_f * values_f, axis=-1, keepdims=True) + EPSILON)


def softmax(q_half, k_pair):
    scores = dot_nt(q_half, k_pair)
    peak = jnp.max(scores, axis=-1, keepdims=True)
    grown = jnp.exp(scores - peak)
    return grown * (1.0 / jnp.sum(grown, axis=-1, keepdims=True))


def slot(col_local, group, row_local):
    return col_local * 8 + group * 2 + row_local


def copies_of(source, target, sems, count):
    return [pltpu.make_async_copy(source.at[i], target.at[i], sems.at[i]) for i in range(count)]


def start_all(copies):
    for copy in copies:
        copy.start()


def wait_all(copies):
    for copy in copies:
        copy.wait()


def project(normed, qkv_ref, w_s, copies):
    copies[0].wait()
    qkv_ref[0] = (dot(normed, w_s[0]).astype(BF16).astype(F32) * SCALE).astype(BF16)
    copies[1].wait()
    qkv_ref[1] = dot(normed, w_s[1]).astype(BF16)
    copies[2].wait()
    qkv_ref[2] = dot(normed, w_s[2]).astype(BF16)


PER_STEP = 2


def each_pair(visit):
    def step(index, carry):
        line = index // (N_PAIR // PER_STEP)
        first = lax.rem(index, N_PAIR // PER_STEP) * PER_STEP
        rows = pl.ds(pl.multiple_of(line * LINE, LINE), LINE)
        for offset in range(PER_STEP):
            pair = first + offset
            lanes = pl.ds(pl.multiple_of(pair * PAIR, PAIR), PAIR)
            visit(rows, lanes, (line * N_PAIR + pair) * 2)
        return carry

    lax.fori_loop(0, 2 * N_PAIR // PER_STEP, step, 0)


def row_forward_kernel(
    x_ref, gain_ref, w_ref, mid_ref, qkv_ref, left_ref,
    mix_s, mid_s, qkv_s, left_s, w_s, w_sem, mid_sem, qkv_sem, left_sem,
):
    weights = copies_of(w_ref, w_s, w_sem, 4)
    start_all(weights)
    saved = copies_of(qkv_s, qkv_ref, qkv_sem, 3)
    lefts = copies_of(left_s, left_ref, left_sem, 2)
    for rr in range(2):
        u = x_ref[:, rr].astype(F32).reshape(LINE, D)
        left_s[0, rr * LINE : (rr + 1) * LINE, :] = (u * inverse_rms(u)).astype(BF16)
    project(left_s[0], qkv_s, w_s, weights)
    lefts[0].start()
    start_all(saved)

    def visit(rows, lanes, head):
        q_half = halves(qkv_s[0, rows, lanes])
        v_half = halves(qkv_s[2, rows, lanes])
        k_pair = qkv_s[1, rows, lanes]
        probs = [softmax(q_half[h], k_pair).astype(BF16) for h in range(2)]
        mixed = dot(probs[0], v_half[0]) + dot(probs[1], v_half[1])
        left_s[1, rows, lanes] = (mixed * gain_ref[:, lanes]).astype(BF16)

    each_pair(visit)
    lefts[1].start()
    weights[3].wait()
    added = dot(left_s[1], w_s[3])
    for rr in range(2):
        u = x_ref[:, rr].astype(F32).reshape(LINE, D)
        mid = (u + added[rr * LINE : (rr + 1) * LINE]).reshape(16, 2, 8, D)
        for cc in range(2):
            for group in range(4):
                piece = mid[:, cc, :, group * 128 : (group + 1) * 128].reshape(128, 128)
                mix_s[pl.ds(slot(cc, group, rr), 128, stride=16), :] = piece
    sends = []
    for part in range(4):
        rows = slice(part * 32, (part + 1) * 32)
        mid_s[rows] = mix_s[part * 512 : (part + 1) * 512, :].reshape(32, 16, 128).astype(BF16)
        sends.append(pltpu.make_async_copy(mid_s.at[rows], mid_ref.at[rows], mid_sem.at[part]))
        sends[-1].start()
    wait_all(saved + lefts + sends)


def row_prepare_kernel(qkv_ref, left_ref, probs_ref, turned_ref):
    def visit(rows, lanes, head):
        q_half = halves(qkv_ref[0, rows, lanes])
        k_pair = qkv_ref[1, rows, lanes]
        for h in range(2):
            probs_ref[head + h] = softmax(q_half[h], k_pair)

    each_pair(visit)
    for which in range(2):
        turned_ref[which] = left_ref[which].T


def attention_backward(rows, lanes, qkv, da_ref, probs_of, right_ref):
    q_half = halves(qkv[0, rows, lanes])
    k_pair = qkv[1, rows, lanes]
    k_half = halves(k_pair)
    v_pair = qkv[2, rows, lanes]
    da_half = halves(da_ref[rows, lanes])
    grads = []
    lows = []
    for h in range(2):
        probs = probs_of(h, q_half, k_pair)
        lows.append(probs.astype(BF16))
        grad_probs = dot_nt(da_half[h], v_pair)
        total = jnp.sum(probs * grad_probs, axis=-1, keepdims=True)
        grads.append((probs * (grad_probs - total)).astype(BF16))
    right_ref[0, rows, lanes] = (
        (dot(grads[0], k_half[0]) + dot(grads[1], k_half[1])) * SCALE
    ).astype(BF16)
    right_ref[1, rows, lanes] = (
        dot_tn(grads[0], q_half[0]) + dot_tn(grads[1], q_half[1])
    ).astype(BF16)
    right_ref[2, rows, lanes] = (
        dot_tn(lows[0], da_half[0]) + dot_tn(lows[1], da_half[1])
    ).astype(BF16)
    return lows


def input_gradient(u, right_ref, w_s, rows):
    inv = inverse_rms(u)
    dn = (
        dot_nt(right_ref[0, rows, :], w_s[0])
        + dot_nt(right_ref[1, rows, :], w_s[1])
        + dot_nt(right_ref[2, rows, :], w_s[2])
    )
    mean = jnp.mean(dn * u, axis=-1, keepdims=True)
    return right_ref[3, rows, :].astype(F32) + inv * dn - u * (inv * inv * inv * mean)


def recomputed(h, q_half, k_pair):
    return softmax(q_half[h], k_pair)


def weight_gradients(side, turned, right_ref, target):
    for j in range(2):
        which = side * 2 + j
        target[j] = dot(turned[which // 3], right_ref[which]).astype(BF16)


def row_backward_kernel(
    where_ref, g_ref, gain_ref, qkv_ref, turned_ref, probs_ref, w_ref,
    keep_ref, send_ref, right_ref,
    mix_s, da_s, wo_s, qkv_s, turned_s, probs_s, keep_s, send_s, right_s,
    wo_sem, qkv_sem, turned_sem, probs_sem, half_sem, right_sem,
):
    weight = pltpu.make_async_copy(w_ref.at[3], wo_s, wo_sem)
    weight.start()
    saved = copies_of(qkv_ref, qkv_s, qkv_sem, 3)
    start_all(saved)
    probs = [
        pltpu.make_async_copy(
            probs_ref.at[i * 4 : (i + 1) * 4], probs_s.at[i * 4 : (i + 1) * 4], probs_sem.at[i]
        )
        for i in range(4)
    ]
    start_all(probs)
    turned = copies_of(turned_ref, turned_s, turned_sem, 2)
    start_all(turned)
    mix_s[...] = g_ref[...].astype(F32).reshape(N_DEV * 16, 128)
    for rr in range(2):
        for group in range(4):
            sides = [
                mix_s[pl.ds(slot(cc, group, rr), 128, stride=16), :].reshape(16, 8, 128)
                for cc in range(2)
            ]
            right_s[3, rr * LINE : (rr + 1) * LINE, group * 128 : (group + 1) * 128] = (
                jnp.stack(sides, axis=1).reshape(LINE, 128).astype(BF16)
            )
    weight.wait()
    da_s[...] = (dot_nt(right_s[3], wo_s[...]) * gain_ref[...]).astype(BF16)
    wait_all(saved + probs)

    def visit(rows, lanes, head):
        attention_backward(
            rows, lanes, qkv_s, da_s, lambda h, q, k: probs_s[head + h], right_s
        )

    each_pair(visit)
    rights = copies_of(right_s, right_ref, right_sem, 4)
    start_all(rights)
    wait_all(turned)
    core = where_ref[2]
    weight_gradients(1 - core, turned_s, right_s, send_s)
    sent = pltpu.make_async_copy(send_s, send_ref, half_sem.at[0])
    sent.start()
    weight_gradients(core, turned_s, right_s, keep_s)
    kept = pltpu.make_async_copy(keep_s, keep_ref, half_sem.at[1])
    kept.start()
    wait_all(rights + [sent, kept])


def row_input_gradient_kernel(where_ref, x_ref, right_ref, w_ref, *refs):
    outs, w_s, sems = refs[:8], refs[8], refs[9]
    gin_s = refs[10]
    chip = where_ref[1]
    copies = copies_of(w_ref, w_s, sems, 3)
    start_all(copies)
    wait_all(copies)
    for rr in range(2):
        rows = slice(rr * LINE, (rr + 1) * LINE)
        u = x_ref[:, rr].astype(F32).reshape(LINE, D)
        grad_in = input_gradient(u, right_ref, w_s, rows)
        gin_s[:, :, rr] = grad_in.astype(BF16).reshape(8, 2, 16, D)
    for shift in range(8):
        outs[shift][...] = gin_s[lax.rem(chip + shift, 8)]


def col_kernel(where_ref, m_ref, gain_ref, w_ref, *refs):
    parts, refs = refs[:8], refs[8:]
    gmid_ref, left_ref, right_ref, u_ref = refs[:4]
    mix_s, u_s, ulow_s, left_s, right_s, qkv_s, da_s, w_s = refs[4:12]
    w_sem, left_sem, right_sem, u_sem = refs[12:]
    me = where_ref[0]
    weights = copies_of(w_ref, w_s, w_sem, 4)
    for i in (3, 0, 1, 2):
        weights[i].start()
    lefts = copies_of(left_s, left_ref, left_sem, 2)
    rights = copies_of(right_s, right_ref, right_sem, 4)
    for shift in range(8):
        start = lax.rem(me + (8 - shift), 8) * 16
        for cc in range(2):
            for rr in range(2):
                at = pl.multiple_of(start + (cc * LINE + rr * 128), 16)
                right_s[3, pl.ds(at, 16), :] = parts[shift][cc, rr * 16 : (rr + 1) * 16, :]
    rights[3].start()
    weights[3].wait()
    da_s[...] = (dot_nt(right_s[3], w_s[3]) * gain_ref[...]).astype(BF16)
    mix_s[...] = m_ref[...].astype(F32).reshape(N_DEV * 16, 128)
    for cc in range(2):
        for rr in range(2):
            base = cc * LINE + rr * 128
            for group in range(4):
                for grid_row in range(N_ROW):
                    start = base + grid_row * 16
                    u_s[start : start + 16, group * 128 : (group + 1) * 128] = mix_s[
                        pl.ds(grid_row * 16 + slot(cc, group, rr), 16, stride=128), :
                    ]
    u = u_s[...]
    ulow_s[...] = u.astype(BF16)
    kept_u = pltpu.make_async_copy(ulow_s, u_ref, u_sem)
    kept_u.start()
    left_s[0] = (u * inverse_rms(u)).astype(BF16)
    lefts[0].start()
    project(left_s[0], qkv_s, w_s, weights)

    def visit(rows, lanes, head):
        lows = attention_backward(rows, lanes, qkv_s, da_s, recomputed, right_s)
        v_half = halves(qkv_s[2, rows, lanes])
        mixed = dot(lows[0], v_half[0]) + dot(lows[1], v_half[1])
        left_s[1, rows, lanes] = (mixed * gain_ref[:, lanes]).astype(BF16)

    each_pair(visit)
    lefts[1].start()
    start_all(rights[:3])
    for cc in range(2):
        rows = slice(cc * LINE, (cc + 1) * LINE)
        grad_in = input_gradient(u_s[rows, :], right_s, w_s, rows)
        for rr in range(2):
            for group in range(4):
                for grid_row in range(N_ROW):
                    start = rr * 128 + grid_row * 16
                    mix_s[pl.ds(grid_row * 16 + slot(cc, group, rr), 16, stride=128), :] = grad_in[
                        start : start + 16, group * 128 : (group + 1) * 128
                    ]
    gmid_ref[...] = mix_s[...].reshape(N_DEV, 16, 128).astype(BF16)
    wait_all(lefts + rights + [kept_u])


def col_output_kernel(where_ref, left_ref, right_ref, u_ref, w_ref, *refs):
    keep_ref, send_ref, outs = refs[0], refs[1], refs[2:10]
    turned_s, out_s, wo_s, sem = refs[10:]
    me, core = where_ref[0], where_ref[2]
    copy = pltpu.make_async_copy(w_ref.at[3], wo_s, sem)
    copy.start()
    for which in range(2):
        turned_s[which] = left_ref[which].T
    weight_gradients(1 - core, turned_s, right_ref, send_ref)
    weight_gradients(core, turned_s, right_ref, keep_ref)
    copy.wait()
    out_s[...] = (u_ref[...].astype(F32) + dot(left_ref[1], wo_s[...])).astype(BF16)
    for shift in range(8):
        start = lax.rem(me + shift, 8) * 16
        for cc in range(2):
            for rr in range(2):
                at = pl.multiple_of(start + (cc * LINE + rr * 128), 16)
                outs[shift][cc, rr * 16 : (rr + 1) * 16, :] = out_s[pl.ds(at, 16), :]


def tile_to_lines_kernel(where_ref, tile_ref, *refs):
    outs, mix_s = refs[:8], refs[8]
    me = where_ref[0]
    tile = tile_ref[...].astype(F32).reshape(TOK, D)
    for group in range(4):
        lanes = slice(group * 128, (group + 1) * 128)
        mix_s[group] = tile[:, lanes]
        for shift in range(8):
            peer = lax.rem(me + shift, 8)
            for cc in range(2):
                for rr in range(2):
                    piece = mix_s[group, pl.ds(peer + (rr * 16 + cc * 8), 16, stride=32), :]
                    outs[shift][cc, rr * 16 : (rr + 1) * 16, lanes] = piece.astype(BF16)


def lines_to_tile_kernel(where_ref, *refs):
    parts, tile_ref, mix_s = refs[:8], refs[8], refs[9]
    me = where_ref[0]
    for group in range(4):
        lanes = slice(group * 128, (group + 1) * 128)
        for shift in range(8):
            peer = lax.rem(me + (8 - shift), 8)
            for cc in range(2):
                for rr in range(2):
                    piece = parts[shift][cc, rr * 16 : (rr + 1) * 16, lanes].astype(F32)
                    mix_s[group, pl.ds(peer + (rr * 16 + cc * 8), 16, stride=32), :] = piece
        tile_ref[:, :, lanes] = mix_s[group].astype(BF16).reshape(32, 16, 128)


def forward_kernel(where_ref, *refs):
    parts, pass_ref, mine_ref = refs[:8], refs[8], refs[9]
    chip, core = where_ref[1], where_ref[2]
    for shift in range(8):
        source = lax.rem(chip + (8 - shift), 8)
        pass_ref[source] = parts[shift][1 - core]
        mine_ref[source] = parts[shift][core]


def join_kernel(where_ref, mine_ref, passed_ref, tile_ref):
    core = where_ref[2]
    for source in range(8):
        tile_ref[source, core] = mine_ref[source]
        tile_ref[source, 1 - core] = passed_ref[source]


def pair_sum_kernel(keep_ref, got_ref, sum_ref):
    total = keep_ref[...].astype(F32) + got_ref[...].astype(F32)
    sum_ref[...] = total.astype(BF16).reshape(64, 16, D)


def chip_sum(parts_ref, first):
    total = parts_ref[0, first : first + 16, :].astype(F32)
    for chip in range(1, 64):
        total = total + parts_ref[chip, first : first + 16, :].astype(F32)
    return total.astype(BF16)


def pair_sum_first_kernel(keep_ref, got_ref, both_ref, sum_s, sem):
    total = keep_ref[...].astype(F32) + got_ref[...].astype(F32)
    sum_s[...] = total.astype(BF16).reshape(64, 16, D)
    copy = pltpu.make_async_copy(sum_s, both_ref.at[:, 0:16, :], sem)
    copy.start()
    copy.wait()


def spread_second_kernel(parts_ref, first_ref, both_ref, sum_s, sem):
    sum_s[...] = jnp.broadcast_to(chip_sum(parts_ref, 0)[None], (64, 16, D))
    copy = pltpu.make_async_copy(sum_s, both_ref.at[:, 16:32, :], sem)
    copy.start()
    copy.wait()


def spread_kernel(both_ref, spread_ref):
    spread_ref[...] = jnp.broadcast_to(chip_sum(both_ref, 0)[None], (64, 16, D))


def pick_kernel(both_ref, half_ref):
    half_ref[...] = both_ref[:, 16:32, :]


def widen_kernel(where_ref, own_ref, got_ref, out_ref):
    core = where_ref[2]
    out_ref[core] = own_ref[...].reshape(256, D).astype(F32)
    out_ref[1 - core] = got_ref[...].reshape(256, D).astype(F32)


MIB = 1 << 20
SMEM = pl.BlockSpec(memory_space=pltpu.SMEM)
VMEM = pl.BlockSpec(memory_space=pltpu.VMEM)
HBM = pl.BlockSpec(memory_space=pltpu.HBM)


SPACE = {"s": SMEM, "v": VMEM, "h": HBM}


def call(kernel, ins, out_kinds, outs, scratch, flops, moved, limit=24, aliases=None):
    spaces = tuple(SPACE[kind] for kind in out_kinds)
    return pl.pallas_call(
        kernel,
        in_specs=[SPACE[kind] for kind in ins],
        out_specs=spaces if isinstance(outs, tuple) else spaces[0],
        out_shape=outs,
        scratch_shapes=scratch,
        input_output_aliases=aliases or {},
        compiler_params=pltpu.CompilerParams(vmem_limit_bytes=limit * MIB),
        cost_estimate=pl.CostEstimate(flops=flops, bytes_accessed=moved, transcendentals=0),
    )


def shape(*dims, dtype=BF16):
    return jax.ShapeDtypeStruct(dims, dtype)


MATMUL = 2 * TOK * D * D
ATTEND = 2 * 16 * LINE * LINE * HEAD
MIX = pltpu.VMEM((N_DEV * 16, 128), F32)
MIX_TILE = pltpu.VMEM((4, TOK, 128), F32)
DMA = pltpu.SemaphoreType.DMA
WEIGHTS = [pltpu.VMEM((4, D, D), BF16), DMA((4,))]
WEIGHT = [pltpu.VMEM((D, D), BF16), DMA]
PIECE = shape(2, 32, D)
HALF = shape(2, D, D)
HALF_S = pltpu.VMEM((2, D, D), BF16)


def token_scratch(*lead, dtype=BF16):
    return pltpu.VMEM((*lead, TOK, D), dtype)


row_forward = call(
    row_forward_kernel,
    "vvh",
    "hhh",
    (shape(N_DEV, 16, 128), shape(3, TOK, D), shape(2, TOK, D)),
    [
        MIX, pltpu.VMEM((N_DEV, 16, 128), BF16), token_scratch(3), token_scratch(2), *WEIGHTS,
        DMA((4,)), DMA((3,)), DMA((2,)),
    ],
    4 * MATMUL + 2 * ATTEND,
    6 * MIB,
)
row_prepare = call(
    row_prepare_kernel,
    "vv",
    "vv",
    (shape(16, LINE, LINE, dtype=F32), shape(2, D, TOK)),
    [],
    ATTEND,
    8 * MIB,
)
row_backward = call(
    row_backward_kernel,
    "svvhhhh",
    "hhh",
    (HALF, HALF, shape(4, TOK, D)),
    [
        MIX, token_scratch(), pltpu.VMEM((D, D), BF16), token_scratch(3),
        pltpu.VMEM((2, D, TOK), BF16), pltpu.VMEM((16, LINE, LINE), F32), HALF_S, HALF_S,
        token_scratch(4), DMA, DMA((3,)), DMA((2,)), DMA((4,)), DMA((2,)), DMA((4,)),
    ],
    5 * MATMUL + 5 * ATTEND,
    12 * MIB,
    limit=32,
)
row_input_gradient = call(
    row_input_gradient_kernel,
    "svvh",
    "v" * 8,
    (shape(2, 2, 16, D),) * 8,
    [*WEIGHTS, pltpu.VMEM((8, 2, 2, 16, D), BF16)],
    3 * MATMUL,
    5 * MIB,
)
col_grad = call(
    col_kernel,
    "svvh" + "v" * 8,
    "vhhh",
    (shape(N_DEV, 16, 128), shape(2, TOK, D), shape(4, TOK, D), shape(TOK, D)),
    [
        MIX, token_scratch(dtype=F32), token_scratch(), token_scratch(2), token_scratch(4),
        token_scratch(3), token_scratch(), *WEIGHTS, DMA((2,)), DMA((4,)), DMA,
    ],
    8 * MATMUL + 6 * ATTEND,
    8 * MIB,
    limit=32,
)
col_output = call(
    col_output_kernel,
    "svvvh",
    "v" * 10,
    (HALF, HALF) + (PIECE,) * 8,
    [pltpu.VMEM((2, D, TOK), BF16), token_scratch(), *WEIGHT],
    5 * MATMUL,
    7 * MIB,
)
tile_to_lines = call(tile_to_lines_kernel, "sv", "v" * 8, (PIECE,) * 8, [MIX_TILE], 0, MIB)
lines_to_tile = call(lines_to_tile_kernel, "s" + "v" * 8, "v", shape(32, 16, D), [MIX_TILE], 0, MIB)
forward = call(
    forward_kernel, "s" + "v" * 8, "vv", (shape(8, 2, 16, D), shape(8, 2, 16, D)), [], 0, MIB
)
join = call(join_kernel, "svv", "v", shape(8, 2, 2, 16, D), [], 0, MIB)
CHUNKS = pltpu.VMEM((64, 16, D), BF16)
pair_sum = call(pair_sum_kernel, "vv", "v", shape(64, 16, D), [], 0, 3 * MIB)
pair_sum_first = call(pair_sum_first_kernel, "vv", "h", shape(64, 32, D), [CHUNKS, DMA], 0, 3 * MIB)
spread_second = call(
    spread_second_kernel, "vh", "h", shape(64, 32, D), [CHUNKS, DMA], 0, 2 * MIB,
    aliases={1: 0},
)
spread = call(spread_kernel, "v", "v", shape(64, 16, D), [], 0, 3 * MIB)
pick = call(pick_kernel, "v", "v", shape(64, 16, D), [], 0, 3 * MIB)


def widen(where, own, got):
    block = pl.BlockSpec((16, 16, D), lambda i: (i, 0, 0))
    return pl.pallas_call(
        widen_kernel,
        grid=(4,),
        in_specs=[SMEM, block, block],
        out_specs=pl.BlockSpec((2, 256, D), lambda i: (0, i, 0)),
        out_shape=shape(2, 1024, D, dtype=F32),
        name="widen",
        compiler_params=pltpu.CompilerParams(vmem_limit_bytes=8 * MIB),
        cost_estimate=pl.CostEstimate(flops=0, bytes_accessed=6 * MIB, transcendentals=0),
    )(where, own, got).reshape(4, D, D)


def exchange(values, axes):
    return lax.all_to_all(values, axes, split_axis=0, concat_axis=0, tiled=True)


def shifted(pieces, axes):
    n = len(pieces)
    return [pieces[0]] + [
        lax.ppermute(pieces[k], axes, [(i, (i + k) % n) for i in range(n)]) for k in range(1, n)
    ]


def swap(value):
    return lax.ppermute(value, "c", [(0, 1), (1, 0)])


def layer(latents, cotangent, w_row, w_col, keep_heads):
    where = jnp.stack(
        [lax.axis_index(ROW), lax.axis_index(("zh", "x")), lax.axis_index("c")]
    ).astype(jnp.int32)
    gain = jnp.repeat(keep_heads.astype(F32), HEAD, axis=1)
    gain_row, gain_col = gain[0:1], gain[1:2]
    rows_in = exchange(latents.reshape(16, 2, 16, D), COL)
    grad_pieces = tile_to_lines(where, cotangent)
    grad_parts = shifted(grad_pieces, ROW)
    mid_send, qkv_row, left_row = row_forward(rows_in, gain_row, w_row)
    mid_lines = exchange(mid_send, BOTH)
    probs_row, turned_row = row_prepare(qkv_row, left_row)
    grad_send, left_col, right_col, u_col = col_grad(where, mid_lines, gain_col, w_col, *grad_parts)
    grad_rows = exchange(grad_send, BOTH)
    keep_col, send_col, *out_pieces = col_output(where, left_col, right_col, u_col, w_col)
    got_col = swap(send_col)
    paired_col = pair_sum(keep_col, got_col)
    sums_col = exchange(paired_col, CHIPS)
    keep_row, send_row, right_row = row_backward(
        where, grad_rows, gain_row, qkv_row, turned_row, probs_row, w_row
    )
    got_row = swap(send_row)
    first = pair_sum_first(keep_row, got_row)
    merged = spread_second(sums_col, first)
    both = exchange(merged, CHIPS)
    spread_row = spread(both)
    own_row = exchange(spread_row, CHIPS)
    gin_pieces = row_input_gradient(where, rows_in, right_row, w_row)
    gin_parts = shifted(gin_pieces, ("zh", "x"))
    passed, mine = forward(where, *gin_parts)
    passed = swap(passed)
    grad_latents = join(where, mine, passed).reshape(32, 16, D)
    out_parts = shifted(out_pieces, ROW)
    output = lines_to_tile(where, *out_parts)
    own_col = pick(both)
    other_col = swap(own_col)
    grad_col = widen(where, own_col, other_col)
    other_row = swap(own_row)
    grad_row = widen(where, own_row, other_row)
    return (output, grad_latents, grad_row, grad_col)


def solution(mesh):
    fine = Mesh(mesh.devices.reshape(4, 2, 2, 4, 2), ("y", "zl", "zh", "x", "c"))
    tile = P(ROW, COL, None)
    return jax.shard_map(
        layer,
        mesh=fine,
        in_specs=(tile, tile, P(), P(), P()),
        out_specs=(tile, tile, P(), P()),
        check_vma=False,
    )
```

```python
import jax
import jax.numpy as jnp
from jax import lax
from jax.experimental import pallas as pl
from jax.experimental.pallas import tpu as pltpu
from jax.sharding import Mesh, PartitionSpec as P


HEADS = 8
HEAD = 64
D = 512
PAIR = 128
N_PAIR = D // PAIR
LINE = 256
TOK = 512
N_ROW = 8
N_COL = 16
N_DEV = N_ROW * N_COL
EPSILON = 1e-06
SCALE = HEAD ** (-0.5)

F32 = jnp.float32
BF16 = jnp.bfloat16

AXES = ("y", "zl", "zh", "x", "c")
ROW = ("y", "zl")
COL = ("zh", "x", "c")
BOTH = COL + ROW
CHIPS = ("y", "zl", "zh", "x")


def dot(left, right):
    return lax.dot_general(left, right, (((1,), (0,)), ((), ())), preferred_element_type=F32)


def dot_nt(left, right):
    return lax.dot_general(left, right, (((1,), (1,)), ((), ())), preferred_element_type=F32)


def stack_halves(value):
    lane = lax.broadcasted_iota(jnp.int32, value.shape, 1)
    zero = jnp.zeros_like(value)
    low, high = jnp.where(lane < HEAD, value, zero), jnp.where(lane >= HEAD, value, zero)
    return jnp.concatenate([low, high], axis=0)


def pick_halves(value):
    low, high = value[:LINE], value[LINE:]
    lane = lax.broadcasted_iota(jnp.int32, low.shape, 1)
    return jnp.where(lane < HEAD, low, high)


def turn_halves(value):
    return jnp.concatenate([value[:LINE].T, value[LINE:].T], axis=0)


def gain_row(keep_ref, block, first, count):
    head = lax.broadcasted_iota(jnp.int32, (1, count * HEAD), 1) // HEAD
    gain = jnp.zeros((1, count * HEAD), F32)
    for i in range(count):
        gain = jnp.where(head == i, keep_ref[block, first + i].astype(F32), gain)
    return gain


def inverse_rms(values_f):
    return lax.rsqrt(jnp.mean(values_f * values_f, axis=-1, keepdims=True) + EPSILON)


def softmax(q_pair, k_pair):
    scores = dot_nt(stack_halves(q_pair), k_pair)
    peak = jnp.max(scores, axis=-1, keepdims=True)
    grown = jnp.exp(scores - peak)
    return grown * (1.0 / jnp.sum(grown, axis=-1, keepdims=True))


def slot(col_local, group, row_local):
    return col_local * 8 + group * 2 + row_local


def copies_of(source, target, sems, count):
    return [pltpu.make_async_copy(source.at[i], target.at[i], sems.at[i]) for i in range(count)]


def start_all(copies):
    for copy in copies:
        copy.start()


def wait_all(copies):
    for copy in copies:
        copy.wait()


def project(normed, qkv_ref, w_s, copies):
    copies[0].wait()
    qkv_ref[0] = (dot(normed, w_s[0]).astype(BF16).astype(F32) * SCALE).astype(BF16)
    copies[1].wait()
    qkv_ref[1] = dot(normed, w_s[1]).astype(BF16)
    copies[2].wait()
    qkv_ref[2] = dot(normed, w_s[2]).astype(BF16)


PER_STEP = 2


def each_pair(visit):
    def step(index, carry):
        line = index // (N_PAIR // PER_STEP)
        first = lax.rem(index, N_PAIR // PER_STEP) * PER_STEP
        rows = pl.ds(pl.multiple_of(line * LINE, LINE), LINE)
        for offset in range(PER_STEP):
            pair = first + offset
            lanes = pl.ds(pl.multiple_of(pair * PAIR, PAIR), PAIR)
            visit(rows, lanes, line * N_PAIR + pair, pair)
        return carry

    lax.fori_loop(0, 2 * N_PAIR // PER_STEP, step, 0)


def row_forward_kernel(
    keep_ref, x_ref, w_ref, mid_ref, qkv_ref, left_ref,
    mix_s, mid_s, qkv_s, left_s, w_s, w_sem, mid_sem, qkv_sem, left_sem,
):
    weights = copies_of(w_ref, w_s, w_sem, 4)
    start_all(weights)
    saved = copies_of(qkv_s, qkv_ref, qkv_sem, 3)
    lefts = copies_of(left_s, left_ref, left_sem, 2)
    for rr in range(2):
        u = x_ref[:, rr].astype(F32).reshape(LINE, D)
        left_s[0, rr * LINE : (rr + 1) * LINE, :] = (u * inverse_rms(u)).astype(BF16)
    project(left_s[0], qkv_s, w_s, weights)
    lefts[0].start()
    start_all(saved)

    def visit(rows, lanes, at, pair):
        probs = softmax(qkv_s[0, rows, lanes], qkv_s[1, rows, lanes]).astype(BF16)
        mixed = pick_halves(dot(probs, qkv_s[2, rows, lanes]))
        left_s[1, rows, lanes] = (mixed * gain_row(keep_ref, 0, pair * 2, 2)).astype(BF16)

    each_pair(visit)
    lefts[1].start()
    weights[3].wait()
    added = dot(left_s[1], w_s[3])
    for rr in range(2):
        u = x_ref[:, rr].astype(F32).reshape(LINE, D)
        mid = (u + added[rr * LINE : (rr + 1) * LINE]).reshape(16, 2, 8, D)
        for cc in range(2):
            for group in range(4):
                piece = mid[:, cc, :, group * 128 : (group + 1) * 128].reshape(128, 128)
                mix_s[pl.ds(slot(cc, group, rr), 128, stride=16), :] = piece
    sends = []
    for part in range(4):
        rows = slice(part * 32, (part + 1) * 32)
        mid_s[rows] = mix_s[part * 512 : (part + 1) * 512, :].reshape(32, 16, 128).astype(BF16)
        sends.append(pltpu.make_async_copy(mid_s.at[rows], mid_ref.at[rows], mid_sem.at[part]))
        sends[-1].start()
    wait_all(saved + lefts + sends)


def row_prepare_kernel(qkv_ref, left_ref, probs_ref, turned_ref):
    def visit(rows, lanes, at, pair):
        probs_ref[at] = softmax(qkv_ref[0, rows, lanes], qkv_ref[1, rows, lanes])

    each_pair(visit)
    for which in range(2):
        turned_ref[which] = left_ref[which].T


def attention_backward(rows, lanes, qkv, da_ref, probs, right_ref):
    q_pair, k_pair, v_pair = (qkv[i, rows, lanes] for i in range(3))
    da_pair = da_ref[rows, lanes]
    low = probs.astype(BF16)
    grad_probs = dot_nt(stack_halves(da_pair), v_pair)
    total = jnp.sum(probs * grad_probs, axis=-1, keepdims=True)
    grads = (probs * (grad_probs - total)).astype(BF16)
    right_ref[0, rows, lanes] = (pick_halves(dot(grads, k_pair)) * SCALE).astype(BF16)
    right_ref[1, rows, lanes] = pick_halves(dot(turn_halves(grads), q_pair)).astype(BF16)
    right_ref[2, rows, lanes] = pick_halves(dot(turn_halves(low), da_pair)).astype(BF16)
    return low


def input_gradient(u, right_ref, w_s, rows):
    inv = inverse_rms(u)
    dn = (
        dot_nt(right_ref[0, rows, :], w_s[0])
        + dot_nt(right_ref[1, rows, :], w_s[1])
        + dot_nt(right_ref[2, rows, :], w_s[2])
    )
    mean = jnp.mean(dn * u, axis=-1, keepdims=True)
    return right_ref[3, rows, :].astype(F32) + inv * dn - u * (inv * inv * inv * mean)


def weight_gradients(side, turned, right_ref, target):
    for j in range(2):
        which = side * 2 + j
        target[j] = dot(turned[which // 3], right_ref[which]).astype(BF16)


def row_backward_kernel(
    where_ref, keep_heads_ref, g_ref, qkv_ref, turned_ref, probs_ref, w_ref,
    keep_ref, send_ref, right_ref,
    mix_s, da_s, wo_s, qkv_s, turned_s, probs_s, keep_s, send_s, right_s,
    wo_sem, qkv_sem, turned_sem, probs_sem, half_sem, right_sem,
):
    weight = pltpu.make_async_copy(w_ref.at[3], wo_s, wo_sem)
    weight.start()
    saved = copies_of(qkv_ref, qkv_s, qkv_sem, 3)
    start_all(saved)
    probs = [
        pltpu.make_async_copy(
            probs_ref.at[i * 2 : (i + 1) * 2], probs_s.at[i * 2 : (i + 1) * 2], probs_sem.at[i]
        )
        for i in range(4)
    ]
    start_all(probs)
    turned = copies_of(turned_ref, turned_s, turned_sem, 2)
    start_all(turned)
    mix_s[...] = g_ref[...].astype(F32).reshape(N_DEV * 16, 128)
    for rr in range(2):
        for group in range(4):
            sides = [
                mix_s[pl.ds(slot(cc, group, rr), 128, stride=16), :].reshape(16, 8, 128)
                for cc in range(2)
            ]
            right_s[3, rr * LINE : (rr + 1) * LINE, group * 128 : (group + 1) * 128] = (
                jnp.stack(sides, axis=1).reshape(LINE, 128).astype(BF16)
            )
    weight.wait()
    gain = gain_row(keep_heads_ref, 0, 0, HEADS)
    da_s[...] = (dot_nt(right_s[3], wo_s[...]) * gain).astype(BF16)
    wait_all(saved + probs)

    def visit(rows, lanes, at, pair):
        attention_backward(rows, lanes, qkv_s, da_s, probs_s[at], right_s)

    each_pair(visit)
    rights = copies_of(right_s, right_ref, right_sem, 4)
    start_all(rights)
    wait_all(turned)
    core = where_ref[4]
    weight_gradients(1 - core, turned_s, right_s, send_s)
    sent = pltpu.make_async_copy(send_s, send_ref, half_sem.at[0])
    sent.start()
    weight_gradients(core, turned_s, right_s, keep_s)
    kept = pltpu.make_async_copy(keep_s, keep_ref, half_sem.at[1])
    kept.start()
    wait_all(rights + [sent, kept])


def row_input_gradient_kernel(where_ref, x_ref, right_ref, w_ref, *refs):
    outs, w_s, sems, gin_s = refs[:4], refs[4], refs[5], refs[6]
    copies = copies_of(w_ref, w_s, sems, 3)
    start_all(copies)
    wait_all(copies)
    for rr in range(2):
        rows = slice(rr * LINE, (rr + 1) * LINE)
        u = x_ref[:, rr].astype(F32).reshape(LINE, D)
        grad_in = input_gradient(u, right_ref, w_s, rows)
        gin_s[:, :, :, rr] = grad_in.astype(BF16).reshape(2, 4, 2, 16, D)
    for shift in range(4):
        outs[shift][...] = gin_s[:, lax.rem(where_ref[3] + shift, 4)]


def col_kernel(where_ref, keep_heads_ref, m_ref, w_ref, *refs):
    parts, got_ref, refs = refs[:4], refs[4], refs[5:]
    gmid_ref, left_ref, right_ref, u_ref = refs[:4]
    mix_s, u_s, ulow_s, left_s, right_s, qkv_s, da_s, w_s = refs[4:12]
    w_sem, left_sem, right_sem, u_sem = refs[12:]
    mine = where_ref[1]
    weights = copies_of(w_ref, w_s, w_sem, 4)
    for i in (3, 0, 1, 2):
        weights[i].start()
    lefts = copies_of(left_s, left_ref, left_sem, 2)
    rights = copies_of(right_s, right_ref, right_sem, 4)
    for shift in range(4):
        source = lax.rem(where_ref[0] + (4 - shift), 4) * 2
        for grid_row, piece in ((source + mine, parts[shift].at[mine]), (source + (1 - mine), got_ref.at[shift])):
            for cc in range(2):
                for rr in range(2):
                    at = pl.multiple_of(grid_row * 16 + (cc * LINE + rr * 128), 16)
                    right_s[3, pl.ds(at, 16), :] = piece[cc, rr * 16 : (rr + 1) * 16, :]
    rights[3].start()
    weights[3].wait()
    gain = gain_row(keep_heads_ref, 1, 0, HEADS)
    da_s[...] = (dot_nt(right_s[3], w_s[3]) * gain).astype(BF16)
    mix_s[...] = m_ref[...].astype(F32).reshape(N_DEV * 16, 128)
    for cc in range(2):
        for rr in range(2):
            base = cc * LINE + rr * 128
            for group in range(4):
                for grid_row in range(N_ROW):
                    start = base + grid_row * 16
                    u_s[start : start + 16, group * 128 : (group + 1) * 128] = mix_s[
                        pl.ds(grid_row * 16 + slot(cc, group, rr), 16, stride=128), :
                    ]
    u = u_s[...]
    ulow_s[...] = u.astype(BF16)
    kept_u = pltpu.make_async_copy(ulow_s, u_ref, u_sem)
    kept_u.start()
    left_s[0] = (u * inverse_rms(u)).astype(BF16)
    lefts[0].start()
    project(left_s[0], qkv_s, w_s, weights)

    def visit(rows, lanes, at, pair):
        probs = softmax(qkv_s[0, rows, lanes], qkv_s[1, rows, lanes])
        low = attention_backward(rows, lanes, qkv_s, da_s, probs, right_s)
        mixed = pick_halves(dot(low, qkv_s[2, rows, lanes]))
        left_s[1, rows, lanes] = (mixed * gain_row(keep_heads_ref, 1, pair * 2, 2)).astype(BF16)

    each_pair(visit)
    lefts[1].start()
    start_all(rights[:3])
    for cc in range(2):
        rows = slice(cc * LINE, (cc + 1) * LINE)
        grad_in = input_gradient(u_s[rows, :], right_s, w_s, rows)
        for rr in range(2):
            for group in range(4):
                for grid_row in range(N_ROW):
                    start = rr * 128 + grid_row * 16
                    mix_s[pl.ds(grid_row * 16 + slot(cc, group, rr), 16, stride=128), :] = grad_in[
                        start : start + 16, group * 128 : (group + 1) * 128
                    ]
    gmid_ref[...] = mix_s[...].reshape(N_DEV, 16, 128).astype(BF16)
    wait_all(lefts + rights + [kept_u])


def col_output_kernel(where_ref, left_ref, right_ref, u_ref, w_ref, *refs):
    keep_ref, send_ref, outs = refs[0], refs[1], refs[2:6]
    turned_s, out_s, wo_s, sem = refs[6:]
    core = where_ref[4]
    copy = pltpu.make_async_copy(w_ref.at[3], wo_s, sem)
    copy.start()
    for which in range(2):
        turned_s[which] = left_ref[which].T
    weight_gradients(1 - core, turned_s, right_ref, send_ref)
    weight_gradients(core, turned_s, right_ref, keep_ref)
    copy.wait()
    out_s[...] = (u_ref[...].astype(F32) + dot(left_ref[1], wo_s[...])).astype(BF16)
    for shift in range(4):
        for low in range(2):
            start = lax.rem(where_ref[0] + shift, 4) * 32 + low * 16
            for cc in range(2):
                for rr in range(2):
                    at = pl.multiple_of(start + (cc * LINE + rr * 128), 16)
                    outs[shift][low, cc, rr * 16 : (rr + 1) * 16, :] = out_s[pl.ds(at, 16), :]


def tile_to_lines_kernel(where_ref, tile_ref, *refs):
    outs, mix_s = refs[:4], refs[4]
    tile = tile_ref[...].astype(F32).reshape(TOK, D)
    for group in range(4):
        lanes = slice(group * 128, (group + 1) * 128)
        mix_s[group] = tile[:, lanes]
        for shift in range(4):
            for low in range(2):
                peer = lax.rem(where_ref[0] + shift, 4) * 2 + low
                for cc in range(2):
                    for rr in range(2):
                        piece = mix_s[group, pl.ds(peer + (rr * 16 + cc * 8), 16, stride=32), :]
                        outs[shift][low, cc, rr * 16 : (rr + 1) * 16, lanes] = piece.astype(BF16)


def pass_low_kernel(where_ref, *refs):
    parts, pass_ref = refs[:4], refs[4]
    for shift in range(4):
        pass_ref[shift] = parts[shift][1 - where_ref[1]]


def lines_to_tile_kernel(where_ref, *refs):
    parts, got_ref, tile_ref, mix_s = refs[:4], refs[4], refs[5], refs[6]
    mine = where_ref[1]
    for group in range(4):
        lanes = slice(group * 128, (group + 1) * 128)
        for shift in range(4):
            source = lax.rem(where_ref[0] + (4 - shift), 4) * 2
            for peer, piece in ((source + mine, parts[shift].at[mine]), (source + (1 - mine), got_ref.at[shift])):
                for cc in range(2):
                    for rr in range(2):
                        value = piece[cc, rr * 16 : (rr + 1) * 16, lanes].astype(F32)
                        mix_s[group, pl.ds(peer + (rr * 16 + cc * 8), 16, stride=32), :] = value
        tile_ref[:, :, lanes] = mix_s[group].astype(BF16).reshape(32, 16, 128)


def pass_high_kernel(where_ref, *refs):
    parts, pass_ref = refs[:4], refs[4]
    for shift in range(4):
        pass_ref[shift] = parts[shift][1 - where_ref[2]]


def pass_core_kernel(where_ref, *refs):
    parts, got_ref, pass_ref = refs[:4], refs[4], refs[5]
    high, other = where_ref[2], 1 - where_ref[4]
    for shift in range(4):
        pass_ref[0, shift] = parts[shift][high, other]
        pass_ref[1, shift] = got_ref[shift, other]


def join_kernel(where_ref, *refs):
    parts, got_ref, passed_ref, tile_ref = refs[:4], refs[4], refs[5], refs[6]
    high, core = where_ref[2], where_ref[4]
    for shift in range(4):
        source = lax.rem(where_ref[3] + (4 - shift), 4)
        tile_ref[high, source, core] = parts[shift][high, core]
        tile_ref[1 - high, source, core] = got_ref[shift, core]
        tile_ref[high, source, 1 - core] = passed_ref[0, shift]
        tile_ref[1 - high, source, 1 - core] = passed_ref[1, shift]


def pair_sum_kernel(where_ref, keep_ref, got_ref, *refs):
    outs, sum_s = refs[:4], refs[4]
    total = keep_ref[...].astype(F32) + got_ref[...].astype(F32)
    sum_s[...] = total.astype(BF16).reshape(4, 256, D)
    for shift in range(4):
        outs[shift][...] = sum_s[lax.rem(where_ref[3] + shift, 4)]


def merge_kernel(keep_ref, got_ref, *refs):
    quarters, both_ref = refs[:4], refs[4]
    total = keep_ref[...].astype(F32) + got_ref[...].astype(F32)
    rows = total.astype(BF16).reshape(64, 16, D)
    quarter = quarters[0][...].astype(F32)
    for i in range(1, 4):
        quarter = quarter + quarters[i][...].astype(F32)
    quarter = quarter.astype(BF16).reshape(16, 16, D)
    for group in range(4):
        lanes = slice(group * 128, (group + 1) * 128)
        both_ref[:, group * 16 : (group + 1) * 16, :] = rows[:, :, lanes]
        for block in range(16):
            both_ref[block * 4 + group, 64:80, :] = quarter[block, :, lanes]


def chip_sum(parts_ref, rows, first, step):
    total = parts_ref[first, rows, :].astype(F32)
    for chip in range(first + step, 64, step):
        total = total + parts_ref[chip, rows, :].astype(F32)
    return total.astype(BF16)


def spread_kernel(both_ref, spread_ref):
    row_sum = chip_sum(both_ref, slice(0, 64), 0, 1)
    spread_ref[:, 0:64, :] = jnp.broadcast_to(row_sum[None], (64, 64, 128))
    for quarter in range(4):
        part = chip_sum(both_ref, slice(64, 80), quarter, 4)
        first = 64 + quarter * 16
        spread_ref[:, first : first + 16, :] = jnp.broadcast_to(part[None], (64, 16, 128))


def widen_kernel(where_ref, chunks_ref, *refs):
    row_ref, col_ref = refs[-2:]
    for group in range(4):
        lanes = slice(group * 128, (group + 1) * 128)
        piece = chunks_ref[:, group * 16 : (group + 1) * 16, :].astype(F32)
        row_ref[0, :, lanes] = piece.reshape(256, 128)
        for quarter in range(4):
            for block in range(4):
                first = 64 + quarter * 16
                col_ref[0, quarter, block * 16 : (block + 1) * 16, lanes] = chunks_ref[
                    block * 4 + group, first : first + 16, :
                ].astype(F32)


MIB = 1 << 20
SMEM = pl.BlockSpec(memory_space=pltpu.SMEM)
VMEM = pl.BlockSpec(memory_space=pltpu.VMEM)
HBM = pl.BlockSpec(memory_space=pltpu.HBM)


GRANT = 60 * 1024 * 1024
SPACE = {"s": SMEM, "v": VMEM, "h": HBM}


def call(kernel, ins, out_kinds, outs, scratch, flops, moved):
    spaces = tuple(SPACE[kind] for kind in out_kinds)
    return pl.pallas_call(
        kernel,
        in_specs=[SPACE[kind] for kind in ins],
        out_specs=spaces if isinstance(outs, tuple) else spaces[0],
        out_shape=outs,
        scratch_shapes=scratch,
        compiler_params=pltpu.CompilerParams(vmem_limit_bytes=GRANT),
        cost_estimate=pl.CostEstimate(flops=flops, bytes_accessed=moved, transcendentals=0),
    )


def shape(*dims, dtype=BF16):
    return jax.ShapeDtypeStruct(dims, dtype)


MATMUL = 2 * TOK * D * D
ATTEND = 2 * 16 * LINE * LINE * HEAD
MIX = pltpu.VMEM((N_DEV * 16, 128), F32)
MIX_TILE = pltpu.VMEM((4, TOK, 128), F32)
DMA = pltpu.SemaphoreType.DMA
WEIGHTS = [pltpu.VMEM((4, D, D), BF16), DMA((4,))]
WEIGHT = [pltpu.VMEM((D, D), BF16), DMA]
PIECE = shape(2, 2, 32, D)
PASS = shape(4, 2, 32, D)
QUARTER = shape(256, D)
HALF = shape(2, D, D)
HALF_S = pltpu.VMEM((2, D, D), BF16)


def token_scratch(*lead, dtype=BF16):
    return pltpu.VMEM((*lead, TOK, D), dtype)


row_forward = call(
    row_forward_kernel,
    "svh",
    "hhh",
    (shape(N_DEV, 16, 128), shape(3, TOK, D), shape(2, TOK, D)),
    [
        MIX, pltpu.VMEM((N_DEV, 16, 128), BF16), token_scratch(3), token_scratch(2), *WEIGHTS,
        DMA((4,)), DMA((3,)), DMA((2,)),
    ],
    4 * MATMUL + 2 * ATTEND,
    6 * MIB,
)
row_prepare = call(
    row_prepare_kernel,
    "vv",
    "vv",
    (shape(8, TOK, LINE, dtype=F32), shape(2, D, TOK)),
    [],
    ATTEND,
    8 * MIB,
)
row_backward = call(
    row_backward_kernel,
    "ssvhhhh",
    "hhh",
    (HALF, HALF, shape(4, TOK, D)),
    [
        MIX, token_scratch(), pltpu.VMEM((D, D), BF16), token_scratch(3),
        pltpu.VMEM((2, D, TOK), BF16), pltpu.VMEM((8, TOK, LINE), F32), HALF_S, HALF_S,
        token_scratch(4), DMA, DMA((3,)), DMA((2,)), DMA((4,)), DMA((2,)), DMA((4,)),
    ],
    5 * MATMUL + 5 * ATTEND,
    12 * MIB,
)
row_input_gradient = call(
    row_input_gradient_kernel,
    "svvh",
    "v" * 4,
    (shape(2, 2, 2, 16, D),) * 4,
    [*WEIGHTS, pltpu.VMEM((2, 4, 2, 2, 16, D), BF16)],
    3 * MATMUL,
    5 * MIB,
)
col_grad = call(
    col_kernel,
    "ssvh" + "v" * 5,
    "vhhh",
    (shape(N_DEV, 16, 128), shape(2, TOK, D), shape(4, TOK, D), shape(TOK, D)),
    [
        MIX, token_scratch(dtype=F32), token_scratch(), token_scratch(2), token_scratch(4),
        token_scratch(3), token_scratch(), *WEIGHTS, DMA((2,)), DMA((4,)), DMA,
    ],
    8 * MATMUL + 6 * ATTEND,
    8 * MIB,
)
col_output = call(
    col_output_kernel,
    "svvvh",
    "v" * 6,
    (HALF, HALF) + (PIECE,) * 4,
    [pltpu.VMEM((2, D, TOK), BF16), token_scratch(), *WEIGHT],
    5 * MATMUL,
    7 * MIB,
)
tile_to_lines = call(tile_to_lines_kernel, "sv", "v" * 4, (PIECE,) * 4, [MIX_TILE], 0, MIB)
pass_low = call(pass_low_kernel, "s" + "v" * 4, "v", PASS, [], 0, MIB)
lines_to_tile = call(lines_to_tile_kernel, "s" + "v" * 5, "v", shape(32, 16, D), [MIX_TILE], 0, MIB)
CHIP_PASS = shape(4, 2, 2, 16, D)
CORE_PASS = shape(2, 4, 2, 16, D)
pass_high = call(pass_high_kernel, "s" + "v" * 4, "v", CHIP_PASS, [], 0, MIB)
pass_core = call(pass_core_kernel, "s" + "v" * 5, "v", CORE_PASS, [], 0, MIB)
join = call(join_kernel, "s" + "v" * 6, "v", shape(2, 4, 2, 2, 16, D), [], 0, MIB)
pair_sum = call(
    pair_sum_kernel, "svv", "v" * 4, (QUARTER,) * 4, [pltpu.VMEM((4, 256, D), BF16)], 0, 3 * MIB,
)
merge = call(merge_kernel, "v" * 6, "v", shape(64, 80, 128), [], 0, 4 * MIB)
spread = call(spread_kernel, "v", "v", shape(64, 128, 128), [], 0, 3 * MIB)


def widen(where, chunks, side, *before):
    half = lambda ref: ref[4] if side == 0 else 1 - ref[4]
    outs = (
        pl.BlockSpec((1, 256, D), lambda i, ref: (half(ref), i, 0)),
        pl.BlockSpec((1, 4, 64, D), lambda i, ref: (half(ref), 0, i, 0)),
    )
    return pl.pallas_call(
        widen_kernel,
        grid_spec=pltpu.PrefetchScalarGridSpec(
            num_scalar_prefetch=1,
            grid=(4,),
            in_specs=[pl.BlockSpec((16, 128, 128), lambda i, ref: (i, 0, 0))]
            + [pl.BlockSpec(memory_space=pl.ANY)] * len(before),
            out_specs=outs,
        ),
        out_shape=(shape(2, 1024, D, dtype=F32), shape(2, 4, 256, D, dtype=F32)),
        input_output_aliases={2: 0, 3: 1} if before else {},
        name="widen",
        compiler_params=pltpu.CompilerParams(vmem_limit_bytes=GRANT),
        cost_estimate=pl.CostEstimate(flops=0, bytes_accessed=6 * MIB, transcendentals=0),
    )(where, chunks, *before)


def exchange(values, axes):
    return lax.all_to_all(values, axes, split_axis=0, concat_axis=0, tiled=True)


def shifted(pieces, axes):
    n = len(pieces)
    return [pieces[0]] + [
        lax.ppermute(pieces[k], axes, [(i, (i + k) % n) for i in range(n)]) for k in range(1, n)
    ]


def swap(value, axis):
    return lax.ppermute(value, axis, [(0, 1), (1, 0)])


def layer(latents, cotangent, w_row, w_col, keep_heads):
    where = jnp.stack([lax.axis_index(name) for name in AXES]).astype(jnp.int32)
    rows_in = exchange(latents.reshape(16, 2, 16, D), COL)
    grad_pieces = tile_to_lines(where, cotangent)
    grad_parts = shifted(grad_pieces, "y")
    grad_pass = pass_low(where, *grad_parts)
    grad_pass = swap(grad_pass, "zl")
    mid_send, qkv_row, left_row = row_forward(keep_heads, rows_in, w_row)
    mid_lines = exchange(mid_send, BOTH)
    probs_row, turned_row = row_prepare(qkv_row, left_row)
    grad_send, left_col, right_col, u_col = col_grad(
        where, keep_heads, mid_lines, w_col, *grad_parts, grad_pass
    )
    grad_rows = exchange(grad_send, BOTH)
    keep_col, send_col, *out_pieces = col_output(where, left_col, right_col, u_col, w_col)
    got_col = swap(send_col, "c")
    quarters = pair_sum(where, keep_col, got_col)
    quarters = shifted(quarters, "x")
    keep_row, send_row, right_row = row_backward(
        where, keep_heads, grad_rows, qkv_row, turned_row, probs_row, w_row
    )
    got_row = swap(send_row, "c")
    merged = merge(keep_row, got_row, *quarters)
    both = exchange(merged, CHIPS)
    totals = spread(both)
    chunks = exchange(totals, CHIPS)
    gin_pieces = row_input_gradient(where, rows_in, right_row, w_row)
    gin_parts = shifted(gin_pieces, "x")
    gin_pass = pass_high(where, *gin_parts)
    gin_got = swap(gin_pass, "zh")
    gin_core = pass_core(where, *gin_parts, gin_got)
    gin_core = swap(gin_core, "c")
    grad_latents = join(where, *gin_parts, gin_got, gin_core).reshape(32, 16, D)
    out_parts = shifted(out_pieces, "y")
    out_pass = pass_low(where, *out_parts)
    out_pass = swap(out_pass, "zl")
    output = lines_to_tile(where, *out_parts, out_pass)
    other = swap(chunks, "c")
    halves_done = widen(where, chunks, 0)
    grad_row, grad_col = widen(where, other, 1, *halves_done)
    return (output, grad_latents, grad_row.reshape(4, D, D), grad_col.reshape(4, D, D))


def solution(mesh):
    fine = Mesh(mesh.devices.reshape(4, 2, 2, 4, 2), AXES)
    tile = P(ROW, COL, None)
    return jax.shard_map(
        layer,
        mesh=fine,
        in_specs=(tile, tile, P(), P(), P()),
        out_specs=(tile, tile, P(), P()),
        check_vma=False,
    )
```

```python
import functools

import jax
import jax.numpy as jnp
from jax import lax
from jax.experimental import pallas as pl
from jax.experimental.pallas import tpu as pltpu
from jax.sharding import Mesh, PartitionSpec as P


HEADS = 8
HEAD = 64
D = 512
PAIR = 128
N_PAIR = D // PAIR
LINE = 256
TOK = 512
N_ROW = 8
N_COL = 16
N_DEV = N_ROW * N_COL
EPSILON = 1e-06
SCALE = HEAD ** (-0.5)

F32 = jnp.float32
BF16 = jnp.bfloat16

AXES = ("y", "zl", "zh", "x", "c")
ROW = ("y", "zl")
COL = ("zh", "x", "c")
BOTH = COL + ROW
CHIPS = ("y", "zl", "zh", "x")


def dot(left, right):
    return lax.dot_general(left, right, (((1,), (0,)), ((), ())), preferred_element_type=F32)


def dot_nt(left, right):
    return lax.dot_general(left, right, (((1,), (1,)), ((), ())), preferred_element_type=F32)


def stack_halves(value):
    lane = lax.broadcasted_iota(jnp.int32, value.shape, 1)
    zero = jnp.zeros_like(value)
    low, high = jnp.where(lane < HEAD, value, zero), jnp.where(lane >= HEAD, value, zero)
    return jnp.concatenate([low, high], axis=0)


def pick_halves(value):
    low, high = value[:LINE], value[LINE:]
    lane = lax.broadcasted_iota(jnp.int32, low.shape, 1)
    return jnp.where(lane < HEAD, low, high)


def turn_halves(value):
    return jnp.concatenate([value[:LINE].T, value[LINE:].T], axis=0)


def gain_row(keep_ref, block, first, count):
    head = lax.broadcasted_iota(jnp.int32, (1, count * HEAD), 1) // HEAD
    gain = jnp.zeros((1, count * HEAD), F32)
    for i in range(count):
        gain = jnp.where(head == i, keep_ref[block, first + i].astype(F32), gain)
    return gain


def inverse_rms(values_f):
    return lax.rsqrt(jnp.mean(values_f * values_f, axis=-1, keepdims=True) + EPSILON)


def softmax(q_pair, k_pair):
    scores = dot_nt(stack_halves(q_pair), k_pair)
    peak = jnp.max(scores, axis=-1, keepdims=True)
    grown = jnp.exp(scores - peak)
    return grown * (1.0 / jnp.sum(grown, axis=-1, keepdims=True))


def slot(col_local, group, row_local):
    return col_local * 8 + group * 2 + row_local


def copies_of(source, target, sems, count):
    return [pltpu.make_async_copy(source.at[i], target.at[i], sems.at[i]) for i in range(count)]


def start_all(copies):
    for copy in copies:
        copy.start()


def wait_all(copies):
    for copy in copies:
        copy.wait()


def project(normed, qkv_ref, w_s, copies):
    copies[0].wait()
    qkv_ref[0] = (dot(normed, w_s[0]).astype(BF16).astype(F32) * SCALE).astype(BF16)
    copies[1].wait()
    qkv_ref[1] = dot(normed, w_s[1]).astype(BF16)
    copies[2].wait()
    qkv_ref[2] = dot(normed, w_s[2]).astype(BF16)


PER_STEP = 2


def each_pair(visit):
    def step(index, carry):
        line = index // (N_PAIR // PER_STEP)
        first = lax.rem(index, N_PAIR // PER_STEP) * PER_STEP
        rows = pl.ds(pl.multiple_of(line * LINE, LINE), LINE)
        for offset in range(PER_STEP):
            pair = first + offset
            lanes = pl.ds(pl.multiple_of(pair * PAIR, PAIR), PAIR)
            visit(rows, lanes, line * N_PAIR + pair, pair)
        return carry

    lax.fori_loop(0, 2 * N_PAIR // PER_STEP, step, 0)


def row_forward_kernel(
    keep_ref, x_ref, w_ref, mid_ref, qkv_ref, left_ref,
    mix_s, mid_s, qkv_s, left_s, w_s, w_sem, mid_sem, qkv_sem, left_sem,
):
    weights = copies_of(w_ref, w_s, w_sem, 4)
    start_all(weights)
    saved = copies_of(qkv_s, qkv_ref, qkv_sem, 3)
    lefts = copies_of(left_s, left_ref, left_sem, 2)
    for rr in range(2):
        u = x_ref[:, rr].astype(F32).reshape(LINE, D)
        left_s[0, rr * LINE : (rr + 1) * LINE, :] = (u * inverse_rms(u)).astype(BF16)
    project(left_s[0], qkv_s, w_s, weights)
    lefts[0].start()
    start_all(saved)

    def visit(rows, lanes, at, pair):
        probs = softmax(qkv_s[0, rows, lanes], qkv_s[1, rows, lanes]).astype(BF16)
        mixed = pick_halves(dot(probs, qkv_s[2, rows, lanes]))
        left_s[1, rows, lanes] = (mixed * gain_row(keep_ref, 0, pair * 2, 2)).astype(BF16)

    each_pair(visit)
    lefts[1].start()
    weights[3].wait()
    added = dot(left_s[1], w_s[3])
    for rr in range(2):
        u = x_ref[:, rr].astype(F32).reshape(LINE, D)
        mid = (u + added[rr * LINE : (rr + 1) * LINE]).reshape(16, 2, 8, D)
        for cc in range(2):
            for group in range(4):
                piece = mid[:, cc, :, group * 128 : (group + 1) * 128].reshape(128, 128)
                mix_s[pl.ds(slot(cc, group, rr), 128, stride=16), :] = piece
    sends = []
    for part in range(4):
        rows = slice(part * 32, (part + 1) * 32)
        mid_s[rows] = mix_s[part * 512 : (part + 1) * 512, :].reshape(32, 16, 128).astype(BF16)
        sends.append(pltpu.make_async_copy(mid_s.at[rows], mid_ref.at[rows], mid_sem.at[part]))
        sends[-1].start()
    wait_all(saved + lefts + sends)


def row_prepare_kernel(qkv_ref, left_ref, probs_ref, turned_ref):
    def visit(rows, lanes, at, pair):
        probs = softmax(qkv_ref[0, rows, lanes], qkv_ref[1, rows, lanes])
        probs_ref[at] = probs.astype(BF16)

    each_pair(visit)
    for which in range(2):
        turned_ref[which] = left_ref[which].T


def attention_backward(rows, lanes, qkv, da_ref, probs, right_ref):
    q_pair, k_pair, v_pair = (qkv[i, rows, lanes] for i in range(3))
    da_pair = da_ref[rows, lanes]
    low = probs.astype(BF16)
    probs = probs.astype(F32)
    grad_probs = dot_nt(stack_halves(da_pair), v_pair)
    total = jnp.sum(probs * grad_probs, axis=-1, keepdims=True)
    grads = (probs * (grad_probs - total)).astype(BF16)
    right_ref[0, rows, lanes] = (pick_halves(dot(grads, k_pair)) * SCALE).astype(BF16)
    right_ref[1, rows, lanes] = pick_halves(dot(turn_halves(grads), q_pair)).astype(BF16)
    right_ref[2, rows, lanes] = pick_halves(dot(turn_halves(low), da_pair)).astype(BF16)
    return low


def input_gradient(u, right_ref, w_s, rows):
    inv = inverse_rms(u)
    dn = (
        dot_nt(right_ref[0, rows, :], w_s[0])
        + dot_nt(right_ref[1, rows, :], w_s[1])
        + dot_nt(right_ref[2, rows, :], w_s[2])
    )
    mean = jnp.mean(dn * u, axis=-1, keepdims=True)
    return right_ref[3, rows, :].astype(F32) + inv * dn - u * (inv * inv * inv * mean)


def weight_gradients(side, turned, right_ref, target):
    for j in range(2):
        which = side * 2 + j
        target[j] = dot(turned[which // 3], right_ref[which]).astype(BF16)


def row_backward_kernel(
    where_ref, keep_heads_ref, g_ref, qkv_ref, turned_ref, probs_ref, w_ref,
    keep_ref, send_ref, right_ref,
    mix_s, da_s, wo_s, qkv_s, turned_s, probs_s, keep_s, send_s, right_s,
    wo_sem, qkv_sem, turned_sem, probs_sem, half_sem, right_sem,
):
    weight = pltpu.make_async_copy(w_ref.at[3], wo_s, wo_sem)
    weight.start()
    saved = copies_of(qkv_ref, qkv_s, qkv_sem, 3)
    start_all(saved)
    probs = [
        pltpu.make_async_copy(
            probs_ref.at[i * 2 : (i + 1) * 2], probs_s.at[i * 2 : (i + 1) * 2], probs_sem.at[i]
        )
        for i in range(4)
    ]
    start_all(probs)
    turned = copies_of(turned_ref, turned_s, turned_sem, 2)
    start_all(turned)
    mix_s[...] = g_ref[...].astype(F32).reshape(N_DEV * 16, 128)
    for rr in range(2):
        for group in range(4):
            sides = [
                mix_s[pl.ds(slot(cc, group, rr), 128, stride=16), :].reshape(16, 8, 128)
                for cc in range(2)
            ]
            right_s[3, rr * LINE : (rr + 1) * LINE, group * 128 : (group + 1) * 128] = (
                jnp.stack(sides, axis=1).reshape(LINE, 128).astype(BF16)
            )
    weight.wait()
    gain = gain_row(keep_heads_ref, 0, 0, HEADS)
    da_s[...] = (dot_nt(right_s[3], wo_s[...]) * gain).astype(BF16)
    wait_all(saved + probs)

    def visit(rows, lanes, at, pair):
        attention_backward(rows, lanes, qkv_s, da_s, probs_s[at], right_s)

    each_pair(visit)
    rights = copies_of(right_s, right_ref, right_sem, 4)
    start_all(rights)
    wait_all(turned)
    core = where_ref[4]
    weight_gradients(1 - core, turned_s, right_s, send_s)
    sent = pltpu.make_async_copy(send_s, send_ref, half_sem.at[0])
    sent.start()
    weight_gradients(core, turned_s, right_s, keep_s)
    kept = pltpu.make_async_copy(keep_s, keep_ref, half_sem.at[1])
    kept.start()
    wait_all(rights + [sent, kept])


def row_input_gradient_kernel(where_ref, x_ref, right_ref, w_ref, *refs):
    outs, w_s, sems, gin_s = refs[:8], refs[8], refs[9], refs[10]
    copies = copies_of(w_ref, w_s, sems, 3)
    start_all(copies)
    wait_all(copies)
    for rr in range(2):
        rows = slice(rr * LINE, (rr + 1) * LINE)
        u = x_ref[:, rr].astype(F32).reshape(LINE, D)
        grad_in = input_gradient(u, right_ref, w_s, rows)
        gin_s[:, :, rr] = grad_in.astype(BF16).reshape(8, 2, 16, D)
    chip = where_ref[2] * 4 + where_ref[3]
    for shift in range(8):
        outs[shift][...] = gin_s[lax.rem(chip + shift, 8)]


def col_kernel(where_ref, keep_heads_ref, m_ref, w_ref, *refs):
    parts, got_ref, refs = refs[:4], refs[4], refs[5:]
    gmid_ref, left_ref, right_ref, u_ref = refs[:4]
    mix_s, u_s, ulow_s, left_s, right_s, qkv_s, da_s, w_s = refs[4:12]
    w_sem, left_sem, right_sem, u_sem = refs[12:]
    mine = where_ref[1]
    weights = copies_of(w_ref, w_s, w_sem, 4)
    for i in (3, 0, 1, 2):
        weights[i].start()
    lefts = copies_of(left_s, left_ref, left_sem, 2)
    rights = copies_of(right_s, right_ref, right_sem, 4)
    mix_s[...] = m_ref[...].astype(F32).reshape(N_DEV * 16, 128)
    for cc in range(2):
        for rr in range(2):
            base = cc * LINE + rr * 128
            for group in range(4):
                for grid_row in range(N_ROW):
                    start = base + grid_row * 16
                    u_s[start : start + 16, group * 128 : (group + 1) * 128] = mix_s[
                        pl.ds(grid_row * 16 + slot(cc, group, rr), 16, stride=128), :
                    ]
    u = u_s[...]
    ulow_s[...] = u.astype(BF16)
    kept_u = pltpu.make_async_copy(ulow_s, u_ref, u_sem)
    kept_u.start()
    left_s[0] = (u * inverse_rms(u)).astype(BF16)
    lefts[0].start()
    for shift in range(4):
        source = lax.rem(where_ref[0] + (4 - shift), 4) * 2
        for grid_row, piece in ((source + mine, parts[shift].at[mine]), (source + (1 - mine), got_ref.at[shift])):
            for cc in range(2):
                for rr in range(2):
                    at = pl.multiple_of(grid_row * 16 + (cc * LINE + rr * 128), 16)
                    right_s[3, pl.ds(at, 16), :] = piece[cc, rr * 16 : (rr + 1) * 16, :]
    rights[3].start()
    weights[3].wait()
    gain = gain_row(keep_heads_ref, 1, 0, HEADS)
    da_s[...] = (dot_nt(right_s[3], w_s[3]) * gain).astype(BF16)
    project(left_s[0], qkv_s, w_s, weights)

    def visit(rows, lanes, at, pair):
        probs = softmax(qkv_s[0, rows, lanes], qkv_s[1, rows, lanes])
        low = attention_backward(rows, lanes, qkv_s, da_s, probs, right_s)
        mixed = pick_halves(dot(low, qkv_s[2, rows, lanes]))
        left_s[1, rows, lanes] = (mixed * gain_row(keep_heads_ref, 1, pair * 2, 2)).astype(BF16)

    each_pair(visit)
    lefts[1].start()
    start_all(rights[:3])
    for cc in range(2):
        rows = slice(cc * LINE, (cc + 1) * LINE)
        grad_in = input_gradient(u_s[rows, :], right_s, w_s, rows)
        for rr in range(2):
            for group in range(4):
                for grid_row in range(N_ROW):
                    start = rr * 128 + grid_row * 16
                    mix_s[pl.ds(grid_row * 16 + slot(cc, group, rr), 16, stride=128), :] = grad_in[
                        start : start + 16, group * 128 : (group + 1) * 128
                    ]
    gmid_ref[...] = mix_s[...].reshape(N_DEV, 16, 128).astype(BF16)
    wait_all(lefts + rights + [kept_u])


def col_output_kernel(where_ref, left_ref, right_ref, u_ref, w_ref, *refs):
    keep_ref, send_ref, outs = refs[0], refs[1], refs[2:10]
    left_s, right_s, ulow_s, wo_s, turned_s, out_s, keep_s, send_s = refs[10:18]
    left_sem, right_sem, one_sem, half_sem = refs[18:]
    lefts = copies_of(left_ref, left_s, left_sem, 2)
    rights = copies_of(right_ref, right_s, right_sem, 4)
    others = [
        pltpu.make_async_copy(w_ref.at[3], wo_s, one_sem.at[0]),
        pltpu.make_async_copy(u_ref, ulow_s, one_sem.at[1]),
    ]
    start_all(lefts + rights + others)
    core = where_ref[4]
    for which in range(2):
        lefts[which].wait()
        turned_s[which] = left_s[which].T
    wait_all(rights)
    weight_gradients(1 - core, turned_s, right_s, send_s)
    sent = pltpu.make_async_copy(send_s, send_ref, half_sem.at[0])
    sent.start()
    weight_gradients(core, turned_s, right_s, keep_s)
    kept = pltpu.make_async_copy(keep_s, keep_ref, half_sem.at[1])
    kept.start()
    wait_all(others)
    out_s[...] = (ulow_s[...].astype(F32) + dot(left_s[1], wo_s[...])).astype(BF16)
    me = where_ref[0] * 2 + where_ref[1]
    for shift in range(8):
        start = lax.rem(me + shift, 8) * 16
        for cc in range(2):
            for rr in range(2):
                at = pl.multiple_of(start + (cc * LINE + rr * 128), 16)
                outs[shift][cc, rr * 16 : (rr + 1) * 16, :] = out_s[pl.ds(at, 16), :]
    wait_all([sent, kept])


def tile_to_lines_kernel(where_ref, tile_ref, *refs):
    outs, mix_s = refs[:4], refs[4]
    tile = tile_ref[...].astype(F32).reshape(TOK, D)
    for group in range(4):
        lanes = slice(group * 128, (group + 1) * 128)
        mix_s[group] = tile[:, lanes]
        for shift in range(4):
            for low in range(2):
                peer = lax.rem(where_ref[0] + shift, 4) * 2 + low
                for cc in range(2):
                    for rr in range(2):
                        piece = mix_s[group, pl.ds(peer + (rr * 16 + cc * 8), 16, stride=32), :]
                        outs[shift][low, cc, rr * 16 : (rr + 1) * 16, lanes] = piece.astype(BF16)


def pass_low_kernel(where_ref, *refs):
    parts, pass_ref = refs[:4], refs[4]
    for shift in range(4):
        pass_ref[shift] = parts[shift][1 - where_ref[1]]


def lines_to_tile_kernel(where_ref, *refs):
    parts, tile_ref, mix_s = refs[:8], refs[8], refs[9]
    me = where_ref[0] * 2 + where_ref[1]
    for group in range(4):
        lanes = slice(group * 128, (group + 1) * 128)
        for shift in range(8):
            peer = lax.rem(me + (8 - shift), 8)
            for cc in range(2):
                for rr in range(2):
                    piece = parts[shift][cc, rr * 16 : (rr + 1) * 16, lanes].astype(F32)
                    mix_s[group, pl.ds(peer + (rr * 16 + cc * 8), 16, stride=32), :] = piece
        tile_ref[:, :, lanes] = mix_s[group].astype(BF16).reshape(32, 16, 128)


def pass_core_kernel(where_ref, *refs):
    parts, pass_ref = refs[:8], refs[8]
    for shift in range(8):
        pass_ref[shift] = parts[shift][1 - where_ref[4]]


def join_kernel(where_ref, *refs):
    parts, passed_ref, tile_ref = refs[:8], refs[8], refs[9]
    chip, core = where_ref[2] * 4 + where_ref[3], where_ref[4]
    for shift in range(8):
        source = lax.rem(chip + (8 - shift), 8)
        tile_ref[source, core] = parts[shift][core]
        tile_ref[source, 1 - core] = passed_ref[shift]


def pair_sum_kernel(where_ref, keep_ref, got_ref, *refs):
    outs, sum_s = refs[:4], refs[4]
    total = keep_ref[...].astype(F32) + got_ref[...].astype(F32)
    sum_s[...] = total.astype(BF16).reshape(4, 256, D)
    for shift in range(4):
        outs[shift][...] = sum_s[lax.rem(where_ref[3] + shift, 4)]


def merge_kernel(keep_ref, got_ref, *refs):
    quarters, both_ref = refs[:4], refs[4]
    total = keep_ref[...].astype(F32) + got_ref[...].astype(F32)
    rows = total.astype(BF16).reshape(64, 16, D)
    quarter = quarters[0][...].astype(F32)
    for i in range(1, 4):
        quarter = quarter + quarters[i][...].astype(F32)
    quarter = quarter.astype(BF16).reshape(16, 16, D)
    for group in range(4):
        lanes = slice(group * 128, (group + 1) * 128)
        both_ref[:, group * 16 : (group + 1) * 16, :] = rows[:, :, lanes]
        for block in range(16):
            both_ref[block * 4 + group, 64:80, :] = quarter[block, :, lanes]


def chip_sum(parts_ref, rows, first, step):
    total = parts_ref[first, rows, :].astype(F32)
    for chip in range(first + step, 64, step):
        total = total + parts_ref[chip, rows, :].astype(F32)
    return total.astype(BF16)


def spread_kernel(both_ref, spread_ref):
    row_sum = chip_sum(both_ref, slice(0, 64), 0, 1)
    spread_ref[:, 0:64, :] = jnp.broadcast_to(row_sum[None], (64, 64, 128))
    for quarter in range(4):
        part = chip_sum(both_ref, slice(64, 80), quarter, 4)
        first = 64 + quarter * 16
        spread_ref[:, first : first + 16, :] = jnp.broadcast_to(part[None], (64, 16, 128))


def widen_kernel(side, where_ref, chunks_ref, *refs):
    row_ref, col_ref, row_s, col_s, row_sem, col_sem = refs[-6:]
    half = where_ref[4] if side == 0 else 1 - where_ref[4]
    copies = []
    for part in range(4):
        chunks = slice(part * 16, (part + 1) * 16)
        for group in range(4):
            lanes = slice(group * 128, (group + 1) * 128)
            piece = chunks_ref[chunks, group * 16 : (group + 1) * 16, :].astype(F32)
            row_s[part, :, lanes] = piece.reshape(256, 128)
        rows = pl.ds(part * 256, 256)
        copies.append(
            pltpu.make_async_copy(row_s.at[part], row_ref.at[half, rows], row_sem.at[part])
        )
        copies[-1].start()
    for quarter in range(4):
        first = 64 + quarter * 16
        for block in range(16):
            for group in range(4):
                col_s[quarter, block * 16 : (block + 1) * 16, group * 128 : (group + 1) * 128] = (
                    chunks_ref[block * 4 + group, first : first + 16, :].astype(F32)
                )
        copies.append(
            pltpu.make_async_copy(col_s.at[quarter], col_ref.at[half, quarter], col_sem.at[quarter])
        )
        copies[-1].start()
    wait_all(copies)


MIB = 1 << 20
SMEM = pl.BlockSpec(memory_space=pltpu.SMEM)
VMEM = pl.BlockSpec(memory_space=pltpu.VMEM)
HBM = pl.BlockSpec(memory_space=pltpu.HBM)


SPACE = {"s": SMEM, "v": VMEM, "h": HBM}


def call(kernel, ins, out_kinds, outs, scratch, flops, moved, grant=16):
    spaces = tuple(SPACE[kind] for kind in out_kinds)
    return pl.pallas_call(
        kernel,
        in_specs=[SPACE[kind] for kind in ins],
        out_specs=spaces if isinstance(outs, tuple) else spaces[0],
        out_shape=outs,
        scratch_shapes=scratch,
        compiler_params=pltpu.CompilerParams(vmem_limit_bytes=grant * MIB),
        cost_estimate=pl.CostEstimate(flops=flops, bytes_accessed=moved, transcendentals=0),
    )


def shape(*dims, dtype=BF16):
    return jax.ShapeDtypeStruct(dims, dtype)


MATMUL = 2 * TOK * D * D
ATTEND = 2 * 16 * LINE * LINE * HEAD
MIX = pltpu.VMEM((N_DEV * 16, 128), F32)
MIX_TILE = pltpu.VMEM((4, TOK, 128), F32)
DMA = pltpu.SemaphoreType.DMA
WEIGHTS = [pltpu.VMEM((4, D, D), BF16), DMA((4,))]
WEIGHT = [pltpu.VMEM((D, D), BF16), DMA]
LINES = shape(2, 32, D)
PIECE = shape(2, 2, 32, D)
PASS = shape(4, 2, 32, D)
QUARTER = shape(256, D)
HALF = shape(2, D, D)
HALF_S = pltpu.VMEM((2, D, D), BF16)


def token_scratch(*lead, dtype=BF16):
    return pltpu.VMEM((*lead, TOK, D), dtype)


row_forward = call(
    row_forward_kernel,
    "svh",
    "hhh",
    (shape(N_DEV, 16, 128), shape(3, TOK, D), shape(2, TOK, D)),
    [
        MIX, pltpu.VMEM((N_DEV, 16, 128), BF16), token_scratch(3), token_scratch(2), *WEIGHTS,
        DMA((4,)), DMA((3,)), DMA((2,)),
    ],
    4 * MATMUL + 2 * ATTEND,
    6 * MIB,
    grant=50,
)
row_prepare = call(
    row_prepare_kernel, "vv", "vv", (shape(8, TOK, LINE), shape(2, D, TOK)), [], ATTEND, 8 * MIB
)
row_backward = call(
    row_backward_kernel,
    "ssvhhhh",
    "hhh",
    (HALF, HALF, shape(4, TOK, D)),
    [
        MIX, token_scratch(), pltpu.VMEM((D, D), BF16), token_scratch(3),
        pltpu.VMEM((2, D, TOK), BF16), pltpu.VMEM((8, TOK, LINE), BF16), HALF_S, HALF_S,
        token_scratch(4), DMA, DMA((3,)), DMA((2,)), DMA((4,)), DMA((2,)), DMA((4,)),
    ],
    5 * MATMUL + 5 * ATTEND,
    12 * MIB,
    grant=50,
)
row_input_gradient = call(
    row_input_gradient_kernel,
    "svvh",
    "v" * 8,
    (shape(2, 2, 16, D),) * 8,
    [*WEIGHTS, pltpu.VMEM((8, 2, 2, 16, D), BF16)],
    3 * MATMUL,
    5 * MIB,
)
col_grad = call(
    col_kernel,
    "ssvh" + "v" * 5,
    "vhhh",
    (shape(N_DEV, 16, 128), shape(2, TOK, D), shape(4, TOK, D), shape(TOK, D)),
    [
        MIX, token_scratch(dtype=F32), token_scratch(), token_scratch(2), token_scratch(4),
        token_scratch(3), token_scratch(), *WEIGHTS, DMA((2,)), DMA((4,)), DMA,
    ],
    8 * MATMUL + 6 * ATTEND,
    8 * MIB,
    grant=48,
)
col_output = call(
    col_output_kernel,
    "shhhh",
    "hh" + "v" * 8,
    (HALF, HALF) + (LINES,) * 8,
    [
        token_scratch(2), token_scratch(4), token_scratch(), pltpu.VMEM((D, D), BF16),
        pltpu.VMEM((2, D, TOK), BF16), token_scratch(), HALF_S, HALF_S,
        DMA((2,)), DMA((4,)), DMA((2,)), DMA((2,)),
    ],
    5 * MATMUL,
    7 * MIB,
    grant=52,
)
tile_to_lines = call(tile_to_lines_kernel, "sv", "v" * 4, (PIECE,) * 4, [MIX_TILE], 0, MIB)
pass_low = call(pass_low_kernel, "s" + "v" * 4, "v", PASS, [], 0, MIB)
lines_to_tile = call(lines_to_tile_kernel, "s" + "v" * 8, "v", shape(32, 16, D), [MIX_TILE], 0, MIB)
CORE_PASS = shape(8, 2, 16, D)
pass_core = call(pass_core_kernel, "s" + "v" * 8, "v", CORE_PASS, [], 0, MIB)
join = call(join_kernel, "s" + "v" * 9, "v", shape(8, 2, 2, 16, D), [], 0, MIB)
pair_sum = call(
    pair_sum_kernel, "svv", "v" * 4, (QUARTER,) * 4, [pltpu.VMEM((4, 256, D), BF16)], 0, 3 * MIB,
)
merge = call(merge_kernel, "v" * 6, "v", shape(64, 80, 128), [], 0, 4 * MIB)
spread = call(spread_kernel, "v", "v", shape(64, 128, 128), [], 0, 3 * MIB)


def widen(where, chunks, side, *before):
    return pl.pallas_call(
        functools.partial(widen_kernel, side),
        in_specs=[SMEM, VMEM] + [HBM] * len(before),
        out_specs=(HBM, HBM),
        out_shape=(shape(2, 1024, D, dtype=F32), shape(2, 4, 256, D, dtype=F32)),
        scratch_shapes=[
            pltpu.VMEM((4, 256, D), F32), pltpu.VMEM((4, 256, D), F32), DMA((4,)), DMA((4,)),
        ],
        input_output_aliases={2: 0, 3: 1} if before else {},
        name="widen",
        compiler_params=pltpu.CompilerParams(vmem_limit_bytes=16 * MIB),
        cost_estimate=pl.CostEstimate(flops=0, bytes_accessed=6 * MIB, transcendentals=0),
    )(where, chunks, *before)


def exchange(values, axes):
    return lax.all_to_all(values, axes, split_axis=0, concat_axis=0, tiled=True)


def shifted(pieces, axes):
    n = len(pieces)
    return [pieces[0]] + [
        lax.ppermute(pieces[k], axes, [(i, (i + k) % n) for i in range(n)]) for k in range(1, n)
    ]


def swap(value, axis):
    return lax.ppermute(value, axis, [(0, 1), (1, 0)])


def layer(latents, cotangent, w_row, w_col, keep_heads):
    where = jnp.stack([lax.axis_index(name) for name in AXES]).astype(jnp.int32)
    rows_in = exchange(latents.reshape(16, 2, 16, D), COL)
    grad_pieces = tile_to_lines(where, cotangent)
    grad_parts = shifted(grad_pieces, "y")
    grad_pass = pass_low(where, *grad_parts)
    grad_pass = swap(grad_pass, "zl")
    mid_send, qkv_row, left_row = row_forward(keep_heads, rows_in, w_row)
    mid_lines = exchange(mid_send, BOTH)
    probs_row, turned_row = row_prepare(qkv_row, left_row)
    grad_send, left_col, right_col, u_col = col_grad(
        where, keep_heads, mid_lines, w_col, *grad_parts, grad_pass
    )
    grad_rows = exchange(grad_send, BOTH)
    keep_col, send_col, *out_pieces = col_output(where, left_col, right_col, u_col, w_col)
    got_col = swap(send_col, "c")
    quarters = pair_sum(where, keep_col, got_col)
    quarters = shifted(quarters, "x")
    keep_row, send_row, right_row = row_backward(
        where, keep_heads, grad_rows, qkv_row, turned_row, probs_row, w_row
    )
    got_row = swap(send_row, "c")
    merged = merge(keep_row, got_row, *quarters)
    both = exchange(merged, CHIPS)
    totals = spread(both)
    chunks = exchange(totals, CHIPS)
    gin_pieces = row_input_gradient(where, rows_in, right_row, w_row)
    gin_parts = shifted(gin_pieces, ("zh", "x"))
    gin_core = pass_core(where, *gin_parts)
    gin_core = swap(gin_core, "c")
    grad_latents = join(where, *gin_parts, gin_core).reshape(32, 16, D)
    out_parts = shifted(out_pieces, ROW)
    output = lines_to_tile(where, *out_parts)
    other = swap(chunks, "c")
    halves_done = widen(where, chunks, 0)
    grad_row, grad_col = widen(where, other, 1, *halves_done)
    return (output, grad_latents, grad_row.reshape(4, D, D), grad_col.reshape(4, D, D))


def solution(mesh):
    fine = Mesh(mesh.devices.reshape(4, 2, 2, 4, 2), AXES)
    tile = P(ROW, COL, None)
    return jax.shard_map(
        layer,
        mesh=fine,
        in_specs=(tile, tile, P(), P(), P()),
        out_specs=(tile, tile, P(), P()),
        check_vma=False,
    )
```

```python
import functools

import jax
import jax.numpy as jnp
from jax import lax
from jax.experimental import pallas as pl
from jax.experimental.pallas import tpu as pltpu
from jax.sharding import Mesh, PartitionSpec as P


HEADS = 8
HEAD = 64
D = 512
PAIR = 128
N_PAIR = D // PAIR
LINE = 256
TOK = 512
N_ROW = 8
N_COL = 16
N_DEV = N_ROW * N_COL
EPSILON = 1e-06
SCALE = HEAD ** (-0.5)

F32 = jnp.float32
BF16 = jnp.bfloat16

AXES = ("y", "zl", "zh", "x", "c")
ROW = ("y", "zl")
COL = ("zh", "x", "c")
BOTH = COL + ROW
CHIPS = ("y", "zl", "zh", "x")


def dot(left, right):
    return lax.dot_general(left, right, (((1,), (0,)), ((), ())), preferred_element_type=F32)


def dot_nt(left, right):
    return lax.dot_general(left, right, (((1,), (1,)), ((), ())), preferred_element_type=F32)


def stack_halves(value):
    lane = lax.broadcasted_iota(jnp.int32, value.shape, 1)
    zero = jnp.zeros_like(value)
    low, high = jnp.where(lane < HEAD, value, zero), jnp.where(lane >= HEAD, value, zero)
    return jnp.concatenate([low, high], axis=0)


def pick_halves(value):
    low, high = value[:LINE], value[LINE:]
    lane = lax.broadcasted_iota(jnp.int32, low.shape, 1)
    return jnp.where(lane < HEAD, low, high)


def turn_halves(value):
    return jnp.concatenate([value[:LINE].T, value[LINE:].T], axis=0)


def gain_row(info_ref, block, first, count):
    head = lax.broadcasted_iota(jnp.int32, (1, count * HEAD), 1) // HEAD
    gain = jnp.zeros((1, count * HEAD), F32)
    for i in range(count):
        gain = jnp.where(head == i, info_ref[5 + block * HEADS + first + i].astype(F32), gain)
    return gain


def inverse_rms(values_f):
    return lax.rsqrt(jnp.mean(values_f * values_f, axis=-1, keepdims=True) + EPSILON)


def softmax(q_pair, k_pair):
    scores = dot_nt(stack_halves(q_pair), k_pair)
    peak = jnp.max(scores, axis=-1, keepdims=True)
    grown = jnp.exp(scores - peak)
    return grown * (1.0 / jnp.sum(grown, axis=-1, keepdims=True))


def slot(col_local, group, row_local):
    return col_local * 8 + group * 2 + row_local


def copies_of(source, target, sems, count):
    return [pltpu.make_async_copy(source.at[i], target.at[i], sems.at[i]) for i in range(count)]


def start_all(copies):
    for copy in copies:
        copy.start()


def wait_all(copies):
    for copy in copies:
        copy.wait()


def project(normed, qkv_ref, w_s, copies):
    copies[0].wait()
    qkv_ref[0] = (dot(normed, w_s[0]).astype(BF16).astype(F32) * SCALE).astype(BF16)
    copies[1].wait()
    qkv_ref[1] = dot(normed, w_s[1]).astype(BF16)
    copies[2].wait()
    qkv_ref[2] = dot(normed, w_s[2]).astype(BF16)


def each_pair(visit, per_step=2):
    def step(index, carry):
        line = index // (N_PAIR // per_step)
        first = lax.rem(index, N_PAIR // per_step) * per_step
        rows = pl.ds(pl.multiple_of(line * LINE, LINE), LINE)
        for offset in range(per_step):
            pair = first + offset
            lanes = pl.ds(pl.multiple_of(pair * PAIR, PAIR), PAIR)
            visit(rows, lanes, line * N_PAIR + pair, pair)
        return carry

    lax.fori_loop(0, 2 * N_PAIR // per_step, step, 0)


def row_forward_kernel(
    where_ref, x_ref, w_ref, mid_ref, saved_ref,
    mix_s, mid_s, qkv_s, left_s, w_s, w_sem, mid_sem, qkv_sem, left_sem,
):
    weights = copies_of(w_ref, w_s, w_sem, 4)
    start_all(weights)
    saved = copies_of(qkv_s, saved_ref, qkv_sem, 3)
    lefts = copies_of(left_s, saved_ref.at[3:5], left_sem, 2)
    for rr in range(2):
        u = x_ref[:, rr].astype(F32).reshape(LINE, D)
        left_s[0, rr * LINE : (rr + 1) * LINE, :] = (u * inverse_rms(u)).astype(BF16)
    project(left_s[0], qkv_s, w_s, weights)
    lefts[0].start()
    start_all(saved)

    def visit(rows, lanes, at, pair):
        probs = softmax(qkv_s[0, rows, lanes], qkv_s[1, rows, lanes]).astype(BF16)
        mixed = pick_halves(dot(probs, qkv_s[2, rows, lanes]))
        left_s[1, rows, lanes] = (mixed * gain_row(where_ref, 0, pair * 2, 2)).astype(BF16)

    each_pair(visit, 4)
    lefts[1].start()
    weights[3].wait()
    added = dot(left_s[1], w_s[3])
    for rr in range(2):
        u = x_ref[:, rr].astype(F32).reshape(LINE, D)
        mid = (u + added[rr * LINE : (rr + 1) * LINE]).reshape(16, 2, 8, D)
        for cc in range(2):
            for group in range(4):
                piece = mid[:, cc, :, group * 128 : (group + 1) * 128].reshape(128, 128)
                mix_s[pl.ds(slot(cc, group, rr), 128, stride=16), :] = piece
    sends = []
    for part in range(4):
        rows = slice(part * 32, (part + 1) * 32)
        mid_s[rows] = mix_s[part * 512 : (part + 1) * 512, :].reshape(32, 16, 128).astype(BF16)
        sends.append(pltpu.make_async_copy(mid_s.at[rows], mid_ref.at[rows], mid_sem.at[part]))
        sends[-1].start()
    wait_all(saved + lefts + sends)


def row_prepare_kernel(saved_ref, probs_ref, turned_ref):
    def visit(rows, lanes, at, pair):
        probs = softmax(saved_ref[0, rows, lanes], saved_ref[1, rows, lanes])
        probs_ref[at] = probs.astype(BF16)

    each_pair(visit)
    for which in range(2):
        turned_ref[which] = saved_ref[3 + which].T


def attention_backward(rows, lanes, qkv, da_ref, probs, right_ref):
    q_pair, k_pair, v_pair = (qkv[i, rows, lanes] for i in range(3))
    da_pair = da_ref[rows, lanes]
    low = probs.astype(BF16)
    probs = probs.astype(F32)
    grad_probs = dot_nt(stack_halves(da_pair), v_pair)
    total = jnp.sum(probs * grad_probs, axis=-1, keepdims=True)
    grads = (probs * (grad_probs - total)).astype(BF16)
    right_ref[0, rows, lanes] = (pick_halves(dot(grads, k_pair)) * SCALE).astype(BF16)
    right_ref[1, rows, lanes] = pick_halves(dot(turn_halves(grads), q_pair)).astype(BF16)
    right_ref[2, rows, lanes] = pick_halves(dot(turn_halves(low), da_pair)).astype(BF16)
    return low


def input_gradient(u, right_ref, w_s, rows):
    inv = inverse_rms(u)
    dn = (
        dot_nt(right_ref[0, rows, :], w_s[0])
        + dot_nt(right_ref[1, rows, :], w_s[1])
        + dot_nt(right_ref[2, rows, :], w_s[2])
    )
    mean = jnp.mean(dn * u, axis=-1, keepdims=True)
    return right_ref[3, rows, :].astype(F32) + inv * dn - u * (inv * inv * inv * mean)


def weight_gradients(side, turned, right_ref, target):
    for j in range(2):
        which = side * 2 + j
        target[j] = dot(turned[which // 3], right_ref[which]).astype(BF16)


def row_backward_kernel(
    where_ref, g_ref, qkv_ref, turned_ref, probs_ref, w_ref,
    keep_ref, send_ref, right_ref,
    mix_s, da_s, wo_s, qkv_s, turned_s, probs_s, keep_s, send_s, right_s,
    wo_sem, qkv_sem, turned_sem, probs_sem, half_sem, right_sem,
):
    weight = pltpu.make_async_copy(w_ref.at[3], wo_s, wo_sem)
    weight.start()
    saved = copies_of(qkv_ref, qkv_s, qkv_sem, 3)
    start_all(saved)
    probs = [
        pltpu.make_async_copy(
            probs_ref.at[i * 2 : (i + 1) * 2], probs_s.at[i * 2 : (i + 1) * 2], probs_sem.at[i]
        )
        for i in range(4)
    ]
    start_all(probs)
    turned = copies_of(turned_ref, turned_s, turned_sem, 2)
    start_all(turned)
    mix_s[...] = g_ref[...].astype(F32).reshape(N_DEV * 16, 128)
    for rr in range(2):
        for group in range(4):
            sides = [
                mix_s[pl.ds(slot(cc, group, rr), 128, stride=16), :].reshape(16, 8, 128)
                for cc in range(2)
            ]
            right_s[3, rr * LINE : (rr + 1) * LINE, group * 128 : (group + 1) * 128] = (
                jnp.stack(sides, axis=1).reshape(LINE, 128).astype(BF16)
            )
    weight.wait()
    gain = gain_row(where_ref, 0, 0, HEADS)
    da_s[...] = (dot_nt(right_s[3], wo_s[...]) * gain).astype(BF16)
    wait_all(saved + probs)

    def visit(rows, lanes, at, pair):
        attention_backward(rows, lanes, qkv_s, da_s, probs_s[at], right_s)

    each_pair(visit, 4)
    rights = copies_of(right_s, right_ref, right_sem, 4)
    start_all(rights)
    wait_all(turned)
    core = where_ref[4]
    weight_gradients(1 - core, turned_s, right_s, send_s)
    sent = pltpu.make_async_copy(send_s, send_ref, half_sem.at[0])
    sent.start()
    weight_gradients(core, turned_s, right_s, keep_s)
    kept = pltpu.make_async_copy(keep_s, keep_ref, half_sem.at[1])
    kept.start()
    wait_all(rights + [sent, kept])


def row_input_gradient_kernel(where_ref, x_ref, right_ref, w_ref, *refs):
    outs, w_s, sems, gin_s = refs[:8], refs[8], refs[9], refs[10]
    copies = copies_of(w_ref, w_s, sems, 3)
    start_all(copies)
    wait_all(copies)
    for rr in range(2):
        rows = slice(rr * LINE, (rr + 1) * LINE)
        u = x_ref[:, rr].astype(F32).reshape(LINE, D)
        grad_in = input_gradient(u, right_ref, w_s, rows)
        gin_s[:, :, rr] = grad_in.astype(BF16).reshape(8, 2, 16, D)
    chip = where_ref[2] * 4 + where_ref[3]
    for shift in range(8):
        outs[shift][...] = gin_s[lax.rem(chip + shift, 8)]


def col_kernel(where_ref, m_ref, w_ref, *refs):
    parts, got_ref, refs = refs[:4], refs[4], refs[5:]
    gmid_ref, saved_ref = refs[:2]
    mix_s, u_s, ulow_s, left_s, right_s, qkv_s, da_s, w_s, parts_s, got_s = refs[2:12]
    w_sem, left_sem, right_sem, u_sem, parts_sem, got_sem = refs[12:]
    mine = where_ref[1]
    pieces = [
        pltpu.make_async_copy(parts[i].at[mine], parts_s.at[i], parts_sem.at[i]) for i in range(4)
    ]
    pieces.append(pltpu.make_async_copy(got_ref, got_s, got_sem))
    start_all(pieces)
    weights = copies_of(w_ref, w_s, w_sem, 4)
    for i in (3, 0, 1, 2):
        weights[i].start()
    rights = copies_of(right_s, saved_ref, right_sem, 4)
    lefts = copies_of(left_s, saved_ref.at[4:6], left_sem, 2)
    mix_s[...] = m_ref[...].astype(F32).reshape(N_DEV * 16, 128)
    for cc in range(2):
        for rr in range(2):
            base = cc * LINE + rr * 128
            for group in range(4):
                for grid_row in range(N_ROW):
                    start = base + grid_row * 16
                    u_s[start : start + 16, group * 128 : (group + 1) * 128] = mix_s[
                        pl.ds(grid_row * 16 + slot(cc, group, rr), 16, stride=128), :
                    ]
    u = u_s[...]
    ulow_s[...] = u.astype(BF16)
    kept_u = pltpu.make_async_copy(ulow_s, saved_ref.at[6], u_sem)
    kept_u.start()
    left_s[0] = (u * inverse_rms(u)).astype(BF16)
    lefts[0].start()
    wait_all(pieces)
    for shift in range(4):
        source = lax.rem(where_ref[0] + (4 - shift), 4) * 2
        for grid_row, piece in ((source + mine, parts_s.at[shift]), (source + (1 - mine), got_s.at[shift])):
            for cc in range(2):
                for rr in range(2):
                    at = pl.multiple_of(grid_row * 16 + (cc * LINE + rr * 128), 16)
                    right_s[3, pl.ds(at, 16), :] = piece[cc, rr * 16 : (rr + 1) * 16, :]
    rights[3].start()
    weights[3].wait()
    gain = gain_row(where_ref, 1, 0, HEADS)
    da_s[...] = (dot_nt(right_s[3], w_s[3]) * gain).astype(BF16)
    project(left_s[0], qkv_s, w_s, weights)

    def visit(rows, lanes, at, pair):
        probs = softmax(qkv_s[0, rows, lanes], qkv_s[1, rows, lanes])
        low = attention_backward(rows, lanes, qkv_s, da_s, probs, right_s)
        mixed = pick_halves(dot(low, qkv_s[2, rows, lanes]))
        left_s[1, rows, lanes] = (mixed * gain_row(where_ref, 1, pair * 2, 2)).astype(BF16)

    each_pair(visit, 4)
    lefts[1].start()
    start_all(rights[:3])
    for cc in range(2):
        rows = slice(cc * LINE, (cc + 1) * LINE)
        grad_in = input_gradient(u_s[rows, :], right_s, w_s, rows)
        for rr in range(2):
            for group in range(4):
                for grid_row in range(N_ROW):
                    start = rr * 128 + grid_row * 16
                    mix_s[pl.ds(grid_row * 16 + slot(cc, group, rr), 16, stride=128), :] = grad_in[
                        start : start + 16, group * 128 : (group + 1) * 128
                    ]
    gmid_ref[...] = mix_s[...].reshape(N_DEV, 16, 128).astype(BF16)
    wait_all(lefts + rights + [kept_u])


def col_weights_kernel(where_ref, saved_ref, keep_ref, send_ref, *refs):
    left_s, right_s, turned_s, keep_s, send_s, left_sem, right_sem, half_sem = refs
    lefts = copies_of(saved_ref.at[4:6], left_s, left_sem, 2)
    rights = copies_of(saved_ref, right_s, right_sem, 4)
    start_all(lefts + rights)
    core = where_ref[4]
    for which in range(2):
        lefts[which].wait()
        turned_s[which] = left_s[which].T
    wait_all(rights)
    weight_gradients(1 - core, turned_s, right_s, send_s)
    sent = pltpu.make_async_copy(send_s, send_ref, half_sem.at[0])
    sent.start()
    weight_gradients(core, turned_s, right_s, keep_s)
    kept = pltpu.make_async_copy(keep_s, keep_ref, half_sem.at[1])
    kept.start()
    wait_all([sent, kept])


def col_output_kernel(where_ref, saved_ref, w_ref, *refs):
    outs, (att_s, ulow_s, wo_s, out_s, sem) = refs[:8], refs[8:]
    copies = [
        pltpu.make_async_copy(saved_ref.at[5], att_s, sem.at[0]),
        pltpu.make_async_copy(w_ref.at[3], wo_s, sem.at[1]),
        pltpu.make_async_copy(saved_ref.at[6], ulow_s, sem.at[2]),
    ]
    start_all(copies)
    wait_all(copies)
    out_s[...] = (ulow_s[...].astype(F32) + dot(att_s[...], wo_s[...])).astype(BF16)
    me = where_ref[0] * 2 + where_ref[1]
    for shift in range(8):
        start = lax.rem(me + shift, 8) * 16
        for cc in range(2):
            for rr in range(2):
                at = pl.multiple_of(start + (cc * LINE + rr * 128), 16)
                outs[shift][cc, rr * 16 : (rr + 1) * 16, :] = out_s[pl.ds(at, 16), :]


def tile_to_lines_kernel(where_ref, tile_ref, *refs):
    outs, mix_s = refs[:4], refs[4]
    tile = tile_ref[...].astype(F32).reshape(TOK, D)
    for group in range(4):
        lanes = slice(group * 128, (group + 1) * 128)
        mix_s[group] = tile[:, lanes]
        for shift in range(4):
            for low in range(2):
                peer = lax.rem(where_ref[0] + shift, 4) * 2 + low
                for cc in range(2):
                    for rr in range(2):
                        piece = mix_s[group, pl.ds(peer + (rr * 16 + cc * 8), 16, stride=32), :]
                        outs[shift][low, cc, rr * 16 : (rr + 1) * 16, lanes] = piece.astype(BF16)


def pass_low_kernel(where_ref, *refs):
    parts, pass_ref = refs[:4], refs[4]
    for shift in range(4):
        pass_ref[shift] = parts[shift][1 - where_ref[1]]


def lines_to_tile_kernel(where_ref, *refs):
    parts, tile_ref, mix_s = refs[:8], refs[8], refs[9]
    me = where_ref[0] * 2 + where_ref[1]
    for group in range(4):
        lanes = slice(group * 128, (group + 1) * 128)
        for shift in range(8):
            peer = lax.rem(me + (8 - shift), 8)
            for cc in range(2):
                for rr in range(2):
                    piece = parts[shift][cc, rr * 16 : (rr + 1) * 16, lanes].astype(F32)
                    mix_s[group, pl.ds(peer + (rr * 16 + cc * 8), 16, stride=32), :] = piece
        tile_ref[:, :, lanes] = mix_s[group].astype(BF16).reshape(32, 16, 128)


def pass_core_kernel(where_ref, *refs):
    parts, pass_ref = refs[:8], refs[8]
    for shift in range(8):
        pass_ref[shift] = parts[shift][1 - where_ref[4]]


def join_kernel(where_ref, *refs):
    parts, passed_ref, tile_ref = refs[:8], refs[8], refs[9]
    chip, core = where_ref[2] * 4 + where_ref[3], where_ref[4]
    for shift in range(8):
        source = lax.rem(chip + (8 - shift), 8)
        tile_ref[source, core] = parts[shift][core]
        tile_ref[source, 1 - core] = passed_ref[shift]


def pair_sum_kernel(where_ref, keep_ref, got_ref, *refs):
    outs, sum_s = refs[:4], refs[4]
    total = keep_ref[...].astype(F32) + got_ref[...].astype(F32)
    sum_s[...] = total.astype(BF16).reshape(4, 256, D)
    for shift in range(4):
        outs[shift][...] = sum_s[lax.rem(where_ref[3] + shift, 4)]


def merge_kernel(keep_ref, got_ref, *refs):
    quarters, both_ref = refs[:4], refs[4]
    total = keep_ref[...].astype(F32) + got_ref[...].astype(F32)
    rows = total.astype(BF16).reshape(64, 16, D)
    quarter = quarters[0][...].astype(F32)
    for i in range(1, 4):
        quarter = quarter + quarters[i][...].astype(F32)
    quarter = quarter.astype(BF16).reshape(16, 16, D)
    for group in range(4):
        lanes = slice(group * 128, (group + 1) * 128)
        both_ref[:, group * 16 : (group + 1) * 16, :] = rows[:, :, lanes]
        for block in range(16):
            both_ref[block * 4 + group, 64:80, :] = quarter[block, :, lanes]


def chip_sum(parts_ref, rows, first, step):
    total = parts_ref[first, rows, :].astype(F32)
    for chip in range(first + step, 64, step):
        total = total + parts_ref[chip, rows, :].astype(F32)
    return total.astype(BF16)


def spread_kernel(both_ref, spread_ref):
    row_sum = chip_sum(both_ref, slice(0, 64), 0, 1)
    spread_ref[:, 0:64, :] = jnp.broadcast_to(row_sum[None], (64, 64, 128))
    for quarter in range(4):
        part = chip_sum(both_ref, slice(64, 80), quarter, 4)
        first = 64 + quarter * 16
        spread_ref[:, first : first + 16, :] = jnp.broadcast_to(part[None], (64, 16, 128))


def widen_kernel(side, where_ref, chunks_ref, *refs):
    row_ref, col_ref, row_s, col_s, row_sem, col_sem = refs[-6:]
    half = where_ref[4] if side == 0 else 1 - where_ref[4]
    copies = []
    for part in range(4):
        chunks = slice(part * 16, (part + 1) * 16)
        for group in range(4):
            lanes = slice(group * 128, (group + 1) * 128)
            piece = chunks_ref[chunks, group * 16 : (group + 1) * 16, :].astype(F32)
            row_s[part, :, lanes] = piece.reshape(256, 128)
        rows = pl.ds(part * 256, 256)
        copies.append(
            pltpu.make_async_copy(row_s.at[part], row_ref.at[half, rows], row_sem.at[part])
        )
        copies[-1].start()
    for quarter in range(4):
        first = 64 + quarter * 16
        for block in range(16):
            for group in range(4):
                col_s[quarter, block * 16 : (block + 1) * 16, group * 128 : (group + 1) * 128] = (
                    chunks_ref[block * 4 + group, first : first + 16, :].astype(F32)
                )
        copies.append(
            pltpu.make_async_copy(col_s.at[quarter], col_ref.at[half, quarter], col_sem.at[quarter])
        )
        copies[-1].start()
    wait_all(copies)


MIB = 1 << 20
SMEM = pl.BlockSpec(memory_space=pltpu.SMEM)
VMEM = pl.BlockSpec(memory_space=pltpu.VMEM)
HBM = pl.BlockSpec(memory_space=pltpu.HBM)


SPACE = {"s": SMEM, "v": VMEM, "h": HBM}


def call(kernel, ins, out_kinds, outs, scratch, flops, moved, grant=16):
    spaces = tuple(SPACE[kind] for kind in out_kinds)
    return pl.pallas_call(
        kernel,
        in_specs=[SPACE[kind] for kind in ins],
        out_specs=spaces if isinstance(outs, tuple) else spaces[0],
        out_shape=outs,
        scratch_shapes=scratch,
        compiler_params=pltpu.CompilerParams(vmem_limit_bytes=grant * MIB),
        cost_estimate=pl.CostEstimate(flops=flops, bytes_accessed=moved, transcendentals=0),
    )


def shape(*dims, dtype=BF16):
    return jax.ShapeDtypeStruct(dims, dtype)


MATMUL = 2 * TOK * D * D
ATTEND = 2 * 16 * LINE * LINE * HEAD
MIX = pltpu.VMEM((N_DEV * 16, 128), F32)
MIX_TILE = pltpu.VMEM((4, TOK, 128), F32)
DMA = pltpu.SemaphoreType.DMA
WEIGHTS = [pltpu.VMEM((4, D, D), BF16), DMA((4,))]
WEIGHT = [pltpu.VMEM((D, D), BF16), DMA]
LINES = shape(2, 32, D)
PIECE = shape(2, 2, 32, D)
PASS = shape(4, 2, 32, D)
QUARTER = shape(256, D)
HALF = shape(2, D, D)
HALF_S = pltpu.VMEM((2, D, D), BF16)


def token_scratch(*lead, dtype=BF16):
    return pltpu.VMEM((*lead, TOK, D), dtype)


row_forward = call(
    row_forward_kernel,
    "svh",
    "hh",
    (shape(N_DEV, 16, 128), shape(5, TOK, D)),
    [
        MIX, pltpu.VMEM((N_DEV, 16, 128), BF16), token_scratch(3), token_scratch(2), *WEIGHTS,
        DMA((4,)), DMA((3,)), DMA((2,)),
    ],
    4 * MATMUL + 2 * ATTEND,
    6 * MIB,
    grant=50,
)
row_prepare = call(
    row_prepare_kernel, "v", "vv", (shape(8, TOK, LINE), shape(2, D, TOK)), [], ATTEND, 8 * MIB
)
row_backward = call(
    row_backward_kernel,
    "svhhhh",
    "hhh",
    (HALF, HALF, shape(4, TOK, D)),
    [
        MIX, token_scratch(), pltpu.VMEM((D, D), BF16), token_scratch(3),
        pltpu.VMEM((2, D, TOK), BF16), pltpu.VMEM((8, TOK, LINE), BF16), HALF_S, HALF_S,
        token_scratch(4), DMA, DMA((3,)), DMA((2,)), DMA((4,)), DMA((2,)), DMA((4,)),
    ],
    5 * MATMUL + 5 * ATTEND,
    12 * MIB,
    grant=50,
)
row_input_gradient = call(
    row_input_gradient_kernel,
    "svvh",
    "v" * 8,
    (shape(2, 2, 16, D),) * 8,
    [*WEIGHTS, pltpu.VMEM((8, 2, 2, 16, D), BF16)],
    3 * MATMUL,
    5 * MIB,
)
col_grad = call(
    col_kernel,
    "svh" + "h" * 5,
    "vh",
    (shape(N_DEV, 16, 128), shape(7, TOK, D)),
    [
        MIX, token_scratch(dtype=F32), token_scratch(), token_scratch(2), token_scratch(4),
        token_scratch(3), token_scratch(), WEIGHTS[0], pltpu.VMEM((4, 2, 32, D), BF16),
        pltpu.VMEM((4, 2, 32, D), BF16), DMA((4,)), DMA((2,)), DMA((4,)), DMA, DMA((4,)), DMA,
    ],
    8 * MATMUL + 6 * ATTEND,
    8 * MIB,
    grant=50,
)
col_weights = call(
    col_weights_kernel,
    "sh",
    "hh",
    (HALF, HALF),
    [
        token_scratch(2), token_scratch(4), pltpu.VMEM((2, D, TOK), BF16), HALF_S, HALF_S,
        DMA((2,)), DMA((4,)), DMA((2,)),
    ],
    4 * MATMUL,
    6 * MIB,
    grant=52,
)
col_output = call(
    col_output_kernel,
    "shh",
    "v" * 8,
    (LINES,) * 8,
    [token_scratch(), token_scratch(), pltpu.VMEM((D, D), BF16), token_scratch(), DMA((3,))],
    MATMUL,
    3 * MIB,
    grant=52,
)
tile_to_lines = call(tile_to_lines_kernel, "sv", "v" * 4, (PIECE,) * 4, [MIX_TILE], 0, MIB)
pass_low = call(pass_low_kernel, "s" + "v" * 4, "v", PASS, [], 0, MIB)
lines_to_tile = call(lines_to_tile_kernel, "s" + "v" * 8, "v", shape(32, 16, D), [MIX_TILE], 0, MIB)
CORE_PASS = shape(8, 2, 16, D)
pass_core = call(pass_core_kernel, "s" + "v" * 8, "v", CORE_PASS, [], 0, MIB)
join = call(join_kernel, "s" + "v" * 9, "v", shape(8, 2, 2, 16, D), [], 0, MIB)
pair_sum = call(
    pair_sum_kernel, "svv", "v" * 4, (QUARTER,) * 4, [pltpu.VMEM((4, 256, D), BF16)], 0, 3 * MIB,
)
merge = call(merge_kernel, "v" * 6, "v", shape(64, 80, 128), [], 0, 4 * MIB)
spread = call(spread_kernel, "v", "v", shape(64, 128, 128), [], 0, 3 * MIB)


def widen(where, chunks, side, *before):
    return pl.pallas_call(
        functools.partial(widen_kernel, side),
        in_specs=[SMEM, VMEM] + [HBM] * len(before),
        out_specs=(HBM, HBM),
        out_shape=(shape(2, 1024, D, dtype=F32), shape(2, 4, 256, D, dtype=F32)),
        scratch_shapes=[
            pltpu.VMEM((4, 256, D), F32), pltpu.VMEM((4, 256, D), F32), DMA((4,)), DMA((4,)),
        ],
        input_output_aliases={2: 0, 3: 1} if before else {},
        name="widen",
        compiler_params=pltpu.CompilerParams(vmem_limit_bytes=16 * MIB),
        cost_estimate=pl.CostEstimate(flops=0, bytes_accessed=6 * MIB, transcendentals=0),
    )(where, chunks, *before)


def exchange(values, axes):
    return lax.all_to_all(values, axes, split_axis=0, concat_axis=0, tiled=True)


def shifted(pieces, axes):
    n = len(pieces)
    return [pieces[0]] + [
        lax.ppermute(pieces[k], axes, [(i, (i + k) % n) for i in range(n)]) for k in range(1, n)
    ]


def swap(value, axis):
    return lax.ppermute(value, axis, [(0, 1), (1, 0)])


def layer(latents, cotangent, w_row, w_col, keep_heads):
    where = jnp.concatenate(
        [jnp.stack([lax.axis_index(name) for name in AXES]), keep_heads.reshape(-1)]
    ).astype(jnp.int32)
    rows_in = exchange(latents.reshape(16, 2, 16, D), COL)
    grad_pieces = tile_to_lines(where, cotangent)
    grad_parts = shifted(grad_pieces, "y")
    grad_pass = pass_low(where, *grad_parts)
    grad_pass = swap(grad_pass, "zl")
    mid_send, saved_row = row_forward(where, rows_in, w_row)
    mid_lines = exchange(mid_send, BOTH)
    probs_row, turned_row = row_prepare(saved_row)
    grad_send, saved_col = col_grad(
        where, mid_lines, w_col, *grad_parts, grad_pass
    )
    grad_rows = exchange(grad_send, BOTH)
    keep_col, send_col = col_weights(where, saved_col)
    got_col = swap(send_col, "c")
    quarters = pair_sum(where, keep_col, got_col)
    quarters = shifted(quarters, "x")
    keep_row, send_row, right_row = row_backward(
        where, grad_rows, saved_row, turned_row, probs_row, w_row
    )
    got_row = swap(send_row, "c")
    merged = merge(keep_row, got_row, *quarters)
    both = exchange(merged, CHIPS)
    totals = spread(both)
    chunks = exchange(totals, CHIPS)
    gin_pieces = row_input_gradient(where, rows_in, right_row, w_row)
    gin_parts = shifted(gin_pieces, ("zh", "x"))
    gin_core = pass_core(where, *gin_parts)
    gin_core = swap(gin_core, "c")
    grad_latents = join(where, *gin_parts, gin_core).reshape(32, 16, D)
    out_pieces = col_output(where, saved_col, w_col)
    out_parts = shifted(out_pieces, ROW)
    output = lines_to_tile(where, *out_parts)
    other = swap(chunks, "c")
    halves_done = widen(where, chunks, 0)
    grad_row, grad_col = widen(where, other, 1, *halves_done)
    return (output, grad_latents, grad_row.reshape(4, D, D), grad_col.reshape(4, D, D))


def solution(mesh):
    fine = Mesh(mesh.devices.reshape(4, 2, 2, 4, 2), AXES)
    tile = P(ROW, COL, None)
    return jax.shard_map(
        layer,
        mesh=fine,
        in_specs=(tile, tile, P(), P(), P()),
        out_specs=(tile, tile, P(), P()),
        check_vma=False,
    )
```

```python
import functools

import jax
import jax.numpy as jnp
from jax import lax
from jax.experimental import pallas as pl
from jax.experimental.pallas import tpu as pltpu
from jax.sharding import Mesh, PartitionSpec as P


HEADS = 8
HEAD = 64
D = 512
PAIR = 128
N_PAIR = D // PAIR
LINE = 256
TOK = 512
N_ROW = 8
N_COL = 16
N_DEV = N_ROW * N_COL
EPSILON = 1e-06
SCALE = HEAD ** (-0.5)

F32 = jnp.float32
BF16 = jnp.bfloat16

AXES = ("y", "zl", "zh", "x", "c")
ROW = ("y", "zl")
COL = ("zh", "x", "c")
BOTH = COL + ROW
CHIPS = ("y", "zl", "zh", "x")


def dot(left, right):
    return lax.dot_general(left, right, (((1,), (0,)), ((), ())), preferred_element_type=F32)


def dot_nt(left, right):
    return lax.dot_general(left, right, (((1,), (1,)), ((), ())), preferred_element_type=F32)


def stack_halves(value):
    lane = lax.broadcasted_iota(jnp.int32, value.shape, 1)
    zero = jnp.zeros_like(value)
    low, high = jnp.where(lane < HEAD, value, zero), jnp.where(lane >= HEAD, value, zero)
    return jnp.concatenate([low, high], axis=0)


def pick_halves(value):
    low, high = value[:LINE], value[LINE:]
    lane = lax.broadcasted_iota(jnp.int32, low.shape, 1)
    return jnp.where(lane < HEAD, low, high)


def turn_halves(value):
    return jnp.concatenate([value[:LINE].T, value[LINE:].T], axis=0)


def gain_row(info_ref, block, first, count):
    head = lax.broadcasted_iota(jnp.int32, (1, count * HEAD), 1) // HEAD
    gain = jnp.zeros((1, count * HEAD), F32)
    for i in range(count):
        gain = jnp.where(head == i, info_ref[5 + block * HEADS + first + i].astype(F32), gain)
    return gain


def inverse_rms(values_f):
    return lax.rsqrt(jnp.mean(values_f * values_f, axis=-1, keepdims=True) + EPSILON)


def softmax(q_pair, k_pair):
    scores = dot_nt(stack_halves(q_pair), k_pair)
    peak = jnp.max(scores, axis=-1, keepdims=True)
    grown = jnp.exp(scores - peak)
    return grown * (1.0 / jnp.sum(grown, axis=-1, keepdims=True))


def slot(col_local, group, row_local):
    return col_local * 8 + group * 2 + row_local


def copies_of(source, target, sems, count):
    return [pltpu.make_async_copy(source.at[i], target.at[i], sems.at[i]) for i in range(count)]


def start_all(copies):
    for copy in copies:
        copy.start()


def wait_all(copies):
    for copy in copies:
        copy.wait()


def project(normed, qkv_ref, w_s, copies):
    copies[0].wait()
    qkv_ref[0] = (dot(normed, w_s[0]).astype(BF16).astype(F32) * SCALE).astype(BF16)
    copies[1].wait()
    qkv_ref[1] = dot(normed, w_s[1]).astype(BF16)
    copies[2].wait()
    qkv_ref[2] = dot(normed, w_s[2]).astype(BF16)


def each_pair(visit, per_step=2):
    def step(index, carry):
        line = index // (N_PAIR // per_step)
        first = lax.rem(index, N_PAIR // per_step) * per_step
        rows = pl.ds(pl.multiple_of(line * LINE, LINE), LINE)
        for offset in range(per_step):
            pair = first + offset
            lanes = pl.ds(pl.multiple_of(pair * PAIR, PAIR), PAIR)
            visit(rows, lanes, line * N_PAIR + pair, pair)
        return carry

    lax.fori_loop(0, 2 * N_PAIR // per_step, step, 0)


def row_forward_kernel(
    where_ref, x_ref, w_ref, mid_ref, saved_ref,
    mix_s, mid_s, qkv_s, left_s, w_s, w_sem, mid_sem, qkv_sem, left_sem,
):
    weights = copies_of(w_ref, w_s, w_sem, 4)
    start_all(weights)
    saved = copies_of(qkv_s, saved_ref, qkv_sem, 3)
    lefts = copies_of(left_s, saved_ref.at[3:5], left_sem, 2)
    for rr in range(2):
        u = x_ref[:, rr].astype(F32).reshape(LINE, D)
        left_s[0, rr * LINE : (rr + 1) * LINE, :] = (u * inverse_rms(u)).astype(BF16)
    project(left_s[0], qkv_s, w_s, weights)
    lefts[0].start()
    start_all(saved)

    def visit(rows, lanes, at, pair):
        probs = softmax(qkv_s[0, rows, lanes], qkv_s[1, rows, lanes]).astype(BF16)
        mixed = pick_halves(dot(probs, qkv_s[2, rows, lanes]))
        left_s[1, rows, lanes] = (mixed * gain_row(where_ref, 0, pair * 2, 2)).astype(BF16)

    each_pair(visit, 4)
    lefts[1].start()
    weights[3].wait()
    added = dot(left_s[1], w_s[3])
    for rr in range(2):
        u = x_ref[:, rr].astype(F32).reshape(LINE, D)
        mid = (u + added[rr * LINE : (rr + 1) * LINE]).reshape(16, 2, 8, D)
        for cc in range(2):
            for group in range(4):
                piece = mid[:, cc, :, group * 128 : (group + 1) * 128].reshape(128, 128)
                mix_s[pl.ds(slot(cc, group, rr), 128, stride=16), :] = piece
    sends = []
    for part in range(4):
        rows = slice(part * 32, (part + 1) * 32)
        mid_s[rows] = mix_s[part * 512 : (part + 1) * 512, :].reshape(32, 16, 128).astype(BF16)
        sends.append(pltpu.make_async_copy(mid_s.at[rows], mid_ref.at[rows], mid_sem.at[part]))
        sends[-1].start()
    wait_all(saved + lefts + sends)


def row_prepare_kernel(saved_ref, probs_ref, turned_ref):
    def visit(rows, lanes, at, pair):
        probs = softmax(saved_ref[0, rows, lanes], saved_ref[1, rows, lanes])
        probs_ref[at] = probs.astype(BF16)

    each_pair(visit)
    for which in range(2):
        turned_ref[which] = saved_ref[3 + which].T


def attention_backward(rows, lanes, qkv, da_ref, probs, right_ref):
    q_pair, k_pair, v_pair = (qkv[i, rows, lanes] for i in range(3))
    da_pair = da_ref[rows, lanes]
    low = probs.astype(BF16)
    probs = probs.astype(F32)
    grad_probs = dot_nt(stack_halves(da_pair), v_pair)
    total = jnp.sum(probs * grad_probs, axis=-1, keepdims=True)
    grads = (probs * (grad_probs - total)).astype(BF16)
    right_ref[0, rows, lanes] = (pick_halves(dot(grads, k_pair)) * SCALE).astype(BF16)
    right_ref[1, rows, lanes] = pick_halves(dot(turn_halves(grads), q_pair)).astype(BF16)
    right_ref[2, rows, lanes] = pick_halves(dot(turn_halves(low), da_pair)).astype(BF16)
    return low


def input_gradient(u, right_ref, w_s, rows):
    inv = inverse_rms(u)
    dn = (
        dot_nt(right_ref[0, rows, :], w_s[0])
        + dot_nt(right_ref[1, rows, :], w_s[1])
        + dot_nt(right_ref[2, rows, :], w_s[2])
    )
    mean = jnp.mean(dn * u, axis=-1, keepdims=True)
    return right_ref[3, rows, :].astype(F32) + inv * dn - u * (inv * inv * inv * mean)


def weight_gradients(side, turned, right_ref, target):
    for j in range(2):
        which = side * 2 + j
        target[j] = dot(turned[which // 3], right_ref[which]).astype(BF16)


def row_backward_kernel(
    where_ref, g_ref, qkv_ref, turned_ref, probs_ref, w_ref,
    send_ref, right_ref,
    mix_s, da_s, wo_s, qkv_s, turned_s, probs_s, send_s, right_s,
    wo_sem, qkv_sem, turned_sem, probs_sem, half_sem, right_sem,
):
    weight = pltpu.make_async_copy(w_ref.at[3], wo_s, wo_sem)
    weight.start()
    saved = copies_of(qkv_ref, qkv_s, qkv_sem, 3)
    start_all(saved)
    probs = [
        pltpu.make_async_copy(
            probs_ref.at[i * 2 : (i + 1) * 2], probs_s.at[i * 2 : (i + 1) * 2], probs_sem.at[i]
        )
        for i in range(4)
    ]
    start_all(probs)
    turned = copies_of(turned_ref, turned_s, turned_sem, 2)
    start_all(turned)
    mix_s[...] = g_ref[...].astype(F32).reshape(N_DEV * 16, 128)
    for rr in range(2):
        for group in range(4):
            sides = [
                mix_s[pl.ds(slot(cc, group, rr), 128, stride=16), :].reshape(16, 8, 128)
                for cc in range(2)
            ]
            right_s[3, rr * LINE : (rr + 1) * LINE, group * 128 : (group + 1) * 128] = (
                jnp.stack(sides, axis=1).reshape(LINE, 128).astype(BF16)
            )
    weight.wait()
    gain = gain_row(where_ref, 0, 0, HEADS)
    da_s[...] = (dot_nt(right_s[3], wo_s[...]) * gain).astype(BF16)
    wait_all(saved + probs)

    def visit(rows, lanes, at, pair):
        attention_backward(rows, lanes, qkv_s, da_s, probs_s[at], right_s)

    each_pair(visit, 4)
    rights = copies_of(right_s, right_ref, right_sem, 4)
    start_all(rights)
    wait_all(turned)
    core = where_ref[4]
    weight_gradients(1 - core, turned_s, right_s, send_s)
    sent = pltpu.make_async_copy(send_s, send_ref, half_sem)
    sent.start()
    wait_all(rights + [sent])


def kept_gradients_kernel(where_ref, turned_ref, right_ref, keep_ref, turned_s, right_s, turned_sem, right_sem):
    core = where_ref[4]
    turned = copies_of(turned_ref, turned_s, turned_sem, 2)
    rights = copies_of(right_ref.at[pl.ds(core * 2, 2)], right_s, right_sem, 2)
    start_all(turned + rights)
    wait_all(turned + rights)
    for j in range(2):
        keep_ref[j] = dot(turned_s[(core * 2 + j) // 3], right_s[j]).astype(BF16)


def row_input_gradient_kernel(where_ref, x_ref, right_ref, w_ref, *refs):
    outs, w_s, right_s, gin_s, w_sem, right_sem = refs[:8], *refs[8:]
    weights = copies_of(w_ref, w_s, w_sem, 3)
    rights = copies_of(right_ref, right_s, right_sem, 4)
    start_all([copy for pair in zip(weights, rights) for copy in pair] + rights[3:])
    wait_all(weights + rights)
    for rr in range(2):
        rows = slice(rr * LINE, (rr + 1) * LINE)
        u = x_ref[:, rr].astype(F32).reshape(LINE, D)
        grad_in = input_gradient(u, right_s, w_s, rows)
        gin_s[:, :, rr] = grad_in.astype(BF16).reshape(8, 2, 16, D)
    chip = where_ref[2] * 4 + where_ref[3]
    for shift in range(8):
        outs[shift][...] = gin_s[lax.rem(chip + shift, 8)]


def col_kernel(where_ref, m_ref, w_ref, *refs):
    parts, got_ref, refs = refs[:4], refs[4], refs[5:]
    gmid_ref, saved_ref = refs[:2]
    mix_s, u_s, ulow_s, left_s, right_s, qkv_s, da_s, w_s, parts_s, got_s = refs[2:12]
    w_sem, left_sem, right_sem, u_sem, parts_sem, got_sem = refs[12:]
    mine = where_ref[1]
    pieces = [
        pltpu.make_async_copy(parts[i].at[mine], parts_s.at[i], parts_sem.at[i]) for i in range(4)
    ]
    pieces.append(pltpu.make_async_copy(got_ref, got_s, got_sem))
    start_all(pieces)
    weights = copies_of(w_ref, w_s, w_sem, 4)
    for i in (3, 0, 1, 2):
        weights[i].start()
    rights = copies_of(right_s, saved_ref, right_sem, 4)
    lefts = copies_of(left_s, saved_ref.at[4:6], left_sem, 2)
    mix_s[...] = m_ref[...].astype(F32).reshape(N_DEV * 16, 128)
    for cc in range(2):
        for rr in range(2):
            base = cc * LINE + rr * 128
            for group in range(4):
                for grid_row in range(N_ROW):
                    start = base + grid_row * 16
                    u_s[start : start + 16, group * 128 : (group + 1) * 128] = mix_s[
                        pl.ds(grid_row * 16 + slot(cc, group, rr), 16, stride=128), :
                    ]
    u = u_s[...]
    ulow_s[...] = u.astype(BF16)
    kept_u = pltpu.make_async_copy(ulow_s, saved_ref.at[6], u_sem)
    kept_u.start()
    left_s[0] = (u * inverse_rms(u)).astype(BF16)
    lefts[0].start()
    wait_all(pieces)
    for shift in range(4):
        source = lax.rem(where_ref[0] + (4 - shift), 4) * 2
        for grid_row, piece in ((source + mine, parts_s.at[shift]), (source + (1 - mine), got_s.at[shift])):
            for cc in range(2):
                for rr in range(2):
                    at = pl.multiple_of(grid_row * 16 + (cc * LINE + rr * 128), 16)
                    right_s[3, pl.ds(at, 16), :] = piece[cc, rr * 16 : (rr + 1) * 16, :]
    rights[3].start()
    weights[3].wait()
    gain = gain_row(where_ref, 1, 0, HEADS)
    da_s[...] = (dot_nt(right_s[3], w_s[3]) * gain).astype(BF16)
    project(left_s[0], qkv_s, w_s, weights)

    def visit(rows, lanes, at, pair):
        probs = softmax(qkv_s[0, rows, lanes], qkv_s[1, rows, lanes])
        low = attention_backward(rows, lanes, qkv_s, da_s, probs, right_s)
        mixed = pick_halves(dot(low, qkv_s[2, rows, lanes]))
        left_s[1, rows, lanes] = (mixed * gain_row(where_ref, 1, pair * 2, 2)).astype(BF16)

    each_pair(visit, 4)
    lefts[1].start()
    start_all(rights[:3])
    for cc in range(2):
        rows = slice(cc * LINE, (cc + 1) * LINE)
        grad_in = input_gradient(u_s[rows, :], right_s, w_s, rows)
        for rr in range(2):
            for group in range(4):
                for grid_row in range(N_ROW):
                    start = rr * 128 + grid_row * 16
                    mix_s[pl.ds(grid_row * 16 + slot(cc, group, rr), 16, stride=128), :] = grad_in[
                        start : start + 16, group * 128 : (group + 1) * 128
                    ]
    gmid_ref[...] = mix_s[...].reshape(N_DEV, 16, 128).astype(BF16)
    wait_all(lefts + rights + [kept_u])


def col_weights_kernel(where_ref, saved_ref, send_ref, turned_ref, *refs):
    left_s, right_s, turned_s, left_sem, right_sem, turned_sem = refs
    side = 1 - where_ref[4]
    lefts = copies_of(saved_ref.at[4:6], left_s, left_sem, 2)
    rights = copies_of(saved_ref.at[pl.ds(side * 2, 2)], right_s, right_sem, 2)
    start_all(lefts + rights)
    turned = copies_of(turned_s, turned_ref, turned_sem, 2)
    for which in range(2):
        lefts[which].wait()
        turned_s[which] = left_s[which].T
        turned[which].start()
    wait_all(rights)
    for j in range(2):
        send_ref[j] = dot(turned_s[(side * 2 + j) // 3], right_s[j]).astype(BF16)
    wait_all(turned)


def col_output_kernel(where_ref, saved_ref, w_ref, *refs):
    outs, (att_s, ulow_s, wo_s, out_s, sem) = refs[:8], refs[8:]
    copies = [
        pltpu.make_async_copy(saved_ref.at[5], att_s, sem.at[0]),
        pltpu.make_async_copy(w_ref.at[3], wo_s, sem.at[1]),
        pltpu.make_async_copy(saved_ref.at[6], ulow_s, sem.at[2]),
    ]
    start_all(copies)
    wait_all(copies)
    out_s[...] = (ulow_s[...].astype(F32) + dot(att_s[...], wo_s[...])).astype(BF16)
    me = where_ref[0] * 2 + where_ref[1]
    for shift in range(8):
        start = lax.rem(me + shift, 8) * 16
        for cc in range(2):
            for rr in range(2):
                at = pl.multiple_of(start + (cc * LINE + rr * 128), 16)
                outs[shift][cc, rr * 16 : (rr + 1) * 16, :] = out_s[pl.ds(at, 16), :]


def tile_to_lines_kernel(where_ref, tile_ref, *refs):
    outs, mix_s = refs[:4], refs[4]
    tile = tile_ref[...].astype(F32).reshape(TOK, D)
    for group in range(4):
        lanes = slice(group * 128, (group + 1) * 128)
        mix_s[group] = tile[:, lanes]
        for shift in range(4):
            for low in range(2):
                peer = lax.rem(where_ref[0] + shift, 4) * 2 + low
                for cc in range(2):
                    for rr in range(2):
                        piece = mix_s[group, pl.ds(peer + (rr * 16 + cc * 8), 16, stride=32), :]
                        outs[shift][low, cc, rr * 16 : (rr + 1) * 16, lanes] = piece.astype(BF16)


def pass_low_kernel(where_ref, *refs):
    parts, pass_ref = refs[:4], refs[4]
    for shift in range(4):
        pass_ref[shift] = parts[shift][1 - where_ref[1]]


def lines_to_tile_kernel(where_ref, *refs):
    parts, tile_ref, mix_s = refs[:8], refs[8], refs[9]
    me = where_ref[0] * 2 + where_ref[1]
    for group in range(4):
        lanes = slice(group * 128, (group + 1) * 128)
        for shift in range(8):
            peer = lax.rem(me + (8 - shift), 8)
            for cc in range(2):
                for rr in range(2):
                    piece = parts[shift][cc, rr * 16 : (rr + 1) * 16, lanes].astype(F32)
                    mix_s[group, pl.ds(peer + (rr * 16 + cc * 8), 16, stride=32), :] = piece
        tile_ref[:, :, lanes] = mix_s[group].astype(BF16).reshape(32, 16, 128)


def pass_core_kernel(where_ref, *refs):
    parts, pass_ref = refs[:8], refs[8]
    for shift in range(8):
        pass_ref[shift] = parts[shift][1 - where_ref[4]]


def join_kernel(where_ref, *refs):
    parts, passed_ref, tile_ref = refs[:8], refs[8], refs[9]
    chip, core = where_ref[2] * 4 + where_ref[3], where_ref[4]
    for shift in range(8):
        source = lax.rem(chip + (8 - shift), 8)
        tile_ref[source, core] = parts[shift][core]
        tile_ref[source, 1 - core] = passed_ref[shift]


def pair_sum_kernel(where_ref, keep_ref, got_ref, *refs):
    outs, sum_s = refs[:4], refs[4]
    total = keep_ref[...].astype(F32) + got_ref[...].astype(F32)
    sum_s[...] = total.astype(BF16).reshape(4, 256, D)
    for shift in range(4):
        outs[shift][...] = sum_s[lax.rem(where_ref[3] + shift, 4)]


def merge_kernel(keep_ref, got_ref, *refs):
    quarters, both_ref = refs[:4], refs[4]
    total = keep_ref[...].astype(F32) + got_ref[...].astype(F32)
    rows = total.astype(BF16).reshape(64, 16, D)
    quarter = quarters[0][...].astype(F32)
    for i in range(1, 4):
        quarter = quarter + quarters[i][...].astype(F32)
    quarter = quarter.astype(BF16).reshape(16, 16, D)
    for group in range(4):
        lanes = slice(group * 128, (group + 1) * 128)
        both_ref[:, group * 16 : (group + 1) * 16, :] = rows[:, :, lanes]
        for block in range(16):
            both_ref[block * 4 + group, 64:80, :] = quarter[block, :, lanes]


def chip_sum(parts_ref, rows, first, step):
    total = parts_ref[first, rows, :].astype(F32)
    for chip in range(first + step, 64, step):
        total = total + parts_ref[chip, rows, :].astype(F32)
    return total.astype(BF16)


def spread_kernel(both_ref, spread_ref):
    row_sum = chip_sum(both_ref, slice(0, 64), 0, 1)
    spread_ref[:, 0:64, :] = jnp.broadcast_to(row_sum[None], (64, 64, 128))
    for quarter in range(4):
        part = chip_sum(both_ref, slice(64, 80), quarter, 4)
        first = 64 + quarter * 16
        spread_ref[:, first : first + 16, :] = jnp.broadcast_to(part[None], (64, 16, 128))


def widen_kernel(side, where_ref, chunks_ref, *refs):
    row_ref, col_ref, row_s, col_s, row_sem, col_sem = refs[-6:]
    half = where_ref[4] if side == 0 else 1 - where_ref[4]
    copies = []
    for part in range(4):
        chunks = slice(part * 16, (part + 1) * 16)
        for group in range(4):
            lanes = slice(group * 128, (group + 1) * 128)
            piece = chunks_ref[chunks, group * 16 : (group + 1) * 16, :].astype(F32)
            row_s[part, :, lanes] = piece.reshape(256, 128)
        rows = pl.ds(part * 256, 256)
        copies.append(
            pltpu.make_async_copy(row_s.at[part], row_ref.at[half, rows], row_sem.at[part])
        )
        copies[-1].start()
    for quarter in range(4):
        first = 64 + quarter * 16
        for block in range(16):
            for group in range(4):
                col_s[quarter, block * 16 : (block + 1) * 16, group * 128 : (group + 1) * 128] = (
                    chunks_ref[block * 4 + group, first : first + 16, :].astype(F32)
                )
        copies.append(
            pltpu.make_async_copy(col_s.at[quarter], col_ref.at[half, quarter], col_sem.at[quarter])
        )
        copies[-1].start()
    wait_all(copies)


MIB = 1 << 20
SMEM = pl.BlockSpec(memory_space=pltpu.SMEM)
VMEM = pl.BlockSpec(memory_space=pltpu.VMEM)
HBM = pl.BlockSpec(memory_space=pltpu.HBM)


SPACE = {"s": SMEM, "v": VMEM, "h": HBM}


def call(kernel, ins, out_kinds, outs, scratch, flops, moved, grant=16):
    spaces = tuple(SPACE[kind] for kind in out_kinds)
    return pl.pallas_call(
        kernel,
        in_specs=[SPACE[kind] for kind in ins],
        out_specs=spaces if isinstance(outs, tuple) else spaces[0],
        out_shape=outs,
        scratch_shapes=scratch,
        compiler_params=pltpu.CompilerParams(vmem_limit_bytes=grant * MIB),
        cost_estimate=pl.CostEstimate(flops=flops, bytes_accessed=moved, transcendentals=0),
    )


def shape(*dims, dtype=BF16):
    return jax.ShapeDtypeStruct(dims, dtype)


MATMUL = 2 * TOK * D * D
ATTEND = 2 * 16 * LINE * LINE * HEAD
MIX = pltpu.VMEM((N_DEV * 16, 128), F32)
MIX_TILE = pltpu.VMEM((4, TOK, 128), F32)
DMA = pltpu.SemaphoreType.DMA
WEIGHTS = [pltpu.VMEM((4, D, D), BF16), DMA((4,))]
WEIGHT = [pltpu.VMEM((D, D), BF16), DMA]
LINES = shape(2, 32, D)
PIECE = shape(2, 2, 32, D)
PASS = shape(4, 2, 32, D)
QUARTER = shape(256, D)
HALF = shape(2, D, D)
HALF_S = pltpu.VMEM((2, D, D), BF16)


def token_scratch(*lead, dtype=BF16):
    return pltpu.VMEM((*lead, TOK, D), dtype)


row_forward = call(
    row_forward_kernel,
    "svh",
    "hh",
    (shape(N_DEV, 16, 128), shape(5, TOK, D)),
    [
        MIX, pltpu.VMEM((N_DEV, 16, 128), BF16), token_scratch(3), token_scratch(2), *WEIGHTS,
        DMA((4,)), DMA((3,)), DMA((2,)),
    ],
    4 * MATMUL + 2 * ATTEND,
    6 * MIB,
    grant=50,
)
row_prepare = call(
    row_prepare_kernel, "v", "vv", (shape(8, TOK, LINE), shape(2, D, TOK)), [], ATTEND, 8 * MIB
)
row_backward = call(
    row_backward_kernel,
    "svhhhh",
    "hh",
    (HALF, shape(4, TOK, D)),
    [
        MIX, token_scratch(), pltpu.VMEM((D, D), BF16), token_scratch(3),
        pltpu.VMEM((2, D, TOK), BF16), pltpu.VMEM((8, TOK, LINE), BF16), HALF_S,
        token_scratch(4), DMA, DMA((3,)), DMA((2,)), DMA((4,)), DMA, DMA((4,)),
    ],
    5 * MATMUL + 5 * ATTEND,
    12 * MIB,
    grant=50,
)
kept_gradients = call(
    kept_gradients_kernel,
    "shh",
    "v",
    HALF,
    [pltpu.VMEM((2, D, TOK), BF16), token_scratch(2), DMA((2,)), DMA((2,))],
    2 * MATMUL,
    3 * MIB,
    grant=50,
)
row_input_gradient = call(
    row_input_gradient_kernel,
    "svhh",
    "v" * 8,
    (shape(2, 2, 16, D),) * 8,
    [
        pltpu.VMEM((3, D, D), BF16), token_scratch(4), pltpu.VMEM((8, 2, 2, 16, D), BF16),
        DMA((3,)), DMA((4,)),
    ],
    3 * MATMUL,
    5 * MIB,
    grant=50,
)
col_grad = call(
    col_kernel,
    "svh" + "h" * 5,
    "vh",
    (shape(N_DEV, 16, 128), shape(7, TOK, D)),
    [
        MIX, token_scratch(dtype=F32), token_scratch(), token_scratch(2), token_scratch(4),
        token_scratch(3), token_scratch(), WEIGHTS[0], pltpu.VMEM((4, 2, 32, D), BF16),
        pltpu.VMEM((4, 2, 32, D), BF16), DMA((4,)), DMA((2,)), DMA((4,)), DMA, DMA((4,)), DMA,
    ],
    8 * MATMUL + 6 * ATTEND,
    8 * MIB,
    grant=50,
)
col_weights = call(
    col_weights_kernel,
    "sh",
    "vh",
    (HALF, shape(2, D, TOK)),
    [
        token_scratch(2), token_scratch(2), pltpu.VMEM((2, D, TOK), BF16),
        DMA((2,)), DMA((2,)), DMA((2,)),
    ],
    2 * MATMUL,
    6 * MIB,
    grant=50,
)
col_output = call(
    col_output_kernel,
    "shh",
    "v" * 8,
    (LINES,) * 8,
    [token_scratch(), token_scratch(), pltpu.VMEM((D, D), BF16), token_scratch(), DMA((3,))],
    MATMUL,
    3 * MIB,
    grant=52,
)
tile_to_lines = call(tile_to_lines_kernel, "sv", "v" * 4, (PIECE,) * 4, [MIX_TILE], 0, MIB)
pass_low = call(pass_low_kernel, "s" + "v" * 4, "v", PASS, [], 0, MIB)
lines_to_tile = call(lines_to_tile_kernel, "s" + "v" * 8, "v", shape(32, 16, D), [MIX_TILE], 0, MIB)
CORE_PASS = shape(8, 2, 16, D)
pass_core = call(pass_core_kernel, "s" + "v" * 8, "v", CORE_PASS, [], 0, MIB)
join = call(join_kernel, "s" + "v" * 9, "v", shape(8, 2, 2, 16, D), [], 0, MIB)
pair_sum = call(
    pair_sum_kernel, "svv", "v" * 4, (QUARTER,) * 4, [pltpu.VMEM((4, 256, D), BF16)], 0, 3 * MIB,
)
merge = call(merge_kernel, "v" * 6, "v", shape(64, 80, 128), [], 0, 4 * MIB, grant=16)
spread = call(spread_kernel, "v", "v", shape(64, 128, 128), [], 0, 3 * MIB)


def widen(where, chunks, side, *before):
    return pl.pallas_call(
        functools.partial(widen_kernel, side),
        in_specs=[SMEM, VMEM] + [HBM] * len(before),
        out_specs=(HBM, HBM),
        out_shape=(shape(2, 1024, D, dtype=F32), shape(2, 4, 256, D, dtype=F32)),
        scratch_shapes=[
            pltpu.VMEM((4, 256, D), F32), pltpu.VMEM((4, 256, D), F32), DMA((4,)), DMA((4,)),
        ],
        input_output_aliases={2: 0, 3: 1} if before else {},
        name="widen",
        compiler_params=pltpu.CompilerParams(vmem_limit_bytes=16 * MIB),
        cost_estimate=pl.CostEstimate(flops=0, bytes_accessed=6 * MIB, transcendentals=0),
    )(where, chunks, *before)


def exchange(values, axes):
    return lax.all_to_all(values, axes, split_axis=0, concat_axis=0, tiled=True)


def shifted(pieces, axes):
    n = len(pieces)
    return [pieces[0]] + [
        lax.ppermute(pieces[k], axes, [(i, (i + k) % n) for i in range(n)]) for k in range(1, n)
    ]


def swap(value, axis):
    return lax.ppermute(value, axis, [(0, 1), (1, 0)])


def layer(latents, cotangent, w_row, w_col, keep_heads):
    where = jnp.concatenate(
        [jnp.stack([lax.axis_index(name) for name in AXES]), keep_heads.reshape(-1)]
    ).astype(jnp.int32)
    rows_in = exchange(latents.reshape(16, 2, 16, D), COL)
    grad_pieces = tile_to_lines(where, cotangent)
    grad_parts = shifted(grad_pieces, "y")
    grad_pass = pass_low(where, *grad_parts)
    grad_pass = swap(grad_pass, "zl")
    mid_send, saved_row = row_forward(where, rows_in, w_row)
    mid_lines = exchange(mid_send, BOTH)
    probs_row, turned_row = row_prepare(saved_row)
    grad_send, saved_col = col_grad(
        where, mid_lines, w_col, *grad_parts, grad_pass
    )
    grad_rows = exchange(grad_send, BOTH)
    send_col, turned_col = col_weights(where, saved_col)
    got_col = swap(send_col, "c")
    keep_col = kept_gradients(where, turned_col, saved_col)
    quarters = pair_sum(where, keep_col, got_col)
    quarters = shifted(quarters, "x")
    send_row, right_row = row_backward(where, grad_rows, saved_row, turned_row, probs_row, w_row)
    got_row = swap(send_row, "c")
    keep_row = kept_gradients(where, turned_row, right_row)
    merged = merge(keep_row, got_row, *quarters)
    both = exchange(merged, CHIPS)
    totals = spread(both)
    chunks = exchange(totals, CHIPS)
    gin_pieces = row_input_gradient(where, rows_in, right_row, w_row)
    gin_parts = shifted(gin_pieces, ("zh", "x"))
    gin_core = pass_core(where, *gin_parts)
    gin_core = swap(gin_core, "c")
    grad_latents = join(where, *gin_parts, gin_core).reshape(32, 16, D)
    out_pieces = col_output(where, saved_col, w_col)
    out_parts = shifted(out_pieces, ROW)
    output = lines_to_tile(where, *out_parts)
    other = swap(chunks, "c")
    halves_done = widen(where, chunks, 0)
    grad_row, grad_col = widen(where, other, 1, *halves_done)
    return (output, grad_latents, grad_row.reshape(4, D, D), grad_col.reshape(4, D, D))


def solution(mesh):
    fine = Mesh(mesh.devices.reshape(4, 2, 2, 4, 2), AXES)
    tile = P(ROW, COL, None)
    return jax.shard_map(
        layer,
        mesh=fine,
        in_specs=(tile, tile, P(), P(), P()),
        out_specs=(tile, tile, P(), P()),
        check_vma=False,
    )
```

```python
import functools

import jax
import jax.numpy as jnp
from jax import lax
from jax.experimental import pallas as pl
from jax.experimental.pallas import tpu as pltpu
from jax.sharding import Mesh, PartitionSpec as P


HEADS = 8
HEAD = 64
D = 512
PAIR = 128
N_PAIR = D // PAIR
LINE = 256
TOK = 512
N_ROW = 8
N_COL = 16
N_DEV = N_ROW * N_COL
EPSILON = 1e-06
SCALE = HEAD ** (-0.5)

F32 = jnp.float32
BF16 = jnp.bfloat16

AXES = ("y", "zl", "zh", "x", "c")
ROW = ("y", "zl")
COL = ("zh", "x", "c")
BOTH = COL + ROW
CHIPS = ("y", "zl", "zh", "x")


def dot(left, right):
    return lax.dot_general(left, right, (((1,), (0,)), ((), ())), preferred_element_type=F32)


def dot_nt(left, right):
    return lax.dot_general(left, right, (((1,), (1,)), ((), ())), preferred_element_type=F32)


def stack_halves(value):
    lane = lax.broadcasted_iota(jnp.int32, value.shape, 1)
    zero = jnp.zeros_like(value)
    low, high = jnp.where(lane < HEAD, value, zero), jnp.where(lane >= HEAD, value, zero)
    return jnp.concatenate([low, high], axis=0)


def pick_halves(value):
    low, high = value[:LINE], value[LINE:]
    lane = lax.broadcasted_iota(jnp.int32, low.shape, 1)
    return jnp.where(lane < HEAD, low, high)


def turn_halves(value):
    return jnp.concatenate([value[:LINE].T, value[LINE:].T], axis=0)


def gain_row(info_ref, block, first, count):
    head = lax.broadcasted_iota(jnp.int32, (1, count * HEAD), 1) // HEAD
    gain = jnp.zeros((1, count * HEAD), F32)
    for i in range(count):
        gain = jnp.where(head == i, info_ref[5 + block * HEADS + first + i].astype(F32), gain)
    return gain


def inverse_rms(values_f):
    return lax.rsqrt(jnp.mean(values_f * values_f, axis=-1, keepdims=True) + EPSILON)


def softmax(q_pair, k_pair):
    scores = dot_nt(stack_halves(q_pair), k_pair)
    peak = jnp.max(scores, axis=-1, keepdims=True)
    grown = jnp.exp(scores - peak)
    return grown * (1.0 / jnp.sum(grown, axis=-1, keepdims=True))


def picked(rows):
    return jnp.where(rows == lax.broadcasted_iota(jnp.int32, (TOK, TOK), 1), 1.0, 0.0).astype(BF16)


def chunk_row(grid_col, grid_row, row_local, col_local):
    return ((grid_col * 8 + grid_row) * 2 + row_local) * 2 + col_local


def positions():
    return lax.broadcasted_iota(jnp.int32, (TOK, 1), 0)


def chunk_parts():
    row = positions()
    return row // 32, (row // 4) % 8, (row // 2) % 2, row % 2


def row_tokens_of_chunks():
    token = positions()
    return picked(chunk_row((token // 16) % 16, token % 8, token // 256, (token // 8) % 2))


def chunks_of_row_tokens():
    grid_col, grid_row, row_local, col_local = chunk_parts()
    return picked(row_local * 256 + grid_col * 16 + col_local * 8 + grid_row)


def col_tokens_of_chunks():
    token = positions()
    return picked(chunk_row(token % 16, (token // 16) % 8, (token // 128) % 2, token // 256))


def chunks_of_col_tokens():
    grid_col, grid_row, row_local, col_local = chunk_parts()
    return picked(col_local * 256 + row_local * 128 + grid_row * 16 + grid_col)


def copies_of(source, target, sems, count):
    return [pltpu.make_async_copy(source.at[i], target.at[i], sems.at[i]) for i in range(count)]


def start_all(copies):
    for copy in copies:
        copy.start()


def wait_all(copies):
    for copy in copies:
        copy.wait()


def project(normed, qkv_ref, w_s, copies):
    copies[0].wait()
    qkv_ref[0] = (dot(normed, w_s[0]).astype(BF16).astype(F32) * SCALE).astype(BF16)
    copies[1].wait()
    qkv_ref[1] = dot(normed, w_s[1]).astype(BF16)
    copies[2].wait()
    qkv_ref[2] = dot(normed, w_s[2]).astype(BF16)


def each_pair(visit, per_step=2):
    def step(index, carry):
        line = index // (N_PAIR // per_step)
        first = lax.rem(index, N_PAIR // per_step) * per_step
        rows = pl.ds(pl.multiple_of(line * LINE, LINE), LINE)
        for offset in range(per_step):
            pair = first + offset
            lanes = pl.ds(pl.multiple_of(pair * PAIR, PAIR), PAIR)
            visit(rows, lanes, line * N_PAIR + pair, pair)
        return carry

    lax.fori_loop(0, 2 * N_PAIR // per_step, step, 0)


def row_forward_kernel(
    where_ref, x_ref, w_ref, mid_ref, saved_ref,
    order_s, mid_s, qkv_s, left_s, w_s, w_sem, mid_sem, qkv_sem, left_sem,
):
    weights = copies_of(w_ref, w_s, w_sem, 4)
    start_all(weights)
    saved = copies_of(qkv_s, saved_ref, qkv_sem, 3)
    lefts = copies_of(left_s, saved_ref.at[3:5], left_sem, 2)
    order_s[...] = chunks_of_row_tokens()
    for rr in range(2):
        u = x_ref[:, rr].astype(F32).reshape(LINE, D)
        left_s[0, rr * LINE : (rr + 1) * LINE, :] = (u * inverse_rms(u)).astype(BF16)
    project(left_s[0], qkv_s, w_s, weights)
    lefts[0].start()
    start_all(saved)

    def visit(rows, lanes, at, pair):
        probs = softmax(qkv_s[0, rows, lanes], qkv_s[1, rows, lanes]).astype(BF16)
        mixed = pick_halves(dot(probs, qkv_s[2, rows, lanes]))
        left_s[1, rows, lanes] = (mixed * gain_row(where_ref, 0, pair * 2, 2)).astype(BF16)

    each_pair(visit, 4)
    lefts[1].start()
    weights[3].wait()
    added = dot(left_s[1], w_s[3])
    mids = []
    for rr in range(2):
        u = x_ref[:, rr].astype(F32).reshape(LINE, D)
        mids.append((u + added[rr * LINE : (rr + 1) * LINE]).astype(BF16))
    mid = jnp.concatenate(mids, axis=0)
    sends = []
    for part in range(4):
        rows = slice(part * 32, (part + 1) * 32)
        turned = dot(order_s[part * 128 : (part + 1) * 128, :], mid)
        mid_s[rows] = turned.astype(BF16).reshape(32, 4, D)
        sends.append(pltpu.make_async_copy(mid_s.at[rows], mid_ref.at[rows], mid_sem.at[part]))
        sends[-1].start()
    wait_all(saved + lefts + sends)


def row_prepare_kernel(saved_ref, probs_ref, turned_ref):
    def visit(rows, lanes, at, pair):
        probs = softmax(saved_ref[0, rows, lanes], saved_ref[1, rows, lanes])
        probs_ref[at] = probs.astype(BF16)

    each_pair(visit)
    for which in range(2):
        turned_ref[which] = saved_ref[3 + which].T


def attention_backward(rows, lanes, qkv, da_ref, probs, right_ref):
    q_pair, k_pair, v_pair = (qkv[i, rows, lanes] for i in range(3))
    da_pair = da_ref[rows, lanes]
    low = probs.astype(BF16)
    probs = probs.astype(F32)
    grad_probs = dot_nt(stack_halves(da_pair), v_pair)
    total = jnp.sum(probs * grad_probs, axis=-1, keepdims=True)
    grads = (probs * (grad_probs - total)).astype(BF16)
    right_ref[0, rows, lanes] = (pick_halves(dot(grads, k_pair)) * SCALE).astype(BF16)
    right_ref[1, rows, lanes] = pick_halves(dot(turn_halves(grads), q_pair)).astype(BF16)
    right_ref[2, rows, lanes] = pick_halves(dot(turn_halves(low), da_pair)).astype(BF16)
    return low


def input_gradient(u, right_ref, w_s, rows):
    inv = inverse_rms(u)
    dn = (
        dot_nt(right_ref[0, rows, :], w_s[0])
        + dot_nt(right_ref[1, rows, :], w_s[1])
        + dot_nt(right_ref[2, rows, :], w_s[2])
    )
    mean = jnp.mean(dn * u, axis=-1, keepdims=True)
    return right_ref[3, rows, :].astype(F32) + inv * dn - u * (inv * inv * inv * mean)


def weight_gradients(side, turned, right_ref, target):
    for j in range(2):
        which = side * 2 + j
        target[j] = dot(turned[which // 3], right_ref[which]).astype(BF16)


def row_backward_kernel(
    where_ref, g_ref, qkv_ref, turned_ref, probs_ref, w_ref,
    send_ref, right_ref,
    da_s, wo_s, qkv_s, turned_s, probs_s, send_s, right_s,
    wo_sem, qkv_sem, turned_sem, probs_sem, half_sem, right_sem,
):
    weight = pltpu.make_async_copy(w_ref.at[3], wo_s, wo_sem)
    weight.start()
    saved = copies_of(qkv_ref, qkv_s, qkv_sem, 3)
    start_all(saved)
    probs = [
        pltpu.make_async_copy(
            probs_ref.at[i * 2 : (i + 1) * 2], probs_s.at[i * 2 : (i + 1) * 2], probs_sem.at[i]
        )
        for i in range(4)
    ]
    start_all(probs)
    turned = copies_of(turned_ref, turned_s, turned_sem, 2)
    start_all(turned)
    right_s[3] = dot(row_tokens_of_chunks(), g_ref[...].reshape(TOK, D)).astype(BF16)
    weight.wait()
    gain = gain_row(where_ref, 0, 0, HEADS)
    da_s[...] = (dot_nt(right_s[3], wo_s[...]) * gain).astype(BF16)
    wait_all(saved + probs)

    def visit(rows, lanes, at, pair):
        attention_backward(rows, lanes, qkv_s, da_s, probs_s[at], right_s)

    each_pair(visit, 4)
    rights = copies_of(right_s, right_ref, right_sem, 4)
    start_all(rights)
    wait_all(turned)
    core = where_ref[4]
    weight_gradients(1 - core, turned_s, right_s, send_s)
    sent = pltpu.make_async_copy(send_s, send_ref, half_sem)
    sent.start()
    wait_all(rights + [sent])


def kept_gradients_kernel(where_ref, turned_ref, right_ref, keep_ref, turned_s, right_s, turned_sem, right_sem):
    core = where_ref[4]
    turned = copies_of(turned_ref, turned_s, turned_sem, 2)
    rights = copies_of(right_ref.at[pl.ds(core * 2, 2)], right_s, right_sem, 2)
    start_all(turned + rights)
    wait_all(turned + rights)
    for j in range(2):
        keep_ref[j] = dot(turned_s[(core * 2 + j) // 3], right_s[j]).astype(BF16)


def row_input_gradient_kernel(where_ref, x_ref, right_ref, w_ref, *refs):
    outs, w_s, right_s, gin_s, w_sem, right_sem = refs[:8], *refs[8:]
    weights = copies_of(w_ref, w_s, w_sem, 3)
    rights = copies_of(right_ref, right_s, right_sem, 4)
    start_all([copy for pair in zip(weights, rights) for copy in pair] + rights[3:])
    wait_all(weights + rights)
    for rr in range(2):
        rows = slice(rr * LINE, (rr + 1) * LINE)
        u = x_ref[:, rr].astype(F32).reshape(LINE, D)
        grad_in = input_gradient(u, right_s, w_s, rows)
        gin_s[:, :, rr] = grad_in.astype(BF16).reshape(8, 2, 16, D)
    chip = where_ref[2] * 4 + where_ref[3]
    for shift in range(8):
        outs[shift][...] = gin_s[lax.rem(chip + shift, 8)]


def col_kernel(where_ref, m_ref, w_ref, *refs):
    parts, got_ref, refs = refs[:4], refs[4], refs[5:]
    gmid_ref, saved_ref = refs[:2]
    order_s, u_s, ulow_s, left_s, right_s, qkv_s, da_s, w_s, parts_s, got_s = refs[2:12]
    w_sem, left_sem, right_sem, u_sem, parts_sem, got_sem = refs[12:]
    mine = where_ref[1]
    pieces = [
        pltpu.make_async_copy(parts[i].at[mine], parts_s.at[i], parts_sem.at[i]) for i in range(4)
    ]
    pieces.append(pltpu.make_async_copy(got_ref, got_s, got_sem))
    start_all(pieces)
    weights = copies_of(w_ref, w_s, w_sem, 4)
    for i in (3, 0, 1, 2):
        weights[i].start()
    rights = copies_of(right_s, saved_ref, right_sem, 4)
    lefts = copies_of(left_s, saved_ref.at[4:6], left_sem, 2)
    order_s[...] = chunks_of_col_tokens()
    u_s[...] = dot(col_tokens_of_chunks(), m_ref[...].reshape(TOK, D))
    u = u_s[...]
    ulow_s[...] = u.astype(BF16)
    kept_u = pltpu.make_async_copy(ulow_s, saved_ref.at[6], u_sem)
    kept_u.start()
    left_s[0] = (u * inverse_rms(u)).astype(BF16)
    lefts[0].start()
    wait_all(pieces)
    for shift in range(4):
        source = lax.rem(where_ref[0] + (4 - shift), 4) * 2
        for grid_row, piece in ((source + mine, parts_s.at[shift]), (source + (1 - mine), got_s.at[shift])):
            for cc in range(2):
                for rr in range(2):
                    at = pl.multiple_of(grid_row * 16 + (cc * LINE + rr * 128), 16)
                    right_s[3, pl.ds(at, 16), :] = piece[cc, rr * 16 : (rr + 1) * 16, :]
    rights[3].start()
    weights[3].wait()
    gain = gain_row(where_ref, 1, 0, HEADS)
    da_s[...] = (dot_nt(right_s[3], w_s[3]) * gain).astype(BF16)
    project(left_s[0], qkv_s, w_s, weights)

    def visit(rows, lanes, at, pair):
        probs = softmax(qkv_s[0, rows, lanes], qkv_s[1, rows, lanes])
        low = attention_backward(rows, lanes, qkv_s, da_s, probs, right_s)
        mixed = pick_halves(dot(low, qkv_s[2, rows, lanes]))
        left_s[1, rows, lanes] = (mixed * gain_row(where_ref, 1, pair * 2, 2)).astype(BF16)

    each_pair(visit, 4)
    lefts[1].start()
    start_all(rights[:3])
    grads = [
        input_gradient(u_s[rows, :], right_s, w_s, rows).astype(BF16)
        for rows in (slice(0, LINE), slice(LINE, TOK))
    ]
    gmid_ref[...] = dot(order_s[...], jnp.concatenate(grads, axis=0)).astype(BF16).reshape(N_DEV, 4, D)
    wait_all(lefts + rights + [kept_u])


def col_weights_kernel(where_ref, saved_ref, send_ref, turned_ref, *refs):
    left_s, right_s, turned_s, left_sem, right_sem, turned_sem = refs
    side = 1 - where_ref[4]
    lefts = copies_of(saved_ref.at[4:6], left_s, left_sem, 2)
    rights = copies_of(saved_ref.at[pl.ds(side * 2, 2)], right_s, right_sem, 2)
    start_all(lefts + rights)
    turned = copies_of(turned_s, turned_ref, turned_sem, 2)
    for which in range(2):
        lefts[which].wait()
        turned_s[which] = left_s[which].T
        turned[which].start()
    wait_all(rights)
    for j in range(2):
        send_ref[j] = dot(turned_s[(side * 2 + j) // 3], right_s[j]).astype(BF16)
    wait_all(turned)


def col_output_kernel(where_ref, saved_ref, w_ref, *refs):
    outs, (att_s, ulow_s, wo_s, out_s, sem) = refs[:8], refs[8:]
    copies = [
        pltpu.make_async_copy(saved_ref.at[5], att_s, sem.at[0]),
        pltpu.make_async_copy(w_ref.at[3], wo_s, sem.at[1]),
        pltpu.make_async_copy(saved_ref.at[6], ulow_s, sem.at[2]),
    ]
    start_all(copies)
    wait_all(copies)
    out_s[...] = (ulow_s[...].astype(F32) + dot(att_s[...], wo_s[...])).astype(BF16)
    me = where_ref[0] * 2 + where_ref[1]
    for shift in range(8):
        start = lax.rem(me + shift, 8) * 16
        for cc in range(2):
            for rr in range(2):
                at = pl.multiple_of(start + (cc * LINE + rr * 128), 16)
                outs[shift][cc, rr * 16 : (rr + 1) * 16, :] = out_s[pl.ds(at, 16), :]


def tile_to_lines_kernel(where_ref, tile_ref, *refs):
    outs, mix_s = refs[:4], refs[4]
    tile = tile_ref[...].astype(F32).reshape(TOK, D)
    for group in range(4):
        lanes = slice(group * 128, (group + 1) * 128)
        mix_s[group] = tile[:, lanes]
        for shift in range(4):
            for low in range(2):
                peer = lax.rem(where_ref[0] + shift, 4) * 2 + low
                for cc in range(2):
                    for rr in range(2):
                        piece = mix_s[group, pl.ds(peer + (rr * 16 + cc * 8), 16, stride=32), :]
                        outs[shift][low, cc, rr * 16 : (rr + 1) * 16, lanes] = piece.astype(BF16)


def pass_low_kernel(where_ref, *refs):
    parts, pass_ref = refs[:4], refs[4]
    for shift in range(4):
        pass_ref[shift] = parts[shift][1 - where_ref[1]]


def lines_to_tile_kernel(where_ref, *refs):
    parts, tile_ref, mix_s = refs[:8], refs[8], refs[9]
    me = where_ref[0] * 2 + where_ref[1]
    for group in range(4):
        lanes = slice(group * 128, (group + 1) * 128)
        for shift in range(8):
            peer = lax.rem(me + (8 - shift), 8)
            for cc in range(2):
                for rr in range(2):
                    piece = parts[shift][cc, rr * 16 : (rr + 1) * 16, lanes].astype(F32)
                    mix_s[group, pl.ds(peer + (rr * 16 + cc * 8), 16, stride=32), :] = piece
        tile_ref[:, :, lanes] = mix_s[group].astype(BF16).reshape(32, 16, 128)


def pass_core_kernel(where_ref, *refs):
    parts, pass_ref = refs[:8], refs[8]
    for shift in range(8):
        pass_ref[shift] = parts[shift][1 - where_ref[4]]


def join_kernel(where_ref, *refs):
    parts, passed_ref, tile_ref = refs[:8], refs[8], refs[9]
    chip, core = where_ref[2] * 4 + where_ref[3], where_ref[4]
    for shift in range(8):
        source = lax.rem(chip + (8 - shift), 8)
        tile_ref[source, core] = parts[shift][core]
        tile_ref[source, 1 - core] = passed_ref[shift]


def pair_sum_kernel(where_ref, keep_ref, got_ref, *refs):
    outs, sum_s = refs[:4], refs[4]
    total = keep_ref[...].astype(F32) + got_ref[...].astype(F32)
    sum_s[...] = total.astype(BF16).reshape(4, 256, D)
    for shift in range(4):
        outs[shift][...] = sum_s[lax.rem(where_ref[3] + shift, 4)]


def merge_kernel(keep_ref, got_ref, *refs):
    quarters, both_ref = refs[:4], refs[4]
    total = keep_ref[...].astype(F32) + got_ref[...].astype(F32)
    rows = total.astype(BF16).reshape(64, 16, D)
    quarter = quarters[0][...].astype(F32)
    for i in range(1, 4):
        quarter = quarter + quarters[i][...].astype(F32)
    quarter = quarter.astype(BF16).reshape(16, 16, D)
    for group in range(4):
        lanes = slice(group * 128, (group + 1) * 128)
        both_ref[:, group * 16 : (group + 1) * 16, :] = rows[:, :, lanes]
        for block in range(16):
            both_ref[block * 4 + group, 64:80, :] = quarter[block, :, lanes]


def chip_sum(parts_ref, rows, first, step):
    total = parts_ref[first, rows, :].astype(F32)
    for chip in range(first + step, 64, step):
        total = total + parts_ref[chip, rows, :].astype(F32)
    return total.astype(BF16)


def spread_kernel(both_ref, spread_ref):
    row_sum = chip_sum(both_ref, slice(0, 64), 0, 1)
    spread_ref[:, 0:64, :] = jnp.broadcast_to(row_sum[None], (64, 64, 128))
    for quarter in range(4):
        part = chip_sum(both_ref, slice(64, 80), quarter, 4)
        first = 64 + quarter * 16
        spread_ref[:, first : first + 16, :] = jnp.broadcast_to(part[None], (64, 16, 128))


def widen_kernel(side, where_ref, chunks_ref, *refs):
    row_ref, col_ref, row_s, col_s, row_sem, col_sem = refs[-6:]
    half = where_ref[4] if side == 0 else 1 - where_ref[4]
    copies = []
    for part in range(4):
        chunks = slice(part * 16, (part + 1) * 16)
        for group in range(4):
            lanes = slice(group * 128, (group + 1) * 128)
            piece = chunks_ref[chunks, group * 16 : (group + 1) * 16, :].astype(F32)
            row_s[part, :, lanes] = piece.reshape(256, 128)
        rows = pl.ds(part * 256, 256)
        copies.append(
            pltpu.make_async_copy(row_s.at[part], row_ref.at[half, rows], row_sem.at[part])
        )
        copies[-1].start()
    for quarter in range(4):
        first = 64 + quarter * 16
        for block in range(16):
            for group in range(4):
                col_s[quarter, block * 16 : (block + 1) * 16, group * 128 : (group + 1) * 128] = (
                    chunks_ref[block * 4 + group, first : first + 16, :].astype(F32)
                )
        copies.append(
            pltpu.make_async_copy(col_s.at[quarter], col_ref.at[half, quarter], col_sem.at[quarter])
        )
        copies[-1].start()
    wait_all(copies)


MIB = 1 << 20
SMEM = pl.BlockSpec(memory_space=pltpu.SMEM)
VMEM = pl.BlockSpec(memory_space=pltpu.VMEM)
HBM = pl.BlockSpec(memory_space=pltpu.HBM)


SPACE = {"s": SMEM, "v": VMEM, "h": HBM}


def call(kernel, ins, out_kinds, outs, scratch, flops, moved, grant=16):
    spaces = tuple(SPACE[kind] for kind in out_kinds)
    return pl.pallas_call(
        kernel,
        in_specs=[SPACE[kind] for kind in ins],
        out_specs=spaces if isinstance(outs, tuple) else spaces[0],
        out_shape=outs,
        scratch_shapes=scratch,
        compiler_params=pltpu.CompilerParams(vmem_limit_bytes=grant * MIB),
        cost_estimate=pl.CostEstimate(flops=flops, bytes_accessed=moved, transcendentals=0),
    )


def shape(*dims, dtype=BF16):
    return jax.ShapeDtypeStruct(dims, dtype)


MATMUL = 2 * TOK * D * D
ATTEND = 2 * 16 * LINE * LINE * HEAD
MIX_TILE = pltpu.VMEM((4, TOK, 128), F32)
DMA = pltpu.SemaphoreType.DMA
WEIGHTS = [pltpu.VMEM((4, D, D), BF16), DMA((4,))]
WEIGHT = [pltpu.VMEM((D, D), BF16), DMA]
LINES = shape(2, 32, D)
PIECE = shape(2, 2, 32, D)
PASS = shape(4, 2, 32, D)
QUARTER = shape(256, D)
HALF = shape(2, D, D)
HALF_S = pltpu.VMEM((2, D, D), BF16)


def token_scratch(*lead, dtype=BF16):
    return pltpu.VMEM((*lead, TOK, D), dtype)


row_forward = call(
    row_forward_kernel,
    "svh",
    "hh",
    (shape(N_DEV, 4, D), shape(5, TOK, D)),
    [
        token_scratch(), pltpu.VMEM((N_DEV, 4, D), BF16), token_scratch(3), token_scratch(2), *WEIGHTS,
        DMA((4,)), DMA((3,)), DMA((2,)),
    ],
    4 * MATMUL + 2 * ATTEND,
    6 * MIB,
    grant=50,
)
row_prepare = call(
    row_prepare_kernel, "v", "vv", (shape(8, TOK, LINE), shape(2, D, TOK)), [], ATTEND, 8 * MIB
)
row_backward = call(
    row_backward_kernel,
    "svhhhh",
    "hh",
    (HALF, shape(4, TOK, D)),
    [
        token_scratch(), pltpu.VMEM((D, D), BF16), token_scratch(3),
        pltpu.VMEM((2, D, TOK), BF16), pltpu.VMEM((8, TOK, LINE), BF16), HALF_S,
        token_scratch(4), DMA, DMA((3,)), DMA((2,)), DMA((4,)), DMA, DMA((4,)),
    ],
    5 * MATMUL + 5 * ATTEND,
    12 * MIB,
    grant=50,
)
kept_gradients = call(
    kept_gradients_kernel,
    "shh",
    "v",
    HALF,
    [pltpu.VMEM((2, D, TOK), BF16), token_scratch(2), DMA((2,)), DMA((2,))],
    2 * MATMUL,
    3 * MIB,
    grant=50,
)
row_input_gradient = call(
    row_input_gradient_kernel,
    "svhh",
    "v" * 8,
    (shape(2, 2, 16, D),) * 8,
    [
        pltpu.VMEM((3, D, D), BF16), token_scratch(4), pltpu.VMEM((8, 2, 2, 16, D), BF16),
        DMA((3,)), DMA((4,)),
    ],
    3 * MATMUL,
    5 * MIB,
    grant=50,
)
col_grad = call(
    col_kernel,
    "svh" + "h" * 5,
    "vh",
    (shape(N_DEV, 4, D), shape(7, TOK, D)),
    [
        token_scratch(), token_scratch(dtype=F32), token_scratch(), token_scratch(2), token_scratch(4),
        token_scratch(3), token_scratch(), WEIGHTS[0], pltpu.VMEM((4, 2, 32, D), BF16),
        pltpu.VMEM((4, 2, 32, D), BF16), DMA((4,)), DMA((2,)), DMA((4,)), DMA, DMA((4,)), DMA,
    ],
    8 * MATMUL + 6 * ATTEND,
    8 * MIB,
    grant=50,
)
col_weights = call(
    col_weights_kernel,
    "sh",
    "vh",
    (HALF, shape(2, D, TOK)),
    [
        token_scratch(2), token_scratch(2), pltpu.VMEM((2, D, TOK), BF16),
        DMA((2,)), DMA((2,)), DMA((2,)),
    ],
    2 * MATMUL,
    6 * MIB,
    grant=50,
)
col_output = call(
    col_output_kernel,
    "shh",
    "v" * 8,
    (LINES,) * 8,
    [token_scratch(), token_scratch(), pltpu.VMEM((D, D), BF16), token_scratch(), DMA((3,))],
    MATMUL,
    3 * MIB,
    grant=52,
)
tile_to_lines = call(tile_to_lines_kernel, "sv", "v" * 4, (PIECE,) * 4, [MIX_TILE], 0, MIB)
pass_low = call(pass_low_kernel, "s" + "v" * 4, "v", PASS, [], 0, MIB)
lines_to_tile = call(lines_to_tile_kernel, "s" + "v" * 8, "v", shape(32, 16, D), [MIX_TILE], 0, MIB)
CORE_PASS = shape(8, 2, 16, D)
pass_core = call(pass_core_kernel, "s" + "v" * 8, "v", CORE_PASS, [], 0, MIB)
join = call(join_kernel, "s" + "v" * 9, "v", shape(8, 2, 2, 16, D), [], 0, MIB)
pair_sum = call(
    pair_sum_kernel, "svv", "v" * 4, (QUARTER,) * 4, [pltpu.VMEM((4, 256, D), BF16)], 0, 3 * MIB,
)
merge = call(merge_kernel, "v" * 6, "v", shape(64, 80, 128), [], 0, 4 * MIB, grant=16)
spread = call(spread_kernel, "v", "v", shape(64, 128, 128), [], 0, 3 * MIB, grant=52)


def widen(where, chunks, side, *before):
    return pl.pallas_call(
        functools.partial(widen_kernel, side),
        in_specs=[SMEM, VMEM] + [HBM] * len(before),
        out_specs=(HBM, HBM),
        out_shape=(shape(2, 1024, D, dtype=F32), shape(2, 4, 256, D, dtype=F32)),
        scratch_shapes=[
            pltpu.VMEM((4, 256, D), F32), pltpu.VMEM((4, 256, D), F32), DMA((4,)), DMA((4,)),
        ],
        input_output_aliases={2: 0, 3: 1} if before else {},
        name="widen",
        compiler_params=pltpu.CompilerParams(vmem_limit_bytes=16 * MIB),
        cost_estimate=pl.CostEstimate(flops=0, bytes_accessed=6 * MIB, transcendentals=0),
    )(where, chunks, *before)


def exchange(values, axes):
    return lax.all_to_all(values, axes, split_axis=0, concat_axis=0, tiled=True)


def shifted(pieces, axes):
    n = len(pieces)
    return [pieces[0]] + [
        lax.ppermute(pieces[k], axes, [(i, (i + k) % n) for i in range(n)]) for k in range(1, n)
    ]


def swap(value, axis):
    return lax.ppermute(value, axis, [(0, 1), (1, 0)])


def layer(latents, cotangent, w_row, w_col, keep_heads):
    where = jnp.concatenate(
        [jnp.stack([lax.axis_index(name) for name in AXES]), keep_heads.reshape(-1)]
    ).astype(jnp.int32)
    rows_in = exchange(latents.reshape(16, 2, 16, D), COL)
    grad_pieces = tile_to_lines(where, cotangent)
    grad_parts = shifted(grad_pieces, "y")
    grad_pass = pass_low(where, *grad_parts)
    grad_pass = swap(grad_pass, "zl")
    mid_send, saved_row = row_forward(where, rows_in, w_row)
    mid_lines = exchange(mid_send, BOTH)
    probs_row, turned_row = row_prepare(saved_row)
    grad_send, saved_col = col_grad(
        where, mid_lines, w_col, *grad_parts, grad_pass
    )
    grad_rows = exchange(grad_send, BOTH)
    send_col, turned_col = col_weights(where, saved_col)
    got_col = swap(send_col, "c")
    keep_col = kept_gradients(where, turned_col, saved_col)
    quarters = pair_sum(where, keep_col, got_col)
    quarters = shifted(quarters, "x")
    send_row, right_row = row_backward(where, grad_rows, saved_row, turned_row, probs_row, w_row)
    got_row = swap(send_row, "c")
    keep_row = kept_gradients(where, turned_row, right_row)
    merged = merge(keep_row, got_row, *quarters)
    both = exchange(merged, CHIPS)
    totals = spread(both)
    chunks = exchange(totals, CHIPS)
    gin_pieces = row_input_gradient(where, rows_in, right_row, w_row)
    gin_parts = shifted(gin_pieces, ("zh", "x"))
    gin_core = pass_core(where, *gin_parts)
    gin_core = swap(gin_core, "c")
    grad_latents = join(where, *gin_parts, gin_core).reshape(32, 16, D)
    out_pieces = col_output(where, saved_col, w_col)
    out_parts = shifted(out_pieces, ROW)
    output = lines_to_tile(where, *out_parts)
    other = swap(chunks, "c")
    halves_done = widen(where, chunks, 0)
    grad_row, grad_col = widen(where, other, 1, *halves_done)
    return (output, grad_latents, grad_row.reshape(4, D, D), grad_col.reshape(4, D, D))


def solution(mesh):
    fine = Mesh(mesh.devices.reshape(4, 2, 2, 4, 2), AXES)
    tile = P(ROW, COL, None)
    return jax.shard_map(
        layer,
        mesh=fine,
        in_specs=(tile, tile, P(), P(), P()),
        out_specs=(tile, tile, P(), P()),
        check_vma=False,
    )
```

```python
import functools

import jax
import jax.numpy as jnp
from jax import lax
from jax.experimental import pallas as pl
from jax.experimental.pallas import tpu as pltpu
from jax.sharding import Mesh, PartitionSpec as P


HEADS = 8
HEAD = 64
D = 512
PAIR = 128
N_PAIR = D // PAIR
LINE = 256
TOK = 512
N_ROW = 8
N_COL = 16
N_DEV = N_ROW * N_COL
EPSILON = 1e-06
SCALE = HEAD ** (-0.5)

F32 = jnp.float32
BF16 = jnp.bfloat16

AXES = ("y", "zl", "zh", "x", "c")
ROW = ("y", "zl")
COL = ("zh", "x", "c")
BOTH = COL + ROW
CHIPS = ("y", "zl", "zh", "x")


def dot(left, right):
    return lax.dot_general(left, right, (((1,), (0,)), ((), ())), preferred_element_type=F32)


def dot_nt(left, right):
    return lax.dot_general(left, right, (((1,), (1,)), ((), ())), preferred_element_type=F32)


def stack_halves(value):
    lane = lax.broadcasted_iota(jnp.int32, value.shape, 1)
    zero = jnp.zeros_like(value)
    low, high = jnp.where(lane < HEAD, value, zero), jnp.where(lane >= HEAD, value, zero)
    return jnp.concatenate([low, high], axis=0)


def pick_halves(value):
    low, high = value[:LINE], value[LINE:]
    lane = lax.broadcasted_iota(jnp.int32, low.shape, 1)
    return jnp.where(lane < HEAD, low, high)


def turn_halves(value):
    return jnp.concatenate([value[:LINE].T, value[LINE:].T], axis=0)


def gain_row(info_ref, block, first, count):
    head = lax.broadcasted_iota(jnp.int32, (1, count * HEAD), 1) // HEAD
    gain = jnp.zeros((1, count * HEAD), F32)
    for i in range(count):
        gain = jnp.where(head == i, info_ref[5 + block * HEADS + first + i].astype(F32), gain)
    return gain


def inverse_rms(values_f):
    return lax.rsqrt(jnp.mean(values_f * values_f, axis=-1, keepdims=True) + EPSILON)


def softmax(q_pair, k_pair):
    scores = dot_nt(stack_halves(q_pair), k_pair)
    peak = jnp.max(scores, axis=-1, keepdims=True)
    grown = jnp.exp(scores - peak)
    return grown * (1.0 / jnp.sum(grown, axis=-1, keepdims=True))


def picked(rows):
    return jnp.where(rows == lax.broadcasted_iota(jnp.int32, (TOK, TOK), 1), 1.0, 0.0).astype(BF16)


def chunk_row(grid_col, grid_row, row_local, col_local):
    return ((grid_col * 8 + grid_row) * 2 + row_local) * 2 + col_local


def positions():
    return lax.broadcasted_iota(jnp.int32, (TOK, 1), 0)


def chunk_parts():
    row = positions()
    return row // 32, (row // 4) % 8, (row // 2) % 2, row % 2


def row_tokens_of_chunks():
    token = positions()
    return picked(chunk_row((token // 16) % 16, token % 8, token // 256, (token // 8) % 2))


def chunks_of_row_tokens():
    grid_col, grid_row, row_local, col_local = chunk_parts()
    return picked(row_local * 256 + grid_col * 16 + col_local * 8 + grid_row)


def col_tokens_of_chunks():
    token = positions()
    return picked(chunk_row(token % 16, (token // 16) % 8, (token // 128) % 2, token // 256))


def chunks_of_col_tokens():
    grid_col, grid_row, row_local, col_local = chunk_parts()
    return picked(col_local * 256 + row_local * 128 + grid_row * 16 + grid_col)


def copies_of(source, target, sems, count):
    return [pltpu.make_async_copy(source.at[i], target.at[i], sems.at[i]) for i in range(count)]


def start_all(copies):
    for copy in copies:
        copy.start()


def wait_all(copies):
    for copy in copies:
        copy.wait()


def project(normed, qkv_ref, w_ref):
    qkv_ref[0] = (dot(normed, w_ref[0]).astype(BF16).astype(F32) * SCALE).astype(BF16)
    qkv_ref[1] = dot(normed, w_ref[1]).astype(BF16)
    qkv_ref[2] = dot(normed, w_ref[2]).astype(BF16)


def each_pair(visit, per_step=2, before=None):
    def step(index, carry):
        line = index // (N_PAIR // per_step)
        first = lax.rem(index, N_PAIR // per_step) * per_step
        if before is not None:
            before(line)
        rows = pl.ds(pl.multiple_of(line * LINE, LINE), LINE)
        for offset in range(per_step):
            pair = first + offset
            lanes = pl.ds(pl.multiple_of(pair * PAIR, PAIR), PAIR)
            visit(rows, lanes, line * N_PAIR + pair, pair)
        return carry

    lax.fori_loop(0, 2 * N_PAIR // per_step, step, 0)


def row_forward_kernel(
    where_ref, x_ref, w_ref, mid_ref, saved_ref,
    order_s, mid_s, qkv_s, left_s, mid_sem, qkv_sem, left_sem,
):
    saved = copies_of(qkv_s, saved_ref, qkv_sem, 3)
    lefts = copies_of(left_s, saved_ref.at[3:5], left_sem, 2)
    order_s[...] = chunks_of_row_tokens()
    for rr in range(2):
        u = x_ref[:, rr].astype(F32).reshape(LINE, D)
        left_s[0, rr * LINE : (rr + 1) * LINE, :] = (u * inverse_rms(u)).astype(BF16)
    project(left_s[0], qkv_s, w_ref)
    lefts[0].start()
    start_all(saved)

    def visit(rows, lanes, at, pair):
        probs = softmax(qkv_s[0, rows, lanes], qkv_s[1, rows, lanes]).astype(BF16)
        mixed = pick_halves(dot(probs, qkv_s[2, rows, lanes]))
        left_s[1, rows, lanes] = (mixed * gain_row(where_ref, 0, pair * 2, 2)).astype(BF16)

    each_pair(visit, 4)
    lefts[1].start()
    added = dot(left_s[1], w_ref[3])
    mids = []
    for rr in range(2):
        u = x_ref[:, rr].astype(F32).reshape(LINE, D)
        mids.append((u + added[rr * LINE : (rr + 1) * LINE]).astype(BF16))
    mid = jnp.concatenate(mids, axis=0)
    sends = []
    for part in range(4):
        rows = slice(part * 32, (part + 1) * 32)
        turned = dot(order_s[part * 128 : (part + 1) * 128, :], mid)
        mid_s[rows] = turned.astype(BF16).reshape(32, 4, D)
        sends.append(pltpu.make_async_copy(mid_s.at[rows], mid_ref.at[rows], mid_sem.at[part]))
        sends[-1].start()
    wait_all(saved + lefts + sends)


def row_prepare_kernel(saved_ref, probs_ref, turned_ref):
    def visit(rows, lanes, at, pair):
        probs = softmax(saved_ref[0, rows, lanes], saved_ref[1, rows, lanes])
        probs_ref[at] = probs.astype(BF16)

    each_pair(visit)
    for which in range(2):
        turned_ref[which] = saved_ref[3 + which].T


def attention_backward(rows, lanes, qkv, da_ref, probs, right_ref):
    q_pair, k_pair, v_pair = (qkv[i, rows, lanes] for i in range(3))
    da_pair = da_ref[rows, lanes]
    low = probs.astype(BF16)
    probs = probs.astype(F32)
    grad_probs = dot_nt(stack_halves(da_pair), v_pair)
    total = jnp.sum(probs * grad_probs, axis=-1, keepdims=True)
    grads = (probs * (grad_probs - total)).astype(BF16)
    right_ref[0, rows, lanes] = (pick_halves(dot(grads, k_pair)) * SCALE).astype(BF16)
    right_ref[1, rows, lanes] = pick_halves(dot(turn_halves(grads), q_pair)).astype(BF16)
    right_ref[2, rows, lanes] = pick_halves(dot(turn_halves(low), da_pair)).astype(BF16)
    return low


def input_gradient(u, right_ref, w_s, rows):
    inv = inverse_rms(u)
    dn = (
        dot_nt(right_ref[0, rows, :], w_s[0])
        + dot_nt(right_ref[1, rows, :], w_s[1])
        + dot_nt(right_ref[2, rows, :], w_s[2])
    )
    mean = jnp.mean(dn * u, axis=-1, keepdims=True)
    return right_ref[3, rows, :].astype(F32) + inv * dn - u * (inv * inv * inv * mean)


def weight_gradients(side, turned, right_ref, target):
    for j in range(2):
        which = side * 2 + j
        target[j] = dot(turned[which // 3], right_ref[which]).astype(BF16)


def row_backward_kernel(
    where_ref, g_ref, qkv_ref, turned_ref, probs_ref, w_ref,
    send_ref, right_ref,
    da_s, wo_s, qkv_s, turned_s, probs_s, send_s, right_s,
    wo_sem, qkv_sem, turned_sem, probs_sem, half_sem, right_sem,
):
    weight = pltpu.make_async_copy(w_ref.at[3], wo_s, wo_sem)
    weight.start()
    saved = copies_of(qkv_ref, qkv_s, qkv_sem, 3)
    start_all(saved)
    turned = copies_of(turned_ref, turned_s, turned_sem, 2)

    def line_probs(line):
        pairs = pl.ds(line * N_PAIR, N_PAIR)
        return pltpu.make_async_copy(probs_ref.at[pairs], probs_s.at[pairs], probs_sem.at[line])

    line_probs(0).start()
    right_s[3] = dot(row_tokens_of_chunks(), g_ref[...].reshape(TOK, D)).astype(BF16)
    weight.wait()
    gain = gain_row(where_ref, 0, 0, HEADS)
    da_s[...] = (dot_nt(right_s[3], wo_s[...]) * gain).astype(BF16)
    line_probs(1).start()
    start_all(turned)
    wait_all(saved)

    def visit(rows, lanes, at, pair):
        attention_backward(rows, lanes, qkv_s, da_s, probs_s[at], right_s)

    each_pair(visit, 4, lambda line: line_probs(line).wait())
    rights = copies_of(right_s, right_ref, right_sem, 4)
    start_all(rights)
    wait_all(turned)
    core = where_ref[4]
    weight_gradients(1 - core, turned_s, right_s, send_s)
    sent = pltpu.make_async_copy(send_s, send_ref, half_sem)
    sent.start()
    wait_all(rights + [sent])


def kept_gradients_kernel(where_ref, turned_ref, right_ref, keep_ref, turned_s, right_s, turned_sem, right_sem):
    core = where_ref[4]
    turned = copies_of(turned_ref, turned_s, turned_sem, 2)
    rights = copies_of(right_ref.at[pl.ds(core * 2, 2)], right_s, right_sem, 2)
    start_all(turned + rights)
    wait_all(turned + rights)
    for j in range(2):
        keep_ref[j] = dot(turned_s[(core * 2 + j) // 3], right_s[j]).astype(BF16)


def row_input_gradient_kernel(where_ref, x_ref, right_ref, w_ref, *refs):
    outs, w_s, right_s, gin_s, w_sem, right_sem = refs[:8], *refs[8:]
    weights = copies_of(w_ref, w_s, w_sem, 3)
    rights = copies_of(right_ref, right_s, right_sem, 4)
    start_all([copy for pair in zip(weights, rights) for copy in pair] + rights[3:])
    wait_all(weights + rights)
    for rr in range(2):
        rows = slice(rr * LINE, (rr + 1) * LINE)
        u = x_ref[:, rr].astype(F32).reshape(LINE, D)
        grad_in = input_gradient(u, right_s, w_s, rows)
        gin_s[:, :, rr] = grad_in.astype(BF16).reshape(8, 2, 16, D)
    chip = where_ref[2] * 4 + where_ref[3]
    for shift in range(8):
        outs[shift][...] = gin_s[lax.rem(chip + shift, 8)]


def col_kernel(where_ref, m_ref, w_ref, *refs):
    parts, got_ref, refs = refs[:4], refs[4], refs[5:]
    gmid_ref, saved_ref = refs[:2]
    order_s, u_s, ulow_s, left_s, right_s, qkv_s, da_s = refs[2:9]
    left_sem, right_sem, u_sem = refs[9:]
    mine = where_ref[1]
    rights = copies_of(right_s, saved_ref, right_sem, 4)
    lefts = copies_of(left_s, saved_ref.at[4:6], left_sem, 2)
    order_s[...] = chunks_of_col_tokens()
    u_s[...] = dot(col_tokens_of_chunks(), m_ref[...].reshape(TOK, D))
    u = u_s[...]
    ulow_s[...] = u.astype(BF16)
    kept_u = pltpu.make_async_copy(ulow_s, saved_ref.at[6], u_sem)
    kept_u.start()
    left_s[0] = (u * inverse_rms(u)).astype(BF16)
    lefts[0].start()
    for shift in range(4):
        source = lax.rem(where_ref[0] + (4 - shift), 4) * 2
        for grid_row, piece in ((source + mine, parts[shift].at[mine]), (source + (1 - mine), got_ref.at[shift])):
            for cc in range(2):
                for rr in range(2):
                    at = pl.multiple_of(grid_row * 16 + (cc * LINE + rr * 128), 16)
                    right_s[3, pl.ds(at, 16), :] = piece[cc, rr * 16 : (rr + 1) * 16, :]
    rights[3].start()
    gain = gain_row(where_ref, 1, 0, HEADS)
    da_s[...] = (dot_nt(right_s[3], w_ref[3]) * gain).astype(BF16)
    project(left_s[0], qkv_s, w_ref)

    def visit(rows, lanes, at, pair):
        probs = softmax(qkv_s[0, rows, lanes], qkv_s[1, rows, lanes])
        low = attention_backward(rows, lanes, qkv_s, da_s, probs, right_s)
        mixed = pick_halves(dot(low, qkv_s[2, rows, lanes]))
        left_s[1, rows, lanes] = (mixed * gain_row(where_ref, 1, pair * 2, 2)).astype(BF16)

    each_pair(visit, 4)
    lefts[1].start()
    start_all(rights[:3])
    grads = [
        input_gradient(u_s[rows, :], right_s, w_ref, rows).astype(BF16)
        for rows in (slice(0, LINE), slice(LINE, TOK))
    ]
    gmid_ref[...] = dot(order_s[...], jnp.concatenate(grads, axis=0)).astype(BF16).reshape(N_DEV, 4, D)
    wait_all(lefts + rights + [kept_u])


def col_weights_kernel(where_ref, saved_ref, send_ref, turned_ref, *refs):
    left_s, right_s, turned_s, left_sem, right_sem, turned_sem = refs
    side = 1 - where_ref[4]
    lefts = copies_of(saved_ref.at[4:6], left_s, left_sem, 2)
    rights = copies_of(saved_ref.at[pl.ds(side * 2, 2)], right_s, right_sem, 2)
    start_all(lefts + rights)
    turned = copies_of(turned_s, turned_ref, turned_sem, 2)
    for which in range(2):
        lefts[which].wait()
        turned_s[which] = left_s[which].T
        turned[which].start()
    wait_all(rights)
    for j in range(2):
        send_ref[j] = dot(turned_s[(side * 2 + j) // 3], right_s[j]).astype(BF16)
    wait_all(turned)


def col_output_kernel(where_ref, saved_ref, w_ref, *refs):
    outs, (att_s, ulow_s, wo_s, out_s, sem) = refs[:8], refs[8:]
    copies = [
        pltpu.make_async_copy(saved_ref.at[5], att_s, sem.at[0]),
        pltpu.make_async_copy(w_ref.at[3], wo_s, sem.at[1]),
        pltpu.make_async_copy(saved_ref.at[6], ulow_s, sem.at[2]),
    ]
    start_all(copies)
    wait_all(copies)
    out_s[...] = (ulow_s[...].astype(F32) + dot(att_s[...], wo_s[...])).astype(BF16)
    me = where_ref[0] * 2 + where_ref[1]
    for shift in range(8):
        start = lax.rem(me + shift, 8) * 16
        for cc in range(2):
            for rr in range(2):
                at = pl.multiple_of(start + (cc * LINE + rr * 128), 16)
                outs[shift][cc, rr * 16 : (rr + 1) * 16, :] = out_s[pl.ds(at, 16), :]


def tile_to_lines_kernel(where_ref, tile_ref, *refs):
    outs, mix_s = refs[:4], refs[4]
    tile = tile_ref[...].astype(F32).reshape(TOK, D)
    for group in range(4):
        lanes = slice(group * 128, (group + 1) * 128)
        mix_s[group] = tile[:, lanes]
        for shift in range(4):
            for low in range(2):
                peer = lax.rem(where_ref[0] + shift, 4) * 2 + low
                for cc in range(2):
                    for rr in range(2):
                        piece = mix_s[group, pl.ds(peer + (rr * 16 + cc * 8), 16, stride=32), :]
                        outs[shift][low, cc, rr * 16 : (rr + 1) * 16, lanes] = piece.astype(BF16)


def pass_low_kernel(where_ref, *refs):
    parts, pass_ref = refs[:4], refs[4]
    for shift in range(4):
        pass_ref[shift] = parts[shift][1 - where_ref[1]]


def lines_to_tile_kernel(where_ref, *refs):
    parts, tile_ref, mix_s = refs[:8], refs[8], refs[9]
    me = where_ref[0] * 2 + where_ref[1]
    for group in range(4):
        lanes = slice(group * 128, (group + 1) * 128)
        for shift in range(8):
            peer = lax.rem(me + (8 - shift), 8)
            for cc in range(2):
                for rr in range(2):
                    piece = parts[shift][cc, rr * 16 : (rr + 1) * 16, lanes].astype(F32)
                    mix_s[group, pl.ds(peer + (rr * 16 + cc * 8), 16, stride=32), :] = piece
        tile_ref[:, :, lanes] = mix_s[group].astype(BF16).reshape(32, 16, 128)


def pass_core_kernel(where_ref, *refs):
    parts, pass_ref = refs[:8], refs[8]
    for shift in range(8):
        pass_ref[shift] = parts[shift][1 - where_ref[4]]


def join_kernel(where_ref, *refs):
    parts, passed_ref, tile_ref = refs[:8], refs[8], refs[9]
    chip, core = where_ref[2] * 4 + where_ref[3], where_ref[4]
    for shift in range(8):
        source = lax.rem(chip + (8 - shift), 8)
        tile_ref[source, core] = parts[shift][core]
        tile_ref[source, 1 - core] = passed_ref[shift]


def pair_sum_kernel(where_ref, keep_ref, got_ref, *refs):
    outs, sum_s = refs[:4], refs[4]
    total = keep_ref[...].astype(F32) + got_ref[...].astype(F32)
    sum_s[...] = total.astype(BF16).reshape(4, 256, D)
    for shift in range(4):
        outs[shift][...] = sum_s[lax.rem(where_ref[3] + shift, 4)]


def merge_kernel(keep_ref, got_ref, *refs):
    quarters, both_ref = refs[:4], refs[4]
    total = keep_ref[...].astype(F32) + got_ref[...].astype(F32)
    rows = total.astype(BF16).reshape(64, 16, D)
    quarter = quarters[0][...].astype(F32)
    for i in range(1, 4):
        quarter = quarter + quarters[i][...].astype(F32)
    quarter = quarter.astype(BF16).reshape(16, 16, D)
    for group in range(4):
        lanes = slice(group * 128, (group + 1) * 128)
        both_ref[:, group * 16 : (group + 1) * 16, :] = rows[:, :, lanes]
        for block in range(16):
            both_ref[block * 4 + group, 64:80, :] = quarter[block, :, lanes]


def chip_sum(parts_ref, rows, first, step):
    total = parts_ref[first, rows, :].astype(F32)
    for chip in range(first + step, 64, step):
        total = total + parts_ref[chip, rows, :].astype(F32)
    return total.astype(BF16)


def spread_kernel(both_ref, spread_ref):
    row_sum = chip_sum(both_ref, slice(0, 64), 0, 1)
    spread_ref[:, 0:64, :] = jnp.broadcast_to(row_sum[None], (64, 64, 128))
    for quarter in range(4):
        part = chip_sum(both_ref, slice(64, 80), quarter, 4)
        first = 64 + quarter * 16
        spread_ref[:, first : first + 16, :] = jnp.broadcast_to(part[None], (64, 16, 128))


def widen_kernel(side, where_ref, chunks_ref, *refs):
    row_ref, col_ref, row_s, col_s, row_sem, col_sem = refs[-6:]
    half = where_ref[4] if side == 0 else 1 - where_ref[4]
    copies = []
    for part in range(4):
        chunks = slice(part * 16, (part + 1) * 16)
        for group in range(4):
            lanes = slice(group * 128, (group + 1) * 128)
            piece = chunks_ref[chunks, group * 16 : (group + 1) * 16, :].astype(F32)
            row_s[part, :, lanes] = piece.reshape(256, 128)
        rows = pl.ds(part * 256, 256)
        copies.append(
            pltpu.make_async_copy(row_s.at[part], row_ref.at[half, rows], row_sem.at[part])
        )
        copies[-1].start()
    for quarter in range(4):
        first = 64 + quarter * 16
        for block in range(16):
            for group in range(4):
                col_s[quarter, block * 16 : (block + 1) * 16, group * 128 : (group + 1) * 128] = (
                    chunks_ref[block * 4 + group, first : first + 16, :].astype(F32)
                )
        copies.append(
            pltpu.make_async_copy(col_s.at[quarter], col_ref.at[half, quarter], col_sem.at[quarter])
        )
        copies[-1].start()
    wait_all(copies)


MIB = 1 << 20
SMEM = pl.BlockSpec(memory_space=pltpu.SMEM)
VMEM = pl.BlockSpec(memory_space=pltpu.VMEM)
HBM = pl.BlockSpec(memory_space=pltpu.HBM)


SPACE = {"s": SMEM, "v": VMEM, "h": HBM}


def call(kernel, ins, out_kinds, outs, scratch, flops, moved, grant=16):
    spaces = tuple(SPACE[kind] for kind in out_kinds)
    return pl.pallas_call(
        kernel,
        in_specs=[SPACE[kind] for kind in ins],
        out_specs=spaces if isinstance(outs, tuple) else spaces[0],
        out_shape=outs,
        scratch_shapes=scratch,
        compiler_params=pltpu.CompilerParams(vmem_limit_bytes=grant * MIB),
        cost_estimate=pl.CostEstimate(flops=flops, bytes_accessed=moved, transcendentals=0),
    )


def shape(*dims, dtype=BF16):
    return jax.ShapeDtypeStruct(dims, dtype)


MATMUL = 2 * TOK * D * D
ATTEND = 2 * 16 * LINE * LINE * HEAD
MIX_TILE = pltpu.VMEM((4, TOK, 128), F32)
DMA = pltpu.SemaphoreType.DMA
WEIGHTS = [pltpu.VMEM((4, D, D), BF16), DMA((4,))]
WEIGHT = [pltpu.VMEM((D, D), BF16), DMA]
LINES = shape(2, 32, D)
PIECE = shape(2, 2, 32, D)
PASS = shape(4, 2, 32, D)
QUARTER = shape(256, D)
HALF = shape(2, D, D)
HALF_S = pltpu.VMEM((2, D, D), BF16)


def token_scratch(*lead, dtype=BF16):
    return pltpu.VMEM((*lead, TOK, D), dtype)


row_forward = call(
    row_forward_kernel,
    "svv",
    "hh",
    (shape(N_DEV, 4, D), shape(5, TOK, D)),
    [
        token_scratch(), pltpu.VMEM((N_DEV, 4, D), BF16), token_scratch(3), token_scratch(2),
        DMA((4,)), DMA((3,)), DMA((2,)),
    ],
    4 * MATMUL + 2 * ATTEND,
    6 * MIB,
    grant=50,
)
row_prepare = call(
    row_prepare_kernel, "v", "vv", (shape(8, TOK, LINE), shape(2, D, TOK)), [], ATTEND, 8 * MIB
)
row_backward = call(
    row_backward_kernel,
    "svhhhh",
    "hh",
    (HALF, shape(4, TOK, D)),
    [
        token_scratch(), pltpu.VMEM((D, D), BF16), token_scratch(3),
        pltpu.VMEM((2, D, TOK), BF16), pltpu.VMEM((8, TOK, LINE), BF16), HALF_S,
        token_scratch(4), DMA, DMA((3,)), DMA((2,)), DMA((2,)), DMA, DMA((4,)),
    ],
    5 * MATMUL + 5 * ATTEND,
    12 * MIB,
    grant=50,
)
kept_gradients = call(
    kept_gradients_kernel,
    "shh",
    "v",
    HALF,
    [pltpu.VMEM((2, D, TOK), BF16), token_scratch(2), DMA((2,)), DMA((2,))],
    2 * MATMUL,
    3 * MIB,
    grant=50,
)
row_input_gradient = call(
    row_input_gradient_kernel,
    "svhh",
    "v" * 8,
    (shape(2, 2, 16, D),) * 8,
    [
        pltpu.VMEM((3, D, D), BF16), token_scratch(4), pltpu.VMEM((8, 2, 2, 16, D), BF16),
        DMA((3,)), DMA((4,)),
    ],
    3 * MATMUL,
    5 * MIB,
    grant=50,
)
col_grad = call(
    col_kernel,
    "svv" + "v" * 5,
    "vh",
    (shape(N_DEV, 4, D), shape(7, TOK, D)),
    [
        token_scratch(), token_scratch(dtype=F32), token_scratch(), token_scratch(2), token_scratch(4),
        token_scratch(3), token_scratch(), DMA((2,)), DMA((4,)), DMA,
    ],
    8 * MATMUL + 6 * ATTEND,
    8 * MIB,
    grant=50,
)
col_weights = call(
    col_weights_kernel,
    "sh",
    "vh",
    (HALF, shape(2, D, TOK)),
    [
        token_scratch(2), token_scratch(2), pltpu.VMEM((2, D, TOK), BF16),
        DMA((2,)), DMA((2,)), DMA((2,)),
    ],
    2 * MATMUL,
    6 * MIB,
    grant=50,
)
col_output = call(
    col_output_kernel,
    "shh",
    "v" * 8,
    (LINES,) * 8,
    [token_scratch(), token_scratch(), pltpu.VMEM((D, D), BF16), token_scratch(), DMA((3,))],
    MATMUL,
    3 * MIB,
    grant=52,
)
tile_to_lines = call(tile_to_lines_kernel, "sv", "v" * 4, (PIECE,) * 4, [MIX_TILE], 0, MIB)
pass_low = call(pass_low_kernel, "s" + "v" * 4, "v", PASS, [], 0, MIB)
lines_to_tile = call(lines_to_tile_kernel, "s" + "v" * 8, "v", shape(32, 16, D), [MIX_TILE], 0, MIB)
CORE_PASS = shape(8, 2, 16, D)
pass_core = call(pass_core_kernel, "s" + "v" * 8, "v", CORE_PASS, [], 0, MIB)
join = call(join_kernel, "s" + "v" * 9, "v", shape(8, 2, 2, 16, D), [], 0, MIB)
pair_sum = call(
    pair_sum_kernel, "svv", "v" * 4, (QUARTER,) * 4, [pltpu.VMEM((4, 256, D), BF16)], 0, 3 * MIB,
)
merge = call(merge_kernel, "v" * 6, "v", shape(64, 80, 128), [], 0, 4 * MIB)
spread = call(spread_kernel, "v", "v", shape(64, 128, 128), [], 0, 3 * MIB, grant=52)


def widen(where, chunks, side, *before):
    return pl.pallas_call(
        functools.partial(widen_kernel, side),
        in_specs=[SMEM, VMEM] + [HBM] * len(before),
        out_specs=(HBM, HBM),
        out_shape=(shape(2, 1024, D, dtype=F32), shape(2, 4, 256, D, dtype=F32)),
        scratch_shapes=[
            pltpu.VMEM((4, 256, D), F32), pltpu.VMEM((4, 256, D), F32), DMA((4,)), DMA((4,)),
        ],
        input_output_aliases={2: 0, 3: 1} if before else {},
        name="widen",
        compiler_params=pltpu.CompilerParams(vmem_limit_bytes=16 * MIB),
        cost_estimate=pl.CostEstimate(flops=0, bytes_accessed=6 * MIB, transcendentals=0),
    )(where, chunks, *before)


def exchange(values, axes):
    return lax.all_to_all(values, axes, split_axis=0, concat_axis=0, tiled=True)


def shifted(pieces, axes):
    n = len(pieces)
    return [pieces[0]] + [
        lax.ppermute(pieces[k], axes, [(i, (i + k) % n) for i in range(n)]) for k in range(1, n)
    ]


def swap(value, axis):
    return lax.ppermute(value, axis, [(0, 1), (1, 0)])


def layer(latents, cotangent, w_row, w_col, keep_heads):
    where = jnp.concatenate(
        [jnp.stack([lax.axis_index(name) for name in AXES]), keep_heads.reshape(-1)]
    ).astype(jnp.int32)
    rows_in = exchange(latents.reshape(16, 2, 16, D), COL)
    grad_pieces = tile_to_lines(where, cotangent)
    grad_parts = shifted(grad_pieces, "y")
    grad_pass = pass_low(where, *grad_parts)
    grad_pass = swap(grad_pass, "zl")
    mid_send, saved_row = row_forward(where, rows_in, w_row)
    mid_lines = exchange(mid_send, BOTH)
    probs_row, turned_row = row_prepare(saved_row)
    grad_send, saved_col = col_grad(
        where, mid_lines, w_col, *grad_parts, grad_pass
    )
    grad_rows = exchange(grad_send, BOTH)
    send_col, turned_col = col_weights(where, saved_col)
    got_col = swap(send_col, "c")
    keep_col = kept_gradients(where, turned_col, saved_col)
    quarters = pair_sum(where, keep_col, got_col)
    quarters = shifted(quarters, "x")
    send_row, right_row = row_backward(where, grad_rows, saved_row, turned_row, probs_row, w_row)
    got_row = swap(send_row, "c")
    keep_row = kept_gradients(where, turned_row, right_row)
    merged = merge(keep_row, got_row, *quarters)
    both = exchange(merged, CHIPS)
    totals = spread(both)
    chunks = exchange(totals, CHIPS)
    gin_pieces = row_input_gradient(where, rows_in, right_row, w_row)
    gin_parts = shifted(gin_pieces, ("zh", "x"))
    gin_core = pass_core(where, *gin_parts)
    gin_core = swap(gin_core, "c")
    grad_latents = join(where, *gin_parts, gin_core).reshape(32, 16, D)
    out_pieces = col_output(where, saved_col, w_col)
    out_parts = shifted(out_pieces, ROW)
    output = lines_to_tile(where, *out_parts)
    other = swap(chunks, "c")
    halves_done = widen(where, chunks, 0)
    grad_row, grad_col = widen(where, other, 1, *halves_done)
    return (output, grad_latents, grad_row.reshape(4, D, D), grad_col.reshape(4, D, D))


def solution(mesh):
    fine = Mesh(mesh.devices.reshape(4, 2, 2, 4, 2), AXES)
    tile = P(ROW, COL, None)
    return jax.shard_map(
        layer,
        mesh=fine,
        in_specs=(tile, tile, P(), P(), P()),
        out_specs=(tile, tile, P(), P()),
        check_vma=False,
    )
```

```python
import functools

import jax
import jax.numpy as jnp
from jax import lax
from jax.experimental import pallas as pl
from jax.experimental.pallas import tpu as pltpu
from jax.sharding import Mesh, PartitionSpec as P


HEADS = 8
HEAD = 64
D = 512
PAIR = 128
N_PAIR = D // PAIR
LINE = 256
TOK = 512
N_ROW = 8
N_COL = 16
N_DEV = N_ROW * N_COL
EPSILON = 1e-06
SCALE = HEAD ** (-0.5)

F32 = jnp.float32
BF16 = jnp.bfloat16

AXES = ("y", "zl", "zh", "x", "c")
ROW = ("y", "zl")
COL = ("zh", "x", "c")
BOTH = COL + ROW
CHIPS = ("y", "zl", "zh", "x")


def dot(left, right):
    return lax.dot_general(left, right, (((1,), (0,)), ((), ())), preferred_element_type=F32)


def dot_nt(left, right):
    return lax.dot_general(left, right, (((1,), (1,)), ((), ())), preferred_element_type=F32)


def stack_halves(value):
    lane = lax.broadcasted_iota(jnp.int32, value.shape, 1)
    zero = jnp.zeros_like(value)
    low, high = jnp.where(lane < HEAD, value, zero), jnp.where(lane >= HEAD, value, zero)
    return jnp.concatenate([low, high], axis=0)


def pick_halves(value):
    low, high = value[:LINE], value[LINE:]
    lane = lax.broadcasted_iota(jnp.int32, low.shape, 1)
    return jnp.where(lane < HEAD, low, high)


def turn_halves(value):
    return jnp.concatenate([value[:LINE].T, value[LINE:].T], axis=0)


def gain_row(info_ref, block, first, count):
    head = lax.broadcasted_iota(jnp.int32, (1, count * HEAD), 1) // HEAD
    gain = jnp.zeros((1, count * HEAD), F32)
    for i in range(count):
        gain = jnp.where(head == i, info_ref[5 + block * HEADS + first + i].astype(F32), gain)
    return gain


def inverse_rms(values_f):
    return lax.rsqrt(jnp.mean(values_f * values_f, axis=-1, keepdims=True) + EPSILON)


def softmax(q_pair, k_pair):
    scores = dot_nt(stack_halves(q_pair), k_pair)
    peak = jnp.max(scores, axis=-1, keepdims=True)
    grown = jnp.exp(scores - peak)
    return grown * (1.0 / jnp.sum(grown, axis=-1, keepdims=True))


def picked(rows):
    return jnp.where(rows == lax.broadcasted_iota(jnp.int32, (TOK, TOK), 1), 1.0, 0.0).astype(BF16)


def chunk_row(grid_col, grid_row, row_local, col_local):
    return ((grid_col * 8 + grid_row) * 2 + row_local) * 2 + col_local


def positions():
    return lax.broadcasted_iota(jnp.int32, (TOK, 1), 0)


def chunk_parts():
    row = positions()
    return row // 32, (row // 4) % 8, (row // 2) % 2, row % 2


def row_tokens_of_chunks():
    token = positions()
    return picked(chunk_row((token // 16) % 16, token % 8, token // 256, (token // 8) % 2))


def chunks_of_row_tokens():
    grid_col, grid_row, row_local, col_local = chunk_parts()
    return picked(row_local * 256 + grid_col * 16 + col_local * 8 + grid_row)


def col_tokens_of_chunks():
    token = positions()
    return picked(chunk_row(token % 16, (token // 16) % 8, (token // 128) % 2, token // 256))


def chunks_of_col_tokens():
    grid_col, grid_row, row_local, col_local = chunk_parts()
    return picked(col_local * 256 + row_local * 128 + grid_row * 16 + grid_col)


def copies_of(source, target, sems, count):
    return [pltpu.make_async_copy(source.at[i], target.at[i], sems.at[i]) for i in range(count)]


def start_all(copies):
    for copy in copies:
        copy.start()


def wait_all(copies):
    for copy in copies:
        copy.wait()


def project(normed, qkv_ref, w_ref, copies=()):
    wait_all(copies[0:1])
    qkv_ref[0] = (dot(normed, w_ref[0]).astype(BF16).astype(F32) * SCALE).astype(BF16)
    wait_all(copies[1:2])
    qkv_ref[1] = dot(normed, w_ref[1]).astype(BF16)
    wait_all(copies[2:3])
    qkv_ref[2] = dot(normed, w_ref[2]).astype(BF16)


def each_pair(visit, per_step=2, before=None, after=None):
    def step(index, carry):
        line = index // (N_PAIR // per_step)
        first = lax.rem(index, N_PAIR // per_step) * per_step
        if before is not None:
            before(line)
        rows = pl.ds(pl.multiple_of(line * LINE, LINE), LINE)
        for offset in range(per_step):
            pair = first + offset
            lanes = pl.ds(pl.multiple_of(pair * PAIR, PAIR), PAIR)
            visit(rows, lanes, line * N_PAIR + pair, pair)
        if after is not None:
            after(line)
        return carry

    lax.fori_loop(0, 2 * N_PAIR // per_step, step, 0)


def row_forward_kernel(
    where_ref, x_ref, w_ref, mid_ref, saved_ref,
    w_s, order_s, mid_s, qkv_s, left_s, w_sem, mid_sem, qkv_sem, left_sem,
):
    weights = copies_of(w_ref, w_s, w_sem, 4)
    start_all(weights)
    saved = copies_of(qkv_s, saved_ref, qkv_sem, 3)
    lefts = copies_of(left_s, saved_ref.at[3:5], left_sem, 2)
    order_s[...] = chunks_of_row_tokens()
    for rr in range(2):
        u = x_ref[:, rr].astype(F32).reshape(LINE, D)
        left_s[0, rr * LINE : (rr + 1) * LINE, :] = (u * inverse_rms(u)).astype(BF16)
    project(left_s[0], qkv_s, w_s, weights)
    lefts[0].start()
    start_all(saved)

    def visit(rows, lanes, at, pair):
        probs = softmax(qkv_s[0, rows, lanes], qkv_s[1, rows, lanes]).astype(BF16)
        mixed = pick_halves(dot(probs, qkv_s[2, rows, lanes]))
        left_s[1, rows, lanes] = (mixed * gain_row(where_ref, 0, pair * 2, 2)).astype(BF16)

    each_pair(visit, 4)
    lefts[1].start()
    weights[3].wait()
    added = dot(left_s[1], w_s[3])
    mids = []
    for rr in range(2):
        u = x_ref[:, rr].astype(F32).reshape(LINE, D)
        mids.append((u + added[rr * LINE : (rr + 1) * LINE]).astype(BF16))
    mid = jnp.concatenate(mids, axis=0)
    sends = []
    for part in range(4):
        rows = slice(part * 32, (part + 1) * 32)
        turned = dot(order_s[part * 128 : (part + 1) * 128, :], mid)
        mid_s[rows] = turned.astype(BF16).reshape(32, 4, D)
        sends.append(pltpu.make_async_copy(mid_s.at[rows], mid_ref.at[rows], mid_sem.at[part]))
        sends[-1].start()
    wait_all(saved + lefts + sends)


def row_prepare_kernel(saved_ref, probs_ref, turned_ref):
    def visit(rows, lanes, at, pair):
        probs = softmax(saved_ref[0, rows, lanes], saved_ref[1, rows, lanes])
        probs_ref[at] = probs.astype(BF16)

    each_pair(visit)
    for which in range(2):
        turned_ref[which] = saved_ref[3 + which].T


def attention_backward(rows, lanes, qkv, da_ref, probs, right_ref):
    q_pair, k_pair, v_pair = (qkv[i, rows, lanes] for i in range(3))
    da_pair = da_ref[rows, lanes]
    low = probs.astype(BF16)
    probs = probs.astype(F32)
    grad_probs = dot_nt(stack_halves(da_pair), v_pair)
    total = jnp.sum(probs * grad_probs, axis=-1, keepdims=True)
    grads = (probs * (grad_probs - total)).astype(BF16)
    right_ref[0, rows, lanes] = (pick_halves(dot(grads, k_pair)) * SCALE).astype(BF16)
    right_ref[1, rows, lanes] = pick_halves(dot(turn_halves(grads), q_pair)).astype(BF16)
    right_ref[2, rows, lanes] = pick_halves(dot(turn_halves(low), da_pair)).astype(BF16)
    return low


def input_gradient(u, right_ref, w_s, rows):
    inv = inverse_rms(u)
    dn = (
        dot_nt(right_ref[0, rows, :], w_s[0])
        + dot_nt(right_ref[1, rows, :], w_s[1])
        + dot_nt(right_ref[2, rows, :], w_s[2])
    )
    mean = jnp.mean(dn * u, axis=-1, keepdims=True)
    return right_ref[3, rows, :].astype(F32) + inv * dn - u * (inv * inv * inv * mean)


def weight_gradients(side, turned, right_ref, target):
    for j in range(2):
        which = side * 2 + j
        target[j] = dot(turned[which // 3], right_ref[which]).astype(BF16)


def row_backward_kernel(
    where_ref, g_ref, qkv_ref, turned_ref, probs_ref, w_ref,
    send_ref, right_ref,
    da_s, wo_s, qkv_s, turned_s, probs_s, right_s,
    wo_sem, qkv_sem, turned_sem, probs_sem, grad_sem, right_sem,
):
    weight = pltpu.make_async_copy(w_ref.at[3], wo_s, wo_sem)
    weight.start()
    saved = copies_of(qkv_ref, qkv_s, qkv_sem, 3)
    start_all(saved)
    turned = copies_of(turned_ref, turned_s, turned_sem, 2)

    def line_probs(line):
        pairs = pl.ds(line * N_PAIR, N_PAIR)
        return pltpu.make_async_copy(probs_ref.at[pairs], probs_s.at[pairs], probs_sem.at[line])

    line_probs(0).start()
    right_s[3] = dot(row_tokens_of_chunks(), g_ref[...].reshape(TOK, D)).astype(BF16)
    grad = pltpu.make_async_copy(right_s.at[3], right_ref.at[3], grad_sem)
    grad.start()
    weight.wait()
    gain = gain_row(where_ref, 0, 0, HEADS)
    da_s[...] = (dot_nt(right_s[3], wo_s[...]) * gain).astype(BF16)
    line_probs(1).start()
    start_all(turned)
    wait_all(saved)

    def visit(rows, lanes, at, pair):
        attention_backward(rows, lanes, qkv_s, da_s, probs_s[at], right_s)

    def line_grads(line):
        rows = pl.ds(pl.multiple_of(line * LINE, LINE), LINE)
        return pltpu.make_async_copy(
            right_s.at[0:3, rows], right_ref.at[0:3, rows], right_sem.at[line]
        )

    each_pair(
        visit, 4, lambda line: line_probs(line).wait(), lambda line: line_grads(line).start()
    )
    wait_all(turned)
    weight_gradients(1 - where_ref[4], turned_s, right_s, send_ref)
    wait_all([line_grads(0), line_grads(1), grad])


def kept_gradients_kernel(where_ref, turned_ref, right_ref, keep_ref, turned_s, right_s, turned_sem, right_sem):
    core = where_ref[4]
    turned = copies_of(turned_ref, turned_s, turned_sem, 2)
    rights = copies_of(right_ref.at[pl.ds(core * 2, 2)], right_s, right_sem, 2)
    start_all(turned + rights)
    wait_all(turned + rights)
    for j in range(2):
        keep_ref[j] = dot(turned_s[(core * 2 + j) // 3], right_s[j]).astype(BF16)


def row_input_gradient_kernel(where_ref, x_ref, right_ref, w_ref, *refs):
    outs, w_s, right_s, gin_s, w_sem, right_sem = refs[:8], *refs[8:]
    weights = copies_of(w_ref, w_s, w_sem, 3)
    rights = copies_of(right_ref, right_s, right_sem, 4)
    start_all([copy for pair in zip(weights, rights) for copy in pair] + rights[3:])
    wait_all(weights + rights)
    for rr in range(2):
        rows = slice(rr * LINE, (rr + 1) * LINE)
        u = x_ref[:, rr].astype(F32).reshape(LINE, D)
        grad_in = input_gradient(u, right_s, w_s, rows)
        gin_s[:, :, rr] = grad_in.astype(BF16).reshape(8, 2, 16, D)
    chip = where_ref[2] * 4 + where_ref[3]
    for shift in range(8):
        outs[shift][...] = gin_s[lax.rem(chip + shift, 8)]


def col_kernel(where_ref, m_ref, w_ref, *refs):
    parts, got_ref, refs = refs[:4], refs[4], refs[5:]
    gmid_ref, saved_ref = refs[:2]
    order_s, u_s, ulow_s, left_s, right_s, qkv_s, da_s = refs[2:9]
    left_sem, right_sem, u_sem = refs[9:]
    mine = where_ref[1]
    rights = copies_of(right_s, saved_ref, right_sem, 4)
    lefts = copies_of(left_s, saved_ref.at[4:6], left_sem, 2)
    order_s[...] = chunks_of_col_tokens()
    u_s[...] = dot(col_tokens_of_chunks(), m_ref[...].reshape(TOK, D))
    u = u_s[...]
    ulow_s[...] = u.astype(BF16)
    kept_u = pltpu.make_async_copy(ulow_s, saved_ref.at[6], u_sem)
    kept_u.start()
    left_s[0] = (u * inverse_rms(u)).astype(BF16)
    lefts[0].start()
    for shift in range(4):
        source = lax.rem(where_ref[0] + (4 - shift), 4) * 2
        for grid_row, piece in ((source + mine, parts[shift].at[mine]), (source + (1 - mine), got_ref.at[shift])):
            for cc in range(2):
                for rr in range(2):
                    at = pl.multiple_of(grid_row * 16 + (cc * LINE + rr * 128), 16)
                    right_s[3, pl.ds(at, 16), :] = piece[cc, rr * 16 : (rr + 1) * 16, :]
    rights[3].start()
    gain = gain_row(where_ref, 1, 0, HEADS)
    da_s[...] = (dot_nt(right_s[3], w_ref[3]) * gain).astype(BF16)
    project(left_s[0], qkv_s, w_ref)

    def visit(rows, lanes, at, pair):
        probs = softmax(qkv_s[0, rows, lanes], qkv_s[1, rows, lanes])
        low = attention_backward(rows, lanes, qkv_s, da_s, probs, right_s)
        mixed = pick_halves(dot(low, qkv_s[2, rows, lanes]))
        left_s[1, rows, lanes] = (mixed * gain_row(where_ref, 1, pair * 2, 2)).astype(BF16)

    each_pair(visit, 4)
    lefts[1].start()
    start_all(rights[:3])
    grads = [
        input_gradient(u_s[rows, :], right_s, w_ref, rows).astype(BF16)
        for rows in (slice(0, LINE), slice(LINE, TOK))
    ]
    gmid_ref[...] = dot(order_s[...], jnp.concatenate(grads, axis=0)).astype(BF16).reshape(N_DEV, 4, D)
    wait_all(lefts + rights + [kept_u])


def col_weights_kernel(where_ref, saved_ref, send_ref, turned_ref, *refs):
    left_s, right_s, turned_s, left_sem, right_sem, turned_sem = refs
    side = 1 - where_ref[4]
    lefts = copies_of(saved_ref.at[4:6], left_s, left_sem, 2)
    rights = copies_of(saved_ref.at[pl.ds(side * 2, 2)], right_s, right_sem, 2)
    start_all(lefts + rights)
    turned = copies_of(turned_s, turned_ref, turned_sem, 2)
    for which in range(2):
        lefts[which].wait()
        turned_s[which] = left_s[which].T
        turned[which].start()
    wait_all(rights)
    for j in range(2):
        send_ref[j] = dot(turned_s[(side * 2 + j) // 3], right_s[j]).astype(BF16)
    wait_all(turned)


def col_output_kernel(where_ref, saved_ref, w_ref, *refs):
    outs, (att_s, ulow_s, wo_s, out_s, sem) = refs[:8], refs[8:]
    copies = [
        pltpu.make_async_copy(saved_ref.at[5], att_s, sem.at[0]),
        pltpu.make_async_copy(w_ref.at[3], wo_s, sem.at[1]),
        pltpu.make_async_copy(saved_ref.at[6], ulow_s, sem.at[2]),
    ]
    start_all(copies)
    wait_all(copies)
    out_s[...] = (ulow_s[...].astype(F32) + dot(att_s[...], wo_s[...])).astype(BF16)
    me = where_ref[0] * 2 + where_ref[1]
    for shift in range(8):
        start = lax.rem(me + shift, 8) * 16
        for cc in range(2):
            for rr in range(2):
                at = pl.multiple_of(start + (cc * LINE + rr * 128), 16)
                outs[shift][cc, rr * 16 : (rr + 1) * 16, :] = out_s[pl.ds(at, 16), :]


def tile_to_lines_kernel(where_ref, tile_ref, *refs):
    outs, mix_s = refs[:4], refs[4]
    tile = tile_ref[...].astype(F32).reshape(TOK, D)
    for group in range(4):
        lanes = slice(group * 128, (group + 1) * 128)
        mix_s[group] = tile[:, lanes]
        for shift in range(4):
            for low in range(2):
                peer = lax.rem(where_ref[0] + shift, 4) * 2 + low
                for cc in range(2):
                    for rr in range(2):
                        piece = mix_s[group, pl.ds(peer + (rr * 16 + cc * 8), 16, stride=32), :]
                        outs[shift][low, cc, rr * 16 : (rr + 1) * 16, lanes] = piece.astype(BF16)


def pass_low_kernel(where_ref, *refs):
    parts, pass_ref = refs[:4], refs[4]
    for shift in range(4):
        pass_ref[shift] = parts[shift][1 - where_ref[1]]


def lines_to_tile_kernel(where_ref, *refs):
    parts, tile_ref = refs[:8], refs[8]
    row = positions()
    shift = (where_ref[0] * 2 + where_ref[1] + 8 - row % 8) % 8
    order = picked(((shift * 2 + (row // 8) % 2) * 2 + (row // 16) % 2) * 16 + row // 32)
    lines = jnp.concatenate([part[...].reshape(64, D) for part in parts], axis=0)
    tile_ref[...] = dot(order, lines).astype(BF16).reshape(32, 16, D)


def pass_core_kernel(where_ref, *refs):
    parts, pass_ref = refs[:8], refs[8]
    for shift in range(8):
        pass_ref[shift] = parts[shift][1 - where_ref[4]]


def join_kernel(where_ref, *refs):
    parts, passed_ref, tile_ref = refs[:8], refs[8], refs[9]
    chip, core = where_ref[2] * 4 + where_ref[3], where_ref[4]
    for shift in range(8):
        source = lax.rem(chip + (8 - shift), 8)
        tile_ref[source, core] = parts[shift][core]
        tile_ref[source, 1 - core] = passed_ref[shift]


def pair_sum_kernel(where_ref, keep_ref, got_ref, *refs):
    outs, sum_s = refs[:4], refs[4]
    total = keep_ref[...].astype(F32) + got_ref[...].astype(F32)
    sum_s[...] = total.astype(BF16).reshape(4, 256, D)
    for shift in range(4):
        outs[shift][...] = sum_s[lax.rem(where_ref[3] + shift, 4)]


def merge_kernel(keep_ref, got_ref, *refs):
    quarters, both_ref = refs[:4], refs[4]
    total = keep_ref[...].astype(F32) + got_ref[...].astype(F32)
    rows = total.astype(BF16).reshape(64, 16, D)
    quarter = quarters[0][...].astype(F32)
    for i in range(1, 4):
        quarter = quarter + quarters[i][...].astype(F32)
    quarter = quarter.astype(BF16).reshape(16, 16, D)
    for group in range(4):
        lanes = slice(group * 128, (group + 1) * 128)
        both_ref[:, group * 16 : (group + 1) * 16, :] = rows[:, :, lanes]
        for block in range(16):
            both_ref[block * 4 + group, 64:80, :] = quarter[block, :, lanes]


def chip_sum(parts_ref, rows, first, step):
    total = parts_ref[first, rows, :].astype(F32)
    for chip in range(first + step, 64, step):
        total = total + parts_ref[chip, rows, :].astype(F32)
    return total.astype(BF16)


def spread_kernel(both_ref, spread_ref):
    row_sum = chip_sum(both_ref, slice(0, 64), 0, 1)
    spread_ref[:, 0:64, :] = jnp.broadcast_to(row_sum[None], (64, 64, 128))
    for quarter in range(4):
        part = chip_sum(both_ref, slice(64, 80), quarter, 4)
        first = 64 + quarter * 16
        spread_ref[:, first : first + 16, :] = jnp.broadcast_to(part[None], (64, 16, 128))


def widen_kernel(side, where_ref, chunks_ref, *refs):
    row_ref, col_ref, row_s, col_s, row_sem, col_sem = refs[-6:]
    half = where_ref[4] if side == 0 else 1 - where_ref[4]
    copies = []
    for part in range(4):
        chunks = slice(part * 16, (part + 1) * 16)
        for group in range(4):
            lanes = slice(group * 128, (group + 1) * 128)
            piece = chunks_ref[chunks, group * 16 : (group + 1) * 16, :].astype(F32)
            row_s[part, :, lanes] = piece.reshape(256, 128)
        rows = pl.ds(part * 256, 256)
        copies.append(
            pltpu.make_async_copy(row_s.at[part], row_ref.at[half, rows], row_sem.at[part])
        )
        copies[-1].start()
    for quarter in range(4):
        first = 64 + quarter * 16
        for block in range(16):
            for group in range(4):
                col_s[quarter, block * 16 : (block + 1) * 16, group * 128 : (group + 1) * 128] = (
                    chunks_ref[block * 4 + group, first : first + 16, :].astype(F32)
                )
        copies.append(
            pltpu.make_async_copy(col_s.at[quarter], col_ref.at[half, quarter], col_sem.at[quarter])
        )
        copies[-1].start()
    wait_all(copies)


MIB = 1 << 20
SMEM = pl.BlockSpec(memory_space=pltpu.SMEM)
VMEM = pl.BlockSpec(memory_space=pltpu.VMEM)
HBM = pl.BlockSpec(memory_space=pltpu.HBM)


SPACE = {"s": SMEM, "v": VMEM, "h": HBM}


def call(kernel, ins, out_kinds, outs, scratch, flops, moved, grant=16):
    spaces = tuple(SPACE[kind] for kind in out_kinds)
    return pl.pallas_call(
        kernel,
        in_specs=[SPACE[kind] for kind in ins],
        out_specs=spaces if isinstance(outs, tuple) else spaces[0],
        out_shape=outs,
        scratch_shapes=scratch,
        compiler_params=pltpu.CompilerParams(vmem_limit_bytes=grant * MIB),
        cost_estimate=pl.CostEstimate(flops=flops, bytes_accessed=moved, transcendentals=0),
    )


def shape(*dims, dtype=BF16):
    return jax.ShapeDtypeStruct(dims, dtype)


MATMUL = 2 * TOK * D * D
ATTEND = 2 * 16 * LINE * LINE * HEAD
MIX_TILE = pltpu.VMEM((4, TOK, 128), F32)
DMA = pltpu.SemaphoreType.DMA
WEIGHTS = [pltpu.VMEM((4, D, D), BF16), DMA((4,))]
WEIGHT = [pltpu.VMEM((D, D), BF16), DMA]
LINES = shape(2, 32, D)
PIECE = shape(2, 2, 32, D)
PASS = shape(4, 2, 32, D)
QUARTER = shape(256, D)
HALF = shape(2, D, D)


def token_scratch(*lead, dtype=BF16):
    return pltpu.VMEM((*lead, TOK, D), dtype)


row_forward = call(
    row_forward_kernel,
    "svh",
    "hh",
    (shape(N_DEV, 4, D), shape(5, TOK, D)),
    [
        WEIGHTS[0], token_scratch(), pltpu.VMEM((N_DEV, 4, D), BF16), token_scratch(3),
        token_scratch(2), WEIGHTS[1],
        DMA((4,)), DMA((3,)), DMA((2,)),
    ],
    4 * MATMUL + 2 * ATTEND,
    6 * MIB,
    grant=51,
)
row_prepare = call(
    row_prepare_kernel, "v", "vv", (shape(8, TOK, LINE), shape(2, D, TOK)), [], ATTEND, 8 * MIB
)
row_backward = call(
    row_backward_kernel,
    "svhhhh",
    "vh",
    (HALF, shape(4, TOK, D)),
    [
        token_scratch(), pltpu.VMEM((D, D), BF16), token_scratch(3),
        pltpu.VMEM((2, D, TOK), BF16), pltpu.VMEM((8, TOK, LINE), BF16),
        token_scratch(4), DMA, DMA((3,)), DMA((2,)), DMA((2,)), DMA, DMA((2,)),
    ],
    5 * MATMUL + 5 * ATTEND,
    12 * MIB,
    grant=50,
)
kept_gradients = call(
    kept_gradients_kernel,
    "shh",
    "v",
    HALF,
    [pltpu.VMEM((2, D, TOK), BF16), token_scratch(2), DMA((2,)), DMA((2,))],
    2 * MATMUL,
    3 * MIB,
    grant=50,
)
row_input_gradient = call(
    row_input_gradient_kernel,
    "svhh",
    "v" * 8,
    (shape(2, 2, 16, D),) * 8,
    [
        pltpu.VMEM((3, D, D), BF16), token_scratch(4), pltpu.VMEM((8, 2, 2, 16, D), BF16),
        DMA((3,)), DMA((4,)),
    ],
    3 * MATMUL,
    5 * MIB,
    grant=51,
)
col_grad = call(
    col_kernel,
    "svv" + "v" * 5,
    "vh",
    (shape(N_DEV, 4, D), shape(7, TOK, D)),
    [
        token_scratch(), token_scratch(dtype=F32), token_scratch(), token_scratch(2), token_scratch(4),
        token_scratch(3), token_scratch(), DMA((2,)), DMA((4,)), DMA,
    ],
    8 * MATMUL + 6 * ATTEND,
    8 * MIB,
    grant=50,
)
col_weights = call(
    col_weights_kernel,
    "sh",
    "vh",
    (HALF, shape(2, D, TOK)),
    [
        token_scratch(2), token_scratch(2), pltpu.VMEM((2, D, TOK), BF16),
        DMA((2,)), DMA((2,)), DMA((2,)),
    ],
    2 * MATMUL,
    6 * MIB,
    grant=54,
)
col_output = call(
    col_output_kernel,
    "shh",
    "v" * 8,
    (LINES,) * 8,
    [token_scratch(), token_scratch(), pltpu.VMEM((D, D), BF16), token_scratch(), DMA((3,))],
    MATMUL,
    3 * MIB,
    grant=52,
)
tile_to_lines = call(
    tile_to_lines_kernel, "sv", "v" * 4, (PIECE,) * 4, [MIX_TILE], 0, MIB, grant=48
)
pass_low = call(pass_low_kernel, "s" + "v" * 4, "v", PASS, [], 0, MIB, grant=12)
lines_to_tile = call(
    lines_to_tile_kernel, "s" + "v" * 8, "v", shape(32, 16, D), [], MATMUL, MIB, grant=48
)
CORE_PASS = shape(8, 2, 16, D)
pass_core = call(pass_core_kernel, "s" + "v" * 8, "v", CORE_PASS, [], 0, MIB, grant=40)
join = call(join_kernel, "s" + "v" * 9, "v", shape(8, 2, 2, 16, D), [], 0, MIB)
pair_sum = call(
    pair_sum_kernel, "svv", "v" * 4, (QUARTER,) * 4, [pltpu.VMEM((4, 256, D), BF16)], 0, 3 * MIB,
)
merge = call(merge_kernel, "v" * 6, "v", shape(64, 80, 128), [], 0, 4 * MIB, grant=32)
spread = call(spread_kernel, "v", "v", shape(64, 128, 128), [], 0, 3 * MIB, grant=52)


def widen(where, chunks, side, *before):
    return pl.pallas_call(
        functools.partial(widen_kernel, side),
        in_specs=[SMEM, VMEM] + [HBM] * len(before),
        out_specs=(HBM, HBM),
        out_shape=(shape(2, 1024, D, dtype=F32), shape(2, 4, 256, D, dtype=F32)),
        scratch_shapes=[
            pltpu.VMEM((4, 256, D), F32), pltpu.VMEM((4, 256, D), F32), DMA((4,)), DMA((4,)),
        ],
        input_output_aliases={2: 0, 3: 1} if before else {},
        name="widen",
        compiler_params=pltpu.CompilerParams(vmem_limit_bytes=16 * MIB),
        cost_estimate=pl.CostEstimate(flops=0, bytes_accessed=6 * MIB, transcendentals=0),
    )(where, chunks, *before)


def exchange(values, axes):
    return lax.all_to_all(values, axes, split_axis=0, concat_axis=0, tiled=True)


def shifted(pieces, axes):
    n = len(pieces)
    return [pieces[0]] + [
        lax.ppermute(pieces[k], axes, [(i, (i + k) % n) for i in range(n)]) for k in range(1, n)
    ]


def swap(value, axis):
    return lax.ppermute(value, axis, [(0, 1), (1, 0)])


def layer(latents, cotangent, w_row, w_col, keep_heads):
    where = jnp.concatenate(
        [jnp.stack([lax.axis_index(name) for name in AXES]), keep_heads.reshape(-1)]
    ).astype(jnp.int32)
    rows_in = exchange(latents.reshape(16, 2, 16, D), COL)
    grad_pieces = tile_to_lines(where, cotangent)
    grad_parts = shifted(grad_pieces, "y")
    grad_pass = pass_low(where, *grad_parts)
    grad_pass = swap(grad_pass, "zl")
    mid_send, saved_row = row_forward(where, rows_in, w_row)
    mid_lines = exchange(mid_send, BOTH)
    probs_row, turned_row = row_prepare(saved_row)
    grad_send, saved_col = col_grad(
        where, mid_lines, w_col, *grad_parts, grad_pass
    )
    grad_rows = exchange(grad_send, BOTH)
    send_col, turned_col = col_weights(where, saved_col)
    got_col = swap(send_col, "c")
    keep_col = kept_gradients(where, turned_col, saved_col)
    quarters = pair_sum(where, keep_col, got_col)
    quarters = shifted(quarters, "x")
    send_row, right_row = row_backward(where, grad_rows, saved_row, turned_row, probs_row, w_row)
    got_row = swap(send_row, "c")
    keep_row = kept_gradients(where, turned_row, right_row)
    merged = merge(keep_row, got_row, *quarters)
    both = exchange(merged, CHIPS)
    totals = spread(both)
    chunks = exchange(totals, CHIPS)
    gin_pieces = row_input_gradient(where, rows_in, right_row, w_row)
    gin_parts = shifted(gin_pieces, ("zh", "x"))
    gin_core = pass_core(where, *gin_parts)
    gin_core = swap(gin_core, "c")
    grad_latents = join(where, *gin_parts, gin_core).reshape(32, 16, D)
    out_pieces = col_output(where, saved_col, w_col)
    out_parts = shifted(out_pieces, ROW)
    output = lines_to_tile(where, *out_parts)
    other = swap(chunks, "c")
    halves_done = widen(where, chunks, 0)
    grad_row, grad_col = widen(where, other, 1, *halves_done)
    return (output, grad_latents, grad_row.reshape(4, D, D), grad_col.reshape(4, D, D))


def solution(mesh):
    fine = Mesh(mesh.devices.reshape(4, 2, 2, 4, 2), AXES)
    tile = P(ROW, COL, None)
    return jax.shard_map(
        layer,
        mesh=fine,
        in_specs=(tile, tile, P(), P(), P()),
        out_specs=(tile, tile, P(), P()),
        check_vma=False,
    )
```

```python
import functools

import jax
import jax.numpy as jnp
from jax import lax
from jax.experimental import pallas as pl
from jax.experimental.pallas import tpu as pltpu
from jax.sharding import Mesh, PartitionSpec as P


HEADS = 8
HEAD = 64
D = 512
PAIR = 128
N_PAIR = D // PAIR
LINE = 256
TOK = 512
N_ROW = 8
N_COL = 16
N_DEV = N_ROW * N_COL
EPSILON = 1e-06
SCALE = HEAD ** (-0.5)

F32 = jnp.float32
BF16 = jnp.bfloat16

AXES = ("y", "zl", "zh", "x", "c")
ROW = ("y", "zl")
COL = ("zh", "x", "c")
BOTH = COL + ROW
CHIPS = ("y", "zl", "zh", "x")


def dot(left, right):
    return lax.dot_general(left, right, (((1,), (0,)), ((), ())), preferred_element_type=F32)


def dot_nt(left, right):
    return lax.dot_general(left, right, (((1,), (1,)), ((), ())), preferred_element_type=F32)


def stack_halves(value):
    lane = lax.broadcasted_iota(jnp.int32, value.shape, 1)
    zero = jnp.zeros_like(value)
    low, high = jnp.where(lane < HEAD, value, zero), jnp.where(lane >= HEAD, value, zero)
    return jnp.concatenate([low, high], axis=0)


def pick_halves(value):
    low, high = value[:LINE], value[LINE:]
    lane = lax.broadcasted_iota(jnp.int32, low.shape, 1)
    return jnp.where(lane < HEAD, low, high)


def turn_halves(value):
    return jnp.concatenate([value[:LINE].T, value[LINE:].T], axis=0)


def gain_row(info_ref, block, first, count):
    head = lax.broadcasted_iota(jnp.int32, (1, count * HEAD), 1) // HEAD
    gain = jnp.zeros((1, count * HEAD), F32)
    for i in range(count):
        gain = jnp.where(head == i, info_ref[5 + block * HEADS + first + i].astype(F32), gain)
    return gain


def inverse_rms(values_f):
    return lax.rsqrt(jnp.mean(values_f * values_f, axis=-1, keepdims=True) + EPSILON)


def softmax(q_pair, k_pair):
    scores = dot_nt(stack_halves(q_pair), k_pair)
    peak = jnp.max(scores, axis=-1, keepdims=True)
    grown = jnp.exp(scores - peak)
    return grown * (1.0 / jnp.sum(grown, axis=-1, keepdims=True))


def picked(rows):
    return jnp.where(rows == lax.broadcasted_iota(jnp.int32, (TOK, TOK), 1), 1.0, 0.0).astype(BF16)


def chunk_row(grid_col, grid_row, row_local, col_local):
    return ((grid_col * 8 + grid_row) * 2 + row_local) * 2 + col_local


def positions():
    return lax.broadcasted_iota(jnp.int32, (TOK, 1), 0)


def chunk_parts():
    row = positions()
    return row // 32, (row // 4) % 8, (row // 2) % 2, row % 2


def row_tokens_of_chunks():
    token = positions()
    return picked(chunk_row((token // 16) % 16, token % 8, token // 256, (token // 8) % 2))


def chunks_of_row_tokens():
    grid_col, grid_row, row_local, col_local = chunk_parts()
    return picked(row_local * 256 + grid_col * 16 + col_local * 8 + grid_row)


def col_tokens_of_chunks():
    token = positions()
    return picked(chunk_row(token % 16, (token // 16) % 8, (token // 128) % 2, token // 256))


def chunks_of_col_tokens():
    grid_col, grid_row, row_local, col_local = chunk_parts()
    return picked(col_local * 256 + row_local * 128 + grid_row * 16 + grid_col)


def copies_of(source, target, sems, count):
    return [pltpu.make_async_copy(source.at[i], target.at[i], sems.at[i]) for i in range(count)]


def start_all(copies):
    for copy in copies:
        copy.start()


def wait_all(copies):
    for copy in copies:
        copy.wait()


def project(normed, qkv_ref, w_ref, copies=()):
    wait_all(copies[0:1])
    qkv_ref[0] = (dot(normed, w_ref[0]).astype(BF16).astype(F32) * SCALE).astype(BF16)
    wait_all(copies[1:2])
    qkv_ref[1] = dot(normed, w_ref[1]).astype(BF16)
    wait_all(copies[2:3])
    qkv_ref[2] = dot(normed, w_ref[2]).astype(BF16)


def each_pair(visit, per_step=2, before=None, after=None):
    def step(index, carry):
        line = index // (N_PAIR // per_step)
        first = lax.rem(index, N_PAIR // per_step) * per_step
        if before is not None:
            before(line)
        rows = pl.ds(pl.multiple_of(line * LINE, LINE), LINE)
        for offset in range(per_step):
            pair = first + offset
            lanes = pl.ds(pl.multiple_of(pair * PAIR, PAIR), PAIR)
            visit(rows, lanes, line * N_PAIR + pair, pair)
        if after is not None:
            after(line)
        return carry

    lax.fori_loop(0, 2 * N_PAIR // per_step, step, 0)


def row_forward_kernel(
    where_ref, x_ref, w_ref, mid_ref, saved_ref,
    w_s, order_s, mid_s, qkv_s, left_s, w_sem, mid_sem, qkv_sem, left_sem,
):
    weights = copies_of(w_ref, w_s, w_sem, 4)
    start_all(weights)
    saved = copies_of(qkv_s, saved_ref, qkv_sem, 3)
    lefts = copies_of(left_s, saved_ref.at[3:5], left_sem, 2)
    order_s[...] = chunks_of_row_tokens()
    for rr in range(2):
        u = x_ref[:, rr].astype(F32).reshape(LINE, D)
        left_s[0, rr * LINE : (rr + 1) * LINE, :] = (u * inverse_rms(u)).astype(BF16)
    project(left_s[0], qkv_s, w_s, weights)
    lefts[0].start()
    start_all(saved)

    def visit(rows, lanes, at, pair):
        probs = softmax(qkv_s[0, rows, lanes], qkv_s[1, rows, lanes]).astype(BF16)
        mixed = pick_halves(dot(probs, qkv_s[2, rows, lanes]))
        left_s[1, rows, lanes] = (mixed * gain_row(where_ref, 0, pair * 2, 2)).astype(BF16)

    each_pair(visit, 4)
    lefts[1].start()
    weights[3].wait()
    added = dot(left_s[1], w_s[3])
    mids = []
    for rr in range(2):
        u = x_ref[:, rr].astype(F32).reshape(LINE, D)
        mids.append((u + added[rr * LINE : (rr + 1) * LINE]).astype(BF16))
    mid = jnp.concatenate(mids, axis=0)
    sends = []
    for part in range(4):
        rows = slice(part * 32, (part + 1) * 32)
        turned = dot(order_s[part * 128 : (part + 1) * 128, :], mid)
        mid_s[rows] = turned.astype(BF16).reshape(32, 4, D)
        sends.append(pltpu.make_async_copy(mid_s.at[rows], mid_ref.at[rows], mid_sem.at[part]))
        sends[-1].start()
    wait_all(saved + lefts + sends)


def row_prepare_kernel(saved_ref, probs_ref, turned_ref):
    def visit(rows, lanes, at, pair):
        probs = softmax(saved_ref[0, rows, lanes], saved_ref[1, rows, lanes])
        probs_ref[at] = probs.astype(BF16)

    each_pair(visit)
    for which in range(2):
        turned_ref[which] = saved_ref[3 + which].T


def attention_backward(rows, lanes, qkv, da_ref, probs, right_ref):
    q_pair, k_pair, v_pair = (qkv[i, rows, lanes] for i in range(3))
    da_pair = da_ref[rows, lanes]
    low = probs.astype(BF16)
    probs = probs.astype(F32)
    grad_probs = dot_nt(stack_halves(da_pair), v_pair)
    total = jnp.sum(probs * grad_probs, axis=-1, keepdims=True)
    grads = (probs * (grad_probs - total)).astype(BF16)
    right_ref[0, rows, lanes] = (pick_halves(dot(grads, k_pair)) * SCALE).astype(BF16)
    right_ref[1, rows, lanes] = pick_halves(dot(turn_halves(grads), q_pair)).astype(BF16)
    right_ref[2, rows, lanes] = pick_halves(dot(turn_halves(low), da_pair)).astype(BF16)
    return low


def input_gradient(u, right_ref, w_s, rows):
    inv = inverse_rms(u)
    dn = (
        dot_nt(right_ref[0, rows, :], w_s[0])
        + dot_nt(right_ref[1, rows, :], w_s[1])
        + dot_nt(right_ref[2, rows, :], w_s[2])
    )
    mean = jnp.mean(dn * u, axis=-1, keepdims=True)
    return right_ref[3, rows, :].astype(F32) + inv * dn - u * (inv * inv * inv * mean)


def weight_gradients(side, turned, right_ref, target):
    for j in range(2):
        which = side * 2 + j
        target[j] = dot(turned[which // 3], right_ref[which]).astype(BF16)


def row_backward_kernel(
    where_ref, g_ref, qkv_ref, turned_ref, probs_ref, w_ref,
    send_ref, right_ref,
    da_s, wo_s, qkv_s, turned_s, probs_s, right_s,
    wo_sem, qkv_sem, turned_sem, probs_sem, grad_sem, right_sem,
):
    weight = pltpu.make_async_copy(w_ref.at[3], wo_s, wo_sem)
    weight.start()
    saved = copies_of(qkv_ref, qkv_s, qkv_sem, 3)
    start_all(saved)
    turned = copies_of(turned_ref, turned_s, turned_sem, 2)

    def line_probs(line):
        pairs = pl.ds(line * N_PAIR, N_PAIR)
        return pltpu.make_async_copy(probs_ref.at[pairs], probs_s.at[pairs], probs_sem.at[line])

    line_probs(0).start()
    right_s[3] = dot(row_tokens_of_chunks(), g_ref[...].reshape(TOK, D)).astype(BF16)
    grad = pltpu.make_async_copy(right_s.at[3], right_ref.at[3], grad_sem)
    grad.start()
    weight.wait()
    gain = gain_row(where_ref, 0, 0, HEADS)
    da_s[...] = (dot_nt(right_s[3], wo_s[...]) * gain).astype(BF16)
    line_probs(1).start()
    start_all(turned)
    wait_all(saved)

    def visit(rows, lanes, at, pair):
        attention_backward(rows, lanes, qkv_s, da_s, probs_s[at], right_s)

    def line_grads(line):
        rows = pl.ds(pl.multiple_of(line * LINE, LINE), LINE)
        return pltpu.make_async_copy(
            right_s.at[0:3, rows], right_ref.at[0:3, rows], right_sem.at[line]
        )

    each_pair(
        visit, 4, lambda line: line_probs(line).wait(), lambda line: line_grads(line).start()
    )
    wait_all(turned)
    weight_gradients(1 - where_ref[4], turned_s, right_s, send_ref)
    wait_all([line_grads(0), line_grads(1), grad])


def kept_gradients_kernel(where_ref, turned_ref, right_ref, keep_ref, turned_s, right_s, turned_sem, right_sem):
    core = where_ref[4]
    turned = copies_of(turned_ref, turned_s, turned_sem, 2)
    rights = copies_of(right_ref.at[pl.ds(core * 2, 2)], right_s, right_sem, 2)
    start_all(turned + rights)
    wait_all(turned + rights)
    for j in range(2):
        keep_ref[j] = dot(turned_s[(core * 2 + j) // 3], right_s[j]).astype(BF16)


def row_input_gradient_kernel(where_ref, x_ref, right_ref, w_ref, *refs):
    outs, w_s, right_s, gin_s, w_sem, right_sem = refs[:8], *refs[8:]
    weights = copies_of(w_ref, w_s, w_sem, 3)
    rights = copies_of(right_ref, right_s, right_sem, 4)
    start_all([copy for pair in zip(weights, rights) for copy in pair] + rights[3:])
    wait_all(weights + rights)
    for rr in range(2):
        rows = slice(rr * LINE, (rr + 1) * LINE)
        u = x_ref[:, rr].astype(F32).reshape(LINE, D)
        grad_in = input_gradient(u, right_s, w_s, rows)
        gin_s[:, :, rr] = grad_in.astype(BF16).reshape(8, 2, 16, D)
    for place in range(8):
        high, x = (where_ref[2] + place // 4) % 2, (where_ref[3] + place % 4) % 4
        outs[place][...] = gin_s[high * 4 + x]


def col_kernel(where_ref, m_ref, w_ref, *refs):
    parts, got_ref, refs = refs[:4], refs[4], refs[5:]
    gmid_ref, saved_ref = refs[:2]
    order_s, u_s, ulow_s, left_s, right_s, qkv_s, da_s = refs[2:9]
    left_sem, right_sem, u_sem = refs[9:]
    mine = where_ref[1]
    rights = copies_of(right_s, saved_ref, right_sem, 4)
    lefts = copies_of(left_s, saved_ref.at[4:6], left_sem, 2)
    order_s[...] = chunks_of_col_tokens()
    u_s[...] = dot(col_tokens_of_chunks(), m_ref[...].reshape(TOK, D))
    u = u_s[...]
    ulow_s[...] = u.astype(BF16)
    kept_u = pltpu.make_async_copy(ulow_s, saved_ref.at[6], u_sem)
    kept_u.start()
    left_s[0] = (u * inverse_rms(u)).astype(BF16)
    lefts[0].start()
    for shift in range(4):
        source = lax.rem(where_ref[0] + (4 - shift), 4) * 2
        for grid_row, piece in ((source + mine, parts[shift].at[mine]), (source + (1 - mine), got_ref.at[shift])):
            for cc in range(2):
                for rr in range(2):
                    at = pl.multiple_of(grid_row * 16 + (cc * LINE + rr * 128), 16)
                    right_s[3, pl.ds(at, 16), :] = piece[cc, rr * 16 : (rr + 1) * 16, :]
    rights[3].start()
    gain = gain_row(where_ref, 1, 0, HEADS)
    da_s[...] = (dot_nt(right_s[3], w_ref[3]) * gain).astype(BF16)
    project(left_s[0], qkv_s, w_ref)

    def visit(rows, lanes, at, pair):
        probs = softmax(qkv_s[0, rows, lanes], qkv_s[1, rows, lanes])
        low = attention_backward(rows, lanes, qkv_s, da_s, probs, right_s)
        mixed = pick_halves(dot(low, qkv_s[2, rows, lanes]))
        left_s[1, rows, lanes] = (mixed * gain_row(where_ref, 1, pair * 2, 2)).astype(BF16)

    each_pair(visit, 4)
    lefts[1].start()
    start_all(rights[:3])
    grads = [
        input_gradient(u_s[rows, :], right_s, w_ref, rows).astype(BF16)
        for rows in (slice(0, LINE), slice(LINE, TOK))
    ]
    gmid_ref[...] = dot(order_s[...], jnp.concatenate(grads, axis=0)).astype(BF16).reshape(N_DEV, 4, D)
    wait_all(lefts + rights + [kept_u])


def col_weights_kernel(where_ref, saved_ref, send_ref, turned_ref, *refs):
    left_s, right_s, turned_s, left_sem, right_sem, turned_sem = refs
    side = 1 - where_ref[4]
    lefts = copies_of(saved_ref.at[4:6], left_s, left_sem, 2)
    rights = copies_of(saved_ref.at[pl.ds(side * 2, 2)], right_s, right_sem, 2)
    start_all(lefts + rights)
    turned = copies_of(turned_s, turned_ref, turned_sem, 2)
    for which in range(2):
        lefts[which].wait()
        turned_s[which] = left_s[which].T
        turned[which].start()
    wait_all(rights)
    for j in range(2):
        send_ref[j] = dot(turned_s[(side * 2 + j) // 3], right_s[j]).astype(BF16)
    wait_all(turned)


def col_output_kernel(where_ref, saved_ref, w_ref, *refs):
    outs, (att_s, ulow_s, wo_s, out_s, sem) = refs[:8], refs[8:]
    copies = [
        pltpu.make_async_copy(saved_ref.at[5], att_s, sem.at[0]),
        pltpu.make_async_copy(w_ref.at[3], wo_s, sem.at[1]),
        pltpu.make_async_copy(saved_ref.at[6], ulow_s, sem.at[2]),
    ]
    start_all(copies)
    wait_all(copies)
    out_s[...] = (ulow_s[...].astype(F32) + dot(att_s[...], wo_s[...])).astype(BF16)
    for shift in range(8):
        y, low = (where_ref[0] + shift % 4) % 4, (where_ref[1] + shift // 4) % 2
        start = (y * 2 + low) * 16
        for cc in range(2):
            for rr in range(2):
                at = pl.multiple_of(start + (cc * LINE + rr * 128), 16)
                outs[shift][cc, rr * 16 : (rr + 1) * 16, :] = out_s[pl.ds(at, 16), :]


def tile_to_lines_kernel(where_ref, tile_ref, *refs):
    outs, mix_s = refs[:4], refs[4]
    tile = tile_ref[...].astype(F32).reshape(TOK, D)
    for group in range(4):
        lanes = slice(group * 128, (group + 1) * 128)
        mix_s[group] = tile[:, lanes]
        for shift in range(4):
            for low in range(2):
                peer = lax.rem(where_ref[0] + shift, 4) * 2 + low
                for cc in range(2):
                    for rr in range(2):
                        piece = mix_s[group, pl.ds(peer + (rr * 16 + cc * 8), 16, stride=32), :]
                        outs[shift][low, cc, rr * 16 : (rr + 1) * 16, lanes] = piece.astype(BF16)


def pass_low_kernel(where_ref, *refs):
    parts, pass_ref = refs[:4], refs[4]
    for shift in range(4):
        pass_ref[shift] = parts[shift][1 - where_ref[1]]


def lines_to_tile_kernel(where_ref, *refs):
    parts, tile_ref = refs[:8], refs[8]
    row = positions()
    y, low = (row // 2) % 4, row % 2
    shift = (where_ref[1] + 2 - low) % 2 * 4 + (where_ref[0] + 4 - y) % 4
    order = picked(((shift * 2 + (row // 8) % 2) * 2 + (row // 16) % 2) * 16 + row // 32)
    lines = jnp.concatenate([part[...].reshape(64, D) for part in parts], axis=0)
    tile_ref[...] = dot(order, lines).astype(BF16).reshape(32, 16, D)


def pass_core_kernel(where_ref, *refs):
    parts, pass_ref = refs[:8], refs[8]
    for shift in range(8):
        pass_ref[shift] = parts[shift][1 - where_ref[4]]


def join_kernel(where_ref, *refs):
    parts, passed_ref, tile_ref = refs[:8], refs[8], refs[9]
    core = where_ref[4]
    for place in range(8):
        high, x = (where_ref[2] + place // 4) % 2, (where_ref[3] + 4 - place % 4) % 4
        tile_ref[high * 4 + x, core] = parts[place][core]
        tile_ref[high * 4 + x, 1 - core] = passed_ref[place]


def pair_sum_kernel(where_ref, keep_ref, got_ref, *refs):
    outs, sum_s = refs[:4], refs[4]
    total = keep_ref[...].astype(F32) + got_ref[...].astype(F32)
    sum_s[...] = total.astype(BF16).reshape(4, 256, D)
    for shift in range(4):
        outs[shift][...] = sum_s[lax.rem(where_ref[3] + shift, 4)]


def merge_kernel(keep_ref, got_ref, *refs):
    quarters, both_ref = refs[:4], refs[4]
    total = keep_ref[...].astype(F32) + got_ref[...].astype(F32)
    rows = total.astype(BF16).reshape(64, 16, D)
    quarter = quarters[0][...].astype(F32)
    for i in range(1, 4):
        quarter = quarter + quarters[i][...].astype(F32)
    quarter = quarter.astype(BF16).reshape(16, 16, D)
    for group in range(4):
        lanes = slice(group * 128, (group + 1) * 128)
        both_ref[:, group * 16 : (group + 1) * 16, :] = rows[:, :, lanes]
        for block in range(16):
            both_ref[block * 4 + group, 64:80, :] = quarter[block, :, lanes]


def chip_sum(parts_ref, rows, first, step):
    total = parts_ref[first, rows, :].astype(F32)
    for chip in range(first + step, 64, step):
        total = total + parts_ref[chip, rows, :].astype(F32)
    return total.astype(BF16)


def spread_kernel(both_ref, spread_ref):
    row_sum = chip_sum(both_ref, slice(0, 64), 0, 1)
    spread_ref[:, 0:64, :] = jnp.broadcast_to(row_sum[None], (64, 64, 128))
    for quarter in range(4):
        part = chip_sum(both_ref, slice(64, 80), quarter, 4)
        first = 64 + quarter * 16
        spread_ref[:, first : first + 16, :] = jnp.broadcast_to(part[None], (64, 16, 128))


def widen_kernel(side, where_ref, chunks_ref, *refs):
    row_ref, col_ref, row_s, col_s, row_sem, col_sem = refs[-6:]
    half = where_ref[4] if side == 0 else 1 - where_ref[4]
    copies = []
    for part in range(4):
        chunks = slice(part * 16, (part + 1) * 16)
        for group in range(4):
            lanes = slice(group * 128, (group + 1) * 128)
            piece = chunks_ref[chunks, group * 16 : (group + 1) * 16, :].astype(F32)
            row_s[part, :, lanes] = piece.reshape(256, 128)
        rows = pl.ds(part * 256, 256)
        copies.append(
            pltpu.make_async_copy(row_s.at[part], row_ref.at[half, rows], row_sem.at[part])
        )
        copies[-1].start()
    for quarter in range(4):
        first = 64 + quarter * 16
        for block in range(16):
            for group in range(4):
                col_s[quarter, block * 16 : (block + 1) * 16, group * 128 : (group + 1) * 128] = (
                    chunks_ref[block * 4 + group, first : first + 16, :].astype(F32)
                )
        copies.append(
            pltpu.make_async_copy(col_s.at[quarter], col_ref.at[half, quarter], col_sem.at[quarter])
        )
        copies[-1].start()
    wait_all(copies)


MIB = 1 << 20
SMEM = pl.BlockSpec(memory_space=pltpu.SMEM)
VMEM = pl.BlockSpec(memory_space=pltpu.VMEM)
HBM = pl.BlockSpec(memory_space=pltpu.HBM)


SPACE = {"s": SMEM, "v": VMEM, "h": HBM}


def call(kernel, ins, out_kinds, outs, scratch, flops, moved, grant=16):
    spaces = tuple(SPACE[kind] for kind in out_kinds)
    return pl.pallas_call(
        kernel,
        in_specs=[SPACE[kind] for kind in ins],
        out_specs=spaces if isinstance(outs, tuple) else spaces[0],
        out_shape=outs,
        scratch_shapes=scratch,
        compiler_params=pltpu.CompilerParams(vmem_limit_bytes=grant * MIB),
        cost_estimate=pl.CostEstimate(flops=flops, bytes_accessed=moved, transcendentals=0),
    )


def shape(*dims, dtype=BF16):
    return jax.ShapeDtypeStruct(dims, dtype)


MATMUL = 2 * TOK * D * D
ATTEND = 2 * 16 * LINE * LINE * HEAD
MIX_TILE = pltpu.VMEM((4, TOK, 128), F32)
DMA = pltpu.SemaphoreType.DMA
WEIGHTS = [pltpu.VMEM((4, D, D), BF16), DMA((4,))]
WEIGHT = [pltpu.VMEM((D, D), BF16), DMA]
LINES = shape(2, 32, D)
PIECE = shape(2, 2, 32, D)
PASS = shape(4, 2, 32, D)
QUARTER = shape(256, D)
HALF = shape(2, D, D)


def token_scratch(*lead, dtype=BF16):
    return pltpu.VMEM((*lead, TOK, D), dtype)


row_forward = call(
    row_forward_kernel,
    "svh",
    "hh",
    (shape(N_DEV, 4, D), shape(5, TOK, D)),
    [
        WEIGHTS[0], token_scratch(), pltpu.VMEM((N_DEV, 4, D), BF16), token_scratch(3),
        token_scratch(2), WEIGHTS[1],
        DMA((4,)), DMA((3,)), DMA((2,)),
    ],
    4 * MATMUL + 2 * ATTEND,
    6 * MIB,
    grant=51,
)
row_prepare = call(
    row_prepare_kernel, "v", "vv", (shape(8, TOK, LINE), shape(2, D, TOK)), [], ATTEND, 8 * MIB
)
row_backward = call(
    row_backward_kernel,
    "svhhhh",
    "vh",
    (HALF, shape(4, TOK, D)),
    [
        token_scratch(), pltpu.VMEM((D, D), BF16), token_scratch(3),
        pltpu.VMEM((2, D, TOK), BF16), pltpu.VMEM((8, TOK, LINE), BF16),
        token_scratch(4), DMA, DMA((3,)), DMA((2,)), DMA((2,)), DMA, DMA((2,)),
    ],
    5 * MATMUL + 5 * ATTEND,
    12 * MIB,
    grant=50,
)
kept_gradients = call(
    kept_gradients_kernel,
    "shh",
    "v",
    HALF,
    [pltpu.VMEM((2, D, TOK), BF16), token_scratch(2), DMA((2,)), DMA((2,))],
    2 * MATMUL,
    3 * MIB,
    grant=50,
)
row_input_gradient = call(
    row_input_gradient_kernel,
    "svhh",
    "v" * 8,
    (shape(2, 2, 16, D),) * 8,
    [
        pltpu.VMEM((3, D, D), BF16), token_scratch(4), pltpu.VMEM((8, 2, 2, 16, D), BF16),
        DMA((3,)), DMA((4,)),
    ],
    3 * MATMUL,
    5 * MIB,
    grant=51,
)
col_grad = call(
    col_kernel,
    "svv" + "v" * 5,
    "vh",
    (shape(N_DEV, 4, D), shape(7, TOK, D)),
    [
        token_scratch(), token_scratch(dtype=F32), token_scratch(), token_scratch(2), token_scratch(4),
        token_scratch(3), token_scratch(), DMA((2,)), DMA((4,)), DMA,
    ],
    8 * MATMUL + 6 * ATTEND,
    8 * MIB,
    grant=50,
)
col_weights = call(
    col_weights_kernel,
    "sh",
    "vh",
    (HALF, shape(2, D, TOK)),
    [
        token_scratch(2), token_scratch(2), pltpu.VMEM((2, D, TOK), BF16),
        DMA((2,)), DMA((2,)), DMA((2,)),
    ],
    2 * MATMUL,
    6 * MIB,
    grant=50,
)
col_output = call(
    col_output_kernel,
    "shh",
    "v" * 8,
    (LINES,) * 8,
    [token_scratch(), token_scratch(), pltpu.VMEM((D, D), BF16), token_scratch(), DMA((3,))],
    MATMUL,
    3 * MIB,
    grant=52,
)
tile_to_lines = call(
    tile_to_lines_kernel, "sv", "v" * 4, (PIECE,) * 4, [MIX_TILE], 0, MIB, grant=48
)
pass_low = call(pass_low_kernel, "s" + "v" * 4, "v", PASS, [], 0, MIB, grant=12)
lines_to_tile = call(
    lines_to_tile_kernel, "s" + "v" * 8, "v", shape(32, 16, D), [], MATMUL, MIB, grant=48
)
CORE_PASS = shape(8, 2, 16, D)
pass_core = call(pass_core_kernel, "s" + "v" * 8, "v", CORE_PASS, [], 0, MIB, grant=40)
join = call(join_kernel, "s" + "v" * 9, "v", shape(8, 2, 2, 16, D), [], 0, MIB)
pair_sum = call(
    pair_sum_kernel, "svv", "v" * 4, (QUARTER,) * 4, [pltpu.VMEM((4, 256, D), BF16)], 0, 3 * MIB,
)
merge = call(merge_kernel, "v" * 6, "v", shape(64, 80, 128), [], 0, 4 * MIB, grant=32)
spread = call(spread_kernel, "v", "v", shape(64, 128, 128), [], 0, 3 * MIB, grant=52)


def widen(where, chunks, side, *before):
    return pl.pallas_call(
        functools.partial(widen_kernel, side),
        in_specs=[SMEM, VMEM] + [HBM] * len(before),
        out_specs=(HBM, HBM),
        out_shape=(shape(2, 1024, D, dtype=F32), shape(2, 4, 256, D, dtype=F32)),
        scratch_shapes=[
            pltpu.VMEM((4, 256, D), F32), pltpu.VMEM((4, 256, D), F32), DMA((4,)), DMA((4,)),
        ],
        input_output_aliases={2: 0, 3: 1} if before else {},
        name="widen",
        compiler_params=pltpu.CompilerParams(vmem_limit_bytes=16 * MIB),
        cost_estimate=pl.CostEstimate(flops=0, bytes_accessed=6 * MIB, transcendentals=0),
    )(where, chunks, *before)


def exchange(values, axes):
    return lax.all_to_all(values, axes, split_axis=0, concat_axis=0, tiled=True)


def shifted(pieces, axis):
    n = len(pieces)
    return [pieces[0]] + [
        lax.ppermute(pieces[k], axis, [(i, (i + k) % n) for i in range(n)]) for k in range(1, n)
    ]


def moved(pieces, axes, sizes, long_axis):
    peers = []
    for place in range(1, 8):
        steps = (place % 4, place // 4) if long_axis == 0 else (place // 4, place % 4)
        peers.append(
            [
                (i * sizes[1] + j, (i + steps[0]) % sizes[0] * sizes[1] + (j + steps[1]) % sizes[1])
                for i in range(sizes[0])
                for j in range(sizes[1])
            ]
        )
    return [pieces[0]] + [lax.ppermute(pieces[k + 1], axes, peers[k]) for k in range(7)]


def swap(value, axis):
    return lax.ppermute(value, axis, [(0, 1), (1, 0)])


def layer(latents, cotangent, w_row, w_col, keep_heads):
    where = jnp.concatenate(
        [jnp.stack([lax.axis_index(name) for name in AXES]), keep_heads.reshape(-1)]
    ).astype(jnp.int32)
    rows_in = exchange(latents.reshape(16, 2, 16, D), COL)
    grad_pieces = tile_to_lines(where, cotangent)
    grad_parts = shifted(grad_pieces, "y")
    grad_pass = pass_low(where, *grad_parts)
    grad_pass = swap(grad_pass, "zl")
    mid_send, saved_row = row_forward(where, rows_in, w_row)
    mid_lines = exchange(mid_send, BOTH)
    probs_row, turned_row = row_prepare(saved_row)
    grad_send, saved_col = col_grad(
        where, mid_lines, w_col, *grad_parts, grad_pass
    )
    grad_rows = exchange(grad_send, BOTH)
    send_col, turned_col = col_weights(where, saved_col)
    got_col = swap(send_col, "c")
    keep_col = kept_gradients(where, turned_col, saved_col)
    quarters = pair_sum(where, keep_col, got_col)
    quarters = shifted(quarters, "x")
    send_row, right_row = row_backward(where, grad_rows, saved_row, turned_row, probs_row, w_row)
    got_row = swap(send_row, "c")
    keep_row = kept_gradients(where, turned_row, right_row)
    merged = merge(keep_row, got_row, *quarters)
    both = exchange(merged, CHIPS)
    totals = spread(both)
    chunks = exchange(totals, CHIPS)
    gin_pieces = row_input_gradient(where, rows_in, right_row, w_row)
    gin_parts = moved(gin_pieces, ("zh", "x"), (2, 4), 1)
    gin_core = pass_core(where, *gin_parts)
    gin_core = swap(gin_core, "c")
    grad_latents = join(where, *gin_parts, gin_core).reshape(32, 16, D)
    out_pieces = col_output(where, saved_col, w_col)
    out_parts = moved(out_pieces, ROW, (4, 2), 0)
    output = lines_to_tile(where, *out_parts)
    other = swap(chunks, "c")
    halves_done = widen(where, chunks, 0)
    grad_row, grad_col = widen(where, other, 1, *halves_done)
    return (output, grad_latents, grad_row.reshape(4, D, D), grad_col.reshape(4, D, D))


def solution(mesh):
    fine = Mesh(mesh.devices.reshape(4, 2, 2, 4, 2), AXES)
    tile = P(ROW, COL, None)
    return jax.shard_map(
        layer,
        mesh=fine,
        in_specs=(tile, tile, P(), P(), P()),
        out_specs=(tile, tile, P(), P()),
        check_vma=False,
    )
```

```python
import functools

import jax
import jax.numpy as jnp
from jax import lax
from jax.experimental import pallas as pl
from jax.experimental.pallas import tpu as pltpu
from jax.sharding import Mesh, PartitionSpec as P


HEADS = 8
HEAD = 64
D = 512
PAIR = 128
N_PAIR = D // PAIR
LINE = 256
TOK = 512
N_ROW = 8
N_COL = 16
N_DEV = N_ROW * N_COL
EPSILON = 1e-06
SCALE = HEAD ** (-0.5)

F32 = jnp.float32
BF16 = jnp.bfloat16

AXES = ("y", "zl", "zh", "x", "c")
ROW = ("y", "zl")
COL = ("zh", "x", "c")
BOTH = COL + ROW
CHIPS = ("y", "zl", "zh", "x")


def dot(left, right):
    return lax.dot_general(left, right, (((1,), (0,)), ((), ())), preferred_element_type=F32)


def dot_nt(left, right):
    return lax.dot_general(left, right, (((1,), (1,)), ((), ())), preferred_element_type=F32)


def stack_halves(value):
    lane = lax.broadcasted_iota(jnp.int32, value.shape, 1)
    zero = jnp.zeros_like(value)
    low, high = jnp.where(lane < HEAD, value, zero), jnp.where(lane >= HEAD, value, zero)
    return jnp.concatenate([low, high], axis=0)


def pick_halves(value):
    low, high = value[:LINE], value[LINE:]
    lane = lax.broadcasted_iota(jnp.int32, low.shape, 1)
    return jnp.where(lane < HEAD, low, high)


def turn_halves(value):
    return jnp.concatenate([value[:LINE].T, value[LINE:].T], axis=0)


def gain_row(info_ref, block, first, count):
    head = lax.broadcasted_iota(jnp.int32, (1, count * HEAD), 1) // HEAD
    gain = jnp.zeros((1, count * HEAD), F32)
    for i in range(count):
        gain = jnp.where(head == i, info_ref[5 + block * HEADS + first + i].astype(F32), gain)
    return gain


def inverse_rms(values_f):
    return lax.rsqrt(jnp.mean(values_f * values_f, axis=-1, keepdims=True) + EPSILON)


def softmax(q_pair, k_pair):
    scores = dot_nt(stack_halves(q_pair), k_pair)
    peak = jnp.max(scores, axis=-1, keepdims=True)
    grown = jnp.exp(scores - peak)
    return grown * (1.0 / jnp.sum(grown, axis=-1, keepdims=True))


def picked(rows):
    return jnp.where(rows == lax.broadcasted_iota(jnp.int32, (TOK, TOK), 1), 1.0, 0.0).astype(BF16)


def chunk_row(grid_col, grid_row, row_local, col_local):
    return ((grid_col * 8 + grid_row) * 2 + row_local) * 2 + col_local


def positions():
    return lax.broadcasted_iota(jnp.int32, (TOK, 1), 0)


def chunk_parts():
    row = positions()
    return row // 32, (row // 4) % 8, (row // 2) % 2, row % 2


def row_tokens_of_chunks():
    token = positions()
    return picked(chunk_row((token // 16) % 16, token % 8, token // 256, (token // 8) % 2))


def chunks_of_row_tokens():
    grid_col, grid_row, row_local, col_local = chunk_parts()
    return picked(row_local * 256 + grid_col * 16 + col_local * 8 + grid_row)


def col_tokens_of_chunks():
    token = positions()
    return picked(chunk_row(token % 16, (token // 16) % 8, (token // 128) % 2, token // 256))


def chunks_of_col_tokens():
    grid_col, grid_row, row_local, col_local = chunk_parts()
    return picked(col_local * 256 + row_local * 128 + grid_row * 16 + grid_col)


def copies_of(source, target, sems, count):
    return [pltpu.make_async_copy(source.at[i], target.at[i], sems.at[i]) for i in range(count)]


def start_all(copies):
    for copy in copies:
        copy.start()


def wait_all(copies):
    for copy in copies:
        copy.wait()


def project(normed, qkv_ref, w_ref, copies=()):
    wait_all(copies[0:1])
    qkv_ref[0] = (dot(normed, w_ref[0]).astype(BF16).astype(F32) * SCALE).astype(BF16)
    wait_all(copies[1:2])
    qkv_ref[1] = dot(normed, w_ref[1]).astype(BF16)
    wait_all(copies[2:3])
    qkv_ref[2] = dot(normed, w_ref[2]).astype(BF16)


def each_pair(visit, per_step=2, before=None, after=None):
    def step(index, carry):
        line = index // (N_PAIR // per_step)
        first = lax.rem(index, N_PAIR // per_step) * per_step
        if before is not None:
            before(line)
        rows = pl.ds(pl.multiple_of(line * LINE, LINE), LINE)
        for offset in range(per_step):
            pair = first + offset
            lanes = pl.ds(pl.multiple_of(pair * PAIR, PAIR), PAIR)
            visit(rows, lanes, line * N_PAIR + pair, pair)
        if after is not None:
            after(line)
        return carry

    lax.fori_loop(0, 2 * N_PAIR // per_step, step, 0)


def row_forward_kernel(
    where_ref, x_ref, w_ref, mid_ref, saved_ref,
    w_s, order_s, mid_s, qkv_s, left_s, w_sem, mid_sem, qkv_sem, left_sem,
):
    weights = copies_of(w_ref, w_s, w_sem, 4)
    start_all(weights)
    saved = copies_of(qkv_s, saved_ref, qkv_sem, 3)
    lefts = copies_of(left_s, saved_ref.at[3:5], left_sem, 2)
    order_s[...] = chunks_of_row_tokens()
    for rr in range(2):
        u = x_ref[:, rr].astype(F32).reshape(LINE, D)
        left_s[0, rr * LINE : (rr + 1) * LINE, :] = (u * inverse_rms(u)).astype(BF16)
    project(left_s[0], qkv_s, w_s, weights)
    lefts[0].start()
    start_all(saved)

    def visit(rows, lanes, at, pair):
        probs = softmax(qkv_s[0, rows, lanes], qkv_s[1, rows, lanes]).astype(BF16)
        mixed = pick_halves(dot(probs, qkv_s[2, rows, lanes]))
        left_s[1, rows, lanes] = (mixed * gain_row(where_ref, 0, pair * 2, 2)).astype(BF16)

    each_pair(visit, 4)
    lefts[1].start()
    weights[3].wait()
    added = dot(left_s[1], w_s[3])
    mids = []
    for rr in range(2):
        u = x_ref[:, rr].astype(F32).reshape(LINE, D)
        mids.append((u + added[rr * LINE : (rr + 1) * LINE]).astype(BF16))
    mid = jnp.concatenate(mids, axis=0)
    sends = []
    for part in range(4):
        rows = slice(part * 32, (part + 1) * 32)
        turned = dot(order_s[part * 128 : (part + 1) * 128, :], mid)
        mid_s[rows] = turned.astype(BF16).reshape(32, 4, D)
        sends.append(pltpu.make_async_copy(mid_s.at[rows], mid_ref.at[rows], mid_sem.at[part]))
        sends[-1].start()
    wait_all(saved + lefts + sends)


def row_prepare_kernel(saved_ref, probs_ref, turned_ref):
    def visit(rows, lanes, at, pair):
        probs = softmax(saved_ref[0, rows, lanes], saved_ref[1, rows, lanes])
        probs_ref[at] = probs.astype(BF16)

    each_pair(visit)
    for which in range(2):
        turned_ref[which] = saved_ref[3 + which].T


def attention_backward(rows, lanes, qkv, da_ref, probs, right_ref):
    q_pair, k_pair, v_pair = (qkv[i, rows, lanes] for i in range(3))
    da_pair = da_ref[rows, lanes]
    low = probs.astype(BF16)
    probs = probs.astype(F32)
    grad_probs = dot_nt(stack_halves(da_pair), v_pair)
    total = jnp.sum(probs * grad_probs, axis=-1, keepdims=True)
    grads = (probs * (grad_probs - total)).astype(BF16)
    right_ref[0, rows, lanes] = (pick_halves(dot(grads, k_pair)) * SCALE).astype(BF16)
    right_ref[1, rows, lanes] = pick_halves(dot(turn_halves(grads), q_pair)).astype(BF16)
    right_ref[2, rows, lanes] = pick_halves(dot(turn_halves(low), da_pair)).astype(BF16)
    return low


def input_gradient(u, right_ref, w_s, rows):
    inv = inverse_rms(u)
    dn = (
        dot_nt(right_ref[0, rows, :], w_s[0])
        + dot_nt(right_ref[1, rows, :], w_s[1])
        + dot_nt(right_ref[2, rows, :], w_s[2])
    )
    mean = jnp.mean(dn * u, axis=-1, keepdims=True)
    return right_ref[3, rows, :].astype(F32) + inv * dn - u * (inv * inv * inv * mean)


def weight_gradients(side, turned, right_ref, target):
    for j in range(2):
        which = side * 2 + j
        target[j] = dot(turned[which // 3], right_ref[which]).astype(BF16)


def row_backward_kernel(
    where_ref, g_ref, qkv_ref, turned_ref, probs_ref, w_ref,
    send_ref, right_ref,
    da_s, wo_s, qkv_s, turned_s, probs_s, right_s,
    wo_sem, qkv_sem, turned_sem, probs_sem, grad_sem, right_sem,
):
    weight = pltpu.make_async_copy(w_ref.at[3], wo_s, wo_sem)
    weight.start()
    saved = copies_of(qkv_ref, qkv_s, qkv_sem, 3)
    start_all(saved)
    turned = copies_of(turned_ref, turned_s, turned_sem, 2)

    def line_probs(line):
        pairs = pl.ds(line * N_PAIR, N_PAIR)
        return pltpu.make_async_copy(probs_ref.at[pairs], probs_s.at[pairs], probs_sem.at[line])

    line_probs(0).start()
    right_s[3] = dot(row_tokens_of_chunks(), g_ref[...].reshape(TOK, D)).astype(BF16)
    grad = pltpu.make_async_copy(right_s.at[3], right_ref.at[3], grad_sem)
    grad.start()
    weight.wait()
    gain = gain_row(where_ref, 0, 0, HEADS)
    da_s[...] = (dot_nt(right_s[3], wo_s[...]) * gain).astype(BF16)
    line_probs(1).start()
    start_all(turned)
    wait_all(saved)

    def visit(rows, lanes, at, pair):
        attention_backward(rows, lanes, qkv_s, da_s, probs_s[at], right_s)

    def line_grads(line):
        rows = pl.ds(pl.multiple_of(line * LINE, LINE), LINE)
        return pltpu.make_async_copy(
            right_s.at[0:3, rows], right_ref.at[0:3, rows], right_sem.at[line]
        )

    each_pair(
        visit, 4, lambda line: line_probs(line).wait(), lambda line: line_grads(line).start()
    )
    wait_all(turned)
    weight_gradients(1 - where_ref[4], turned_s, right_s, send_ref)
    wait_all([line_grads(0), line_grads(1), grad])


def kept_gradients_kernel(where_ref, turned_ref, right_ref, keep_ref, turned_s, right_s, turned_sem, right_sem):
    core = where_ref[4]
    turned = copies_of(turned_ref, turned_s, turned_sem, 2)
    rights = copies_of(right_ref.at[pl.ds(core * 2, 2)], right_s, right_sem, 2)
    start_all(turned + rights)
    wait_all(turned + rights)
    for j in range(2):
        keep_ref[j] = dot(turned_s[(core * 2 + j) // 3], right_s[j]).astype(BF16)


def row_input_gradient_kernel(where_ref, x_ref, right_ref, w_ref, *refs):
    outs, w_s, right_s, gin_s, w_sem, right_sem = refs[:4], *refs[4:]
    weights = copies_of(w_ref, w_s, w_sem, 3)
    rights = copies_of(right_ref, right_s, right_sem, 4)
    start_all([copy for pair in zip(weights, rights) for copy in pair] + rights[3:])
    wait_all(weights + rights)
    for rr in range(2):
        rows = slice(rr * LINE, (rr + 1) * LINE)
        u = x_ref[:, rr].astype(F32).reshape(LINE, D)
        grad_in = input_gradient(u, right_s, w_s, rows)
        gin_s[:, :, rr] = grad_in.astype(BF16).reshape(8, 2, 16, D)
    for shift in range(4):
        for high in range(2):
            outs[shift][high] = gin_s[high * 4 + (where_ref[3] + shift) % 4]


def col_kernel(where_ref, m_ref, w_ref, *refs):
    parts, got_ref, refs = refs[:4], refs[4], refs[5:]
    gmid_ref, saved_ref = refs[:2]
    order_s, u_s, ulow_s, left_s, right_s, qkv_s, da_s = refs[2:9]
    left_sem, right_sem, u_sem = refs[9:]
    mine = where_ref[1]
    rights = copies_of(right_s, saved_ref, right_sem, 4)
    lefts = copies_of(left_s, saved_ref.at[4:6], left_sem, 2)
    order_s[...] = chunks_of_col_tokens()
    u_s[...] = dot(col_tokens_of_chunks(), m_ref[...].reshape(TOK, D))
    u = u_s[...]
    ulow_s[...] = u.astype(BF16)
    kept_u = pltpu.make_async_copy(ulow_s, saved_ref.at[6], u_sem)
    kept_u.start()
    left_s[0] = (u * inverse_rms(u)).astype(BF16)
    lefts[0].start()
    for shift in range(4):
        source = lax.rem(where_ref[0] + (4 - shift), 4) * 2
        for grid_row, piece in ((source + mine, parts[shift].at[mine]), (source + (1 - mine), got_ref.at[shift])):
            for cc in range(2):
                for rr in range(2):
                    at = pl.multiple_of(grid_row * 16 + (cc * LINE + rr * 128), 16)
                    right_s[3, pl.ds(at, 16), :] = piece[cc, rr * 16 : (rr + 1) * 16, :]
    rights[3].start()
    gain = gain_row(where_ref, 1, 0, HEADS)
    da_s[...] = (dot_nt(right_s[3], w_ref[3]) * gain).astype(BF16)
    project(left_s[0], qkv_s, w_ref)

    def visit(rows, lanes, at, pair):
        probs = softmax(qkv_s[0, rows, lanes], qkv_s[1, rows, lanes])
        low = attention_backward(rows, lanes, qkv_s, da_s, probs, right_s)
        mixed = pick_halves(dot(low, qkv_s[2, rows, lanes]))
        left_s[1, rows, lanes] = (mixed * gain_row(where_ref, 1, pair * 2, 2)).astype(BF16)

    each_pair(visit, 4)
    lefts[1].start()
    start_all(rights[:3])
    grads = [
        input_gradient(u_s[rows, :], right_s, w_ref, rows).astype(BF16)
        for rows in (slice(0, LINE), slice(LINE, TOK))
    ]
    gmid_ref[...] = dot(order_s[...], jnp.concatenate(grads, axis=0)).astype(BF16).reshape(N_DEV, 4, D)
    wait_all(lefts + rights + [kept_u])


def col_weights_kernel(where_ref, saved_ref, send_ref, turned_ref, *refs):
    left_s, right_s, turned_s, left_sem, right_sem, turned_sem = refs
    side = 1 - where_ref[4]
    lefts = copies_of(saved_ref.at[4:6], left_s, left_sem, 2)
    rights = copies_of(saved_ref.at[pl.ds(side * 2, 2)], right_s, right_sem, 2)
    start_all(lefts + rights)
    turned = copies_of(turned_s, turned_ref, turned_sem, 2)
    for which in range(2):
        lefts[which].wait()
        turned_s[which] = left_s[which].T
        turned[which].start()
    wait_all(rights)
    for j in range(2):
        send_ref[j] = dot(turned_s[(side * 2 + j) // 3], right_s[j]).astype(BF16)
    wait_all(turned)


def col_output_kernel(where_ref, saved_ref, w_ref, *refs):
    outs, (att_s, ulow_s, wo_s, out_s, sem) = refs[:8], refs[8:]
    copies = [
        pltpu.make_async_copy(saved_ref.at[5], att_s, sem.at[0]),
        pltpu.make_async_copy(w_ref.at[3], wo_s, sem.at[1]),
        pltpu.make_async_copy(saved_ref.at[6], ulow_s, sem.at[2]),
    ]
    start_all(copies)
    wait_all(copies)
    out_s[...] = (ulow_s[...].astype(F32) + dot(att_s[...], wo_s[...])).astype(BF16)
    for shift in range(8):
        y, low = (where_ref[0] + shift % 4) % 4, (where_ref[1] + shift // 4) % 2
        start = (y * 2 + low) * 16
        for cc in range(2):
            for rr in range(2):
                at = pl.multiple_of(start + (cc * LINE + rr * 128), 16)
                outs[shift][cc, rr * 16 : (rr + 1) * 16, :] = out_s[pl.ds(at, 16), :]


def tile_to_lines_kernel(where_ref, tile_ref, *refs):
    outs, mix_s = refs[:4], refs[4]
    tile = tile_ref[...].astype(F32).reshape(TOK, D)
    for group in range(4):
        lanes = slice(group * 128, (group + 1) * 128)
        mix_s[group] = tile[:, lanes]
        for shift in range(4):
            for low in range(2):
                peer = lax.rem(where_ref[0] + shift, 4) * 2 + low
                for cc in range(2):
                    for rr in range(2):
                        piece = mix_s[group, pl.ds(peer + (rr * 16 + cc * 8), 16, stride=32), :]
                        outs[shift][low, cc, rr * 16 : (rr + 1) * 16, lanes] = piece.astype(BF16)


def pass_low_kernel(where_ref, *refs):
    parts, pass_ref = refs[:4], refs[4]
    for shift in range(4):
        pass_ref[shift] = parts[shift][1 - where_ref[1]]


def lines_to_tile_kernel(where_ref, *refs):
    parts, tile_ref = refs[:8], refs[8]
    row = positions()
    y, low = (row // 2) % 4, row % 2
    shift = (where_ref[1] + 2 - low) % 2 * 4 + (where_ref[0] + 4 - y) % 4
    order = picked(((shift * 2 + (row // 8) % 2) * 2 + (row // 16) % 2) * 16 + row // 32)
    lines = jnp.concatenate([part[...].reshape(64, D) for part in parts], axis=0)
    tile_ref[...] = dot(order, lines).astype(BF16).reshape(32, 16, D)


def pass_high_kernel(where_ref, *refs):
    parts, pass_ref = refs[:4], refs[4]
    for shift in range(4):
        pass_ref[shift] = parts[shift][1 - where_ref[2]]


def pass_core_kernel(where_ref, *refs):
    parts, got_ref, pass_ref = refs[:4], refs[4], refs[5]
    high, other = where_ref[2], 1 - where_ref[4]
    for shift in range(4):
        pass_ref[0, shift] = parts[shift][high, other]
        pass_ref[1, shift] = got_ref[shift, other]


def join_kernel(where_ref, *refs):
    parts, got_ref, passed_ref, tile_ref = refs[:4], refs[4], refs[5], refs[6]
    high, core = where_ref[2], where_ref[4]
    for shift in range(4):
        source = (where_ref[3] + 4 - shift) % 4
        tile_ref[high, source, core] = parts[shift][high, core]
        tile_ref[1 - high, source, core] = got_ref[shift, core]
        tile_ref[high, source, 1 - core] = passed_ref[0, shift]
        tile_ref[1 - high, source, 1 - core] = passed_ref[1, shift]


def pair_sum_kernel(where_ref, keep_ref, got_ref, *refs):
    outs, sum_s = refs[:4], refs[4]
    total = keep_ref[...].astype(F32) + got_ref[...].astype(F32)
    sum_s[...] = total.astype(BF16).reshape(4, 256, D)
    for shift in range(4):
        outs[shift][...] = sum_s[lax.rem(where_ref[3] + shift, 4)]


def merge_kernel(keep_ref, got_ref, *refs):
    quarters, both_ref = refs[:4], refs[4]
    total = keep_ref[...].astype(F32) + got_ref[...].astype(F32)
    rows = total.astype(BF16).reshape(64, 16, D)
    quarter = quarters[0][...].astype(F32)
    for i in range(1, 4):
        quarter = quarter + quarters[i][...].astype(F32)
    quarter = quarter.astype(BF16).reshape(16, 16, D)
    for group in range(4):
        lanes = slice(group * 128, (group + 1) * 128)
        both_ref[:, group * 16 : (group + 1) * 16, :] = rows[:, :, lanes]
        for block in range(16):
            both_ref[block * 4 + group, 64:80, :] = quarter[block, :, lanes]


def chip_sum(parts_ref, rows, first, step):
    total = parts_ref[first, rows, :].astype(F32)
    for chip in range(first + step, 64, step):
        total = total + parts_ref[chip, rows, :].astype(F32)
    return total.astype(BF16)


def spread_kernel(both_ref, spread_ref):
    row_sum = chip_sum(both_ref, slice(0, 64), 0, 1)
    spread_ref[:, 0:64, :] = jnp.broadcast_to(row_sum[None], (64, 64, 128))
    for quarter in range(4):
        part = chip_sum(both_ref, slice(64, 80), quarter, 4)
        first = 64 + quarter * 16
        spread_ref[:, first : first + 16, :] = jnp.broadcast_to(part[None], (64, 16, 128))


def widen_kernel(side, where_ref, chunks_ref, *refs):
    row_ref, col_ref, row_s, col_s, row_sem, col_sem = refs[-6:]
    half = where_ref[4] if side == 0 else 1 - where_ref[4]
    copies = []
    for part in range(4):
        chunks = slice(part * 16, (part + 1) * 16)
        for group in range(4):
            lanes = slice(group * 128, (group + 1) * 128)
            piece = chunks_ref[chunks, group * 16 : (group + 1) * 16, :].astype(F32)
            row_s[part, :, lanes] = piece.reshape(256, 128)
        rows = pl.ds(part * 256, 256)
        copies.append(
            pltpu.make_async_copy(row_s.at[part], row_ref.at[half, rows], row_sem.at[part])
        )
        copies[-1].start()
    for quarter in range(4):
        first = 64 + quarter * 16
        for block in range(16):
            for group in range(4):
                col_s[quarter, block * 16 : (block + 1) * 16, group * 128 : (group + 1) * 128] = (
                    chunks_ref[block * 4 + group, first : first + 16, :].astype(F32)
                )
        copies.append(
            pltpu.make_async_copy(col_s.at[quarter], col_ref.at[half, quarter], col_sem.at[quarter])
        )
        copies[-1].start()
    wait_all(copies)


MIB = 1 << 20
SMEM = pl.BlockSpec(memory_space=pltpu.SMEM)
VMEM = pl.BlockSpec(memory_space=pltpu.VMEM)
HBM = pl.BlockSpec(memory_space=pltpu.HBM)


SPACE = {"s": SMEM, "v": VMEM, "h": HBM}


def call(kernel, ins, out_kinds, outs, scratch, flops, moved, grant=16):
    spaces = tuple(SPACE[kind] for kind in out_kinds)
    return pl.pallas_call(
        kernel,
        in_specs=[SPACE[kind] for kind in ins],
        out_specs=spaces if isinstance(outs, tuple) else spaces[0],
        out_shape=outs,
        scratch_shapes=scratch,
        compiler_params=pltpu.CompilerParams(vmem_limit_bytes=grant * MIB),
        cost_estimate=pl.CostEstimate(flops=flops, bytes_accessed=moved, transcendentals=0),
    )


def shape(*dims, dtype=BF16):
    return jax.ShapeDtypeStruct(dims, dtype)


MATMUL = 2 * TOK * D * D
ATTEND = 2 * 16 * LINE * LINE * HEAD
MIX_TILE = pltpu.VMEM((4, TOK, 128), F32)
DMA = pltpu.SemaphoreType.DMA
WEIGHTS = [pltpu.VMEM((4, D, D), BF16), DMA((4,))]
WEIGHT = [pltpu.VMEM((D, D), BF16), DMA]
LINES = shape(2, 32, D)
PIECE = shape(2, 2, 32, D)
PASS = shape(4, 2, 32, D)
QUARTER = shape(256, D)
HALF = shape(2, D, D)


def token_scratch(*lead, dtype=BF16):
    return pltpu.VMEM((*lead, TOK, D), dtype)


row_forward = call(
    row_forward_kernel,
    "svh",
    "hh",
    (shape(N_DEV, 4, D), shape(5, TOK, D)),
    [
        WEIGHTS[0], token_scratch(), pltpu.VMEM((N_DEV, 4, D), BF16), token_scratch(3),
        token_scratch(2), WEIGHTS[1],
        DMA((4,)), DMA((3,)), DMA((2,)),
    ],
    4 * MATMUL + 2 * ATTEND,
    6 * MIB,
    grant=51,
)
row_prepare = call(
    row_prepare_kernel, "v", "vv", (shape(8, TOK, LINE), shape(2, D, TOK)), [], ATTEND, 8 * MIB
)
row_backward = call(
    row_backward_kernel,
    "svhhhh",
    "vh",
    (HALF, shape(4, TOK, D)),
    [
        token_scratch(), pltpu.VMEM((D, D), BF16), token_scratch(3),
        pltpu.VMEM((2, D, TOK), BF16), pltpu.VMEM((8, TOK, LINE), BF16),
        token_scratch(4), DMA, DMA((3,)), DMA((2,)), DMA((2,)), DMA, DMA((2,)),
    ],
    5 * MATMUL + 5 * ATTEND,
    12 * MIB,
    grant=50,
)
kept_gradients = call(
    kept_gradients_kernel,
    "shh",
    "v",
    HALF,
    [pltpu.VMEM((2, D, TOK), BF16), token_scratch(2), DMA((2,)), DMA((2,))],
    2 * MATMUL,
    3 * MIB,
    grant=50,
)
row_input_gradient = call(
    row_input_gradient_kernel,
    "svhh",
    "v" * 4,
    (shape(2, 2, 2, 16, D),) * 4,
    [
        pltpu.VMEM((3, D, D), BF16), token_scratch(4), pltpu.VMEM((8, 2, 2, 16, D), BF16),
        DMA((3,)), DMA((4,)),
    ],
    3 * MATMUL,
    5 * MIB,
    grant=51,
)
col_grad = call(
    col_kernel,
    "svv" + "v" * 5,
    "vh",
    (shape(N_DEV, 4, D), shape(7, TOK, D)),
    [
        token_scratch(), token_scratch(dtype=F32), token_scratch(), token_scratch(2), token_scratch(4),
        token_scratch(3), token_scratch(), DMA((2,)), DMA((4,)), DMA,
    ],
    8 * MATMUL + 6 * ATTEND,
    8 * MIB,
    grant=50,
)
col_weights = call(
    col_weights_kernel,
    "sh",
    "vh",
    (HALF, shape(2, D, TOK)),
    [
        token_scratch(2), token_scratch(2), pltpu.VMEM((2, D, TOK), BF16),
        DMA((2,)), DMA((2,)), DMA((2,)),
    ],
    2 * MATMUL,
    6 * MIB,
    grant=50,
)
col_output = call(
    col_output_kernel,
    "shh",
    "v" * 8,
    (LINES,) * 8,
    [token_scratch(), token_scratch(), pltpu.VMEM((D, D), BF16), token_scratch(), DMA((3,))],
    MATMUL,
    3 * MIB,
    grant=52,
)
tile_to_lines = call(
    tile_to_lines_kernel, "sv", "v" * 4, (PIECE,) * 4, [MIX_TILE], 0, MIB, grant=48
)
pass_low = call(pass_low_kernel, "s" + "v" * 4, "v", PASS, [], 0, MIB, grant=12)
lines_to_tile = call(
    lines_to_tile_kernel, "s" + "v" * 8, "v", shape(32, 16, D), [], MATMUL, MIB, grant=48
)
CHIP_PASS = shape(4, 2, 2, 16, D)
CORE_PASS = shape(2, 4, 2, 16, D)
pass_high = call(pass_high_kernel, "s" + "v" * 4, "v", CHIP_PASS, [], 0, MIB)
pass_core = call(pass_core_kernel, "s" + "v" * 5, "v", CORE_PASS, [], 0, MIB, grant=40)
join = call(join_kernel, "s" + "v" * 6, "v", shape(2, 4, 2, 2, 16, D), [], 0, MIB)
pair_sum = call(
    pair_sum_kernel, "svv", "v" * 4, (QUARTER,) * 4, [pltpu.VMEM((4, 256, D), BF16)], 0, 3 * MIB,
)
merge = call(merge_kernel, "v" * 6, "v", shape(64, 80, 128), [], 0, 4 * MIB, grant=32)
spread = call(spread_kernel, "v", "v", shape(64, 128, 128), [], 0, 3 * MIB, grant=52)


def widen(where, chunks, side, *before):
    return pl.pallas_call(
        functools.partial(widen_kernel, side),
        in_specs=[SMEM, VMEM] + [HBM] * len(before),
        out_specs=(HBM, HBM),
        out_shape=(shape(2, 1024, D, dtype=F32), shape(2, 4, 256, D, dtype=F32)),
        scratch_shapes=[
            pltpu.VMEM((4, 256, D), F32), pltpu.VMEM((4, 256, D), F32), DMA((4,)), DMA((4,)),
        ],
        input_output_aliases={2: 0, 3: 1} if before else {},
        name="widen",
        compiler_params=pltpu.CompilerParams(vmem_limit_bytes=16 * MIB),
        cost_estimate=pl.CostEstimate(flops=0, bytes_accessed=6 * MIB, transcendentals=0),
    )(where, chunks, *before)


def exchange(values, axes):
    return lax.all_to_all(values, axes, split_axis=0, concat_axis=0, tiled=True)


def shifted(pieces, axis):
    n = len(pieces)
    return [pieces[0]] + [
        lax.ppermute(pieces[k], axis, [(i, (i + k) % n) for i in range(n)]) for k in range(1, n)
    ]


def moved(pieces, axes, sizes, long_axis):
    peers = []
    for place in range(1, 8):
        steps = (place % 4, place // 4) if long_axis == 0 else (place // 4, place % 4)
        peers.append(
            [
                (i * sizes[1] + j, (i + steps[0]) % sizes[0] * sizes[1] + (j + steps[1]) % sizes[1])
                for i in range(sizes[0])
                for j in range(sizes[1])
            ]
        )
    return [pieces[0]] + [lax.ppermute(pieces[k + 1], axes, peers[k]) for k in range(7)]


def swap(value, axis):
    return lax.ppermute(value, axis, [(0, 1), (1, 0)])


def layer(latents, cotangent, w_row, w_col, keep_heads):
    where = jnp.concatenate(
        [jnp.stack([lax.axis_index(name) for name in AXES]), keep_heads.reshape(-1)]
    ).astype(jnp.int32)
    rows_in = exchange(latents.reshape(16, 2, 16, D), COL)
    grad_pieces = tile_to_lines(where, cotangent)
    grad_parts = shifted(grad_pieces, "y")
    grad_pass = pass_low(where, *grad_parts)
    grad_pass = swap(grad_pass, "zl")
    mid_send, saved_row = row_forward(where, rows_in, w_row)
    mid_lines = exchange(mid_send, BOTH)
    probs_row, turned_row = row_prepare(saved_row)
    grad_send, saved_col = col_grad(
        where, mid_lines, w_col, *grad_parts, grad_pass
    )
    grad_rows = exchange(grad_send, BOTH)
    send_col, turned_col = col_weights(where, saved_col)
    got_col = swap(send_col, "c")
    keep_col = kept_gradients(where, turned_col, saved_col)
    quarters = pair_sum(where, keep_col, got_col)
    quarters = shifted(quarters, "x")
    send_row, right_row = row_backward(where, grad_rows, saved_row, turned_row, probs_row, w_row)
    got_row = swap(send_row, "c")
    keep_row = kept_gradients(where, turned_row, right_row)
    merged = merge(keep_row, got_row, *quarters)
    both = exchange(merged, CHIPS)
    totals = spread(both)
    chunks = exchange(totals, CHIPS)
    gin_pieces = row_input_gradient(where, rows_in, right_row, w_row)
    gin_parts = shifted(gin_pieces, "x")
    gin_high = pass_high(where, *gin_parts)
    gin_got = swap(gin_high, "zh")
    gin_core = pass_core(where, *gin_parts, gin_got)
    gin_core = swap(gin_core, "c")
    grad_latents = join(where, *gin_parts, gin_got, gin_core).reshape(32, 16, D)
    out_pieces = col_output(where, saved_col, w_col)
    out_parts = moved(out_pieces, ROW, (4, 2), 0)
    output = lines_to_tile(where, *out_parts)
    other = swap(chunks, "c")
    halves_done = widen(where, chunks, 0)
    grad_row, grad_col = widen(where, other, 1, *halves_done)
    return (output, grad_latents, grad_row.reshape(4, D, D), grad_col.reshape(4, D, D))


def solution(mesh):
    fine = Mesh(mesh.devices.reshape(4, 2, 2, 4, 2), AXES)
    tile = P(ROW, COL, None)
    return jax.shard_map(
        layer,
        mesh=fine,
        in_specs=(tile, tile, P(), P(), P()),
        out_specs=(tile, tile, P(), P()),
        check_vma=False,
    )
```
